32 devices in a mesh: group: 2 (over x), src: 4 (over z), tile: 4 (over y, core).
Axes of the slice: x: 2, y: 2, z: 4, core: 2. Of those that a mesh axis runs over, the one named last changes fastest.
Arguments:
- mask_param: float32 [2048, 256], P(('group', 'tile')), parts along dimension 0, may hold values from -6 to 6
- target_image: float32 [2048, 256], P(('group', 'tile')), parts along dimension 0, may hold values from 0 to 1
- source_weights: float32 [128], P(('group', 'src')), parts along dimension 0, may hold values from 0.36 to 8.2
- source_shifts: int32 [64, 2], P('src'), may hold values from -16 to 16, as said below
- pupil_map: float32 [2, 32, 32], replicated, may hold values from -1.4 to 1.4, as said below
Outputs:
- mask_final: float32 [2048, 256], P(('group', 'tile')), parts along dimension 0
- weights_final: float32 [128], P(('group', 'src')), parts along dimension 0
The draws below stay inside these ranges and needn't reach their ends.
There are 2 independent parts, one for each index of `group`. The reference program is written for one: setup_inputs(seed, part) draws one part's arguments, and reference() takes and returns one part's arrays. A program takes and returns all parts, laid end to end along the dimension named above; an argument that names none is the same for every part. Nothing has to cross between parts.
Inputs may be any that keep to these rules, and one draw needn't show every extreme that they name: `source_shifts`: each of the two columns takes the value 16 on some source and the value -16 on another. `pupil_map`: zero outside the disc of radius 32 // 2 - 1 around box index (16, 16).
All inputs are finite; a program needn't handle non-finite values.
Results may differ from the reference program's by a relative error of at most 0.0003.
Values sent between devices are 32-bit elements; how exact they have to be, the bound alone decides.
No kernel may reach another device: no remote copies, remote signals or barrier semaphores. Data moves between devices by JAX's collectives and lax.ppermute only.
A program may use at most 64 MiB of HBM per device.

```python
import math
import jax
import jax.numpy as jnp
from jax import lax

CLIP_TILE = 256
MARGIN = 64
PUPIL_BOX = 32
MAX_SHIFT = 16
OUTER_STEPS = 1
INNER_STEPS = 2
SOURCES = 64
TILES_ALL = 4
CLIP_ROWS = 1024
WINDOW = 384


def draw_target_image(key, part):
    level = jax.random.uniform(key, (CLIP_ROWS, CLIP_TILE), jnp.float32)
    ramp = 0.3 + 0.7 * (jnp.arange(CLIP_ROWS, dtype=jnp.float32) / CLIP_ROWS)[:, None]
    return level * ramp


def draw_source_weights(key, part):
    raw = jax.random.uniform(key, (SOURCES,), jnp.float32, -1.0, 1.0)
    ramp = 1.0 + 2.0 * jnp.arange(SOURCES, dtype=jnp.float32) / (SOURCES - 1)
    return jnp.exp(raw) * ramp


def draw_source_shifts(key, part):
    key_one, key_two = jax.random.split(key)
    values = jax.random.randint(key_one, (SOURCES, 2), -MAX_SHIFT, MAX_SHIFT + 1, dtype=jnp.int32)
    chosen = jax.random.permutation(key_two, SOURCES)[:4]
    ends = jnp.array([[1, 0], [-1, 0], [0, 1], [0, -1]], dtype=jnp.int32) * MAX_SHIFT
    return values.at[chosen].set(ends)


def draw_pupil_map(key, part):
    key_amp, key_phase = jax.random.split(key)
    offsets = jnp.arange(PUPIL_BOX, dtype=jnp.int32) - PUPIL_BOX // 2
    radius = PUPIL_BOX // 2 - 1
    inside = (offsets[:, None] * offsets[:, None] + offsets[None, :] * offsets[None, :] <= radius * radius).astype(jnp.float32)
    amplitude = jax.random.uniform(key_amp, (PUPIL_BOX, PUPIL_BOX), jnp.float32, 0.6, 1.4)
    phases = jax.random.uniform(key_phase, (PUPIL_BOX, PUPIL_BOX), jnp.float32, -1.0, 1.0)
    return jnp.stack([amplitude * jnp.cos(phases), amplitude * jnp.sin(phases)]) * inside[None]


def steps_of(rng, extent, cuts, low, top_value):
    level, own = 1.0, jax.random.fold_in(rng, 6)
    for axis_at, shards_of in cuts:
        heights = jnp.exp(jax.random.uniform(jax.random.fold_in(own, axis_at), (shards_of,), jnp.float32, low / len(cuts), top_value / len(cuts)))
        level = level * jnp.repeat(heights, extent[axis_at] // shards_of).reshape([-1 if axis == axis_at else 1 for axis in range(len(extent))])
    return level


def noise(rng, shape, width, most, cuts=(), kind=jnp.bfloat16):
    gain = steps_of(rng, shape, cuts, -0.22, 0.18) if cuts else 1.0
    entries = jax.random.normal(rng, shape, jnp.float32) * width * gain
    return jnp.minimum(jnp.maximum(entries, -most), most).astype(kind)


def setup_inputs(seed: int = 0, part: int = 0) -> dict:
    key_of = jax.random.split(jax.random.key(seed), 6)
    own_keys = jax.random.split(jax.random.fold_in(key_of[5], part), 6)
    mask_param = noise(own_keys[0], (CLIP_ROWS, CLIP_TILE), 1.0, 6.0, ((0, 4),), jnp.float32)
    target_image = draw_target_image(jax.random.fold_in(jax.random.fold_in(key_of[5], part), 71), part)
    source_weights = draw_source_weights(jax.random.fold_in(jax.random.fold_in(key_of[5], part), 71), part)
    source_shifts = draw_source_shifts(jax.random.fold_in(key_of[5], 71), part)
    pupil_map = draw_pupil_map(jax.random.fold_in(key_of[5], 71), part)
    return dict(mask_param=mask_param, target_image=target_image, source_weights=source_weights, source_shifts=source_shifts, pupil_map=pupil_map)


highest = lax.Precision.HIGHEST
mask_rate = 0.5
weight_rate = 0.3
tiny_eps = 1e-06

def matmul(left, right):
    return jnp.dot(left, right, precision=highest)

def einsum_hi(formula, left, right):
    return jnp.einsum(formula, left, right, precision=highest)

def phase_table(freq_list, pixels, period):
    product = jnp.mod(freq_list[:, None] * pixels[None, :], period)
    angles = product.astype(jnp.float32) * (2.0 * math.pi / period)
    return (jnp.cos(angles), jnp.sin(angles))

def make_tables(period, tile_len, margin, box_len, max_shift):
    wide_freqs = jnp.arange(box_len + 2 * max_shift, dtype=jnp.int32) - (box_len // 2 + max_shift)
    box_freqs = jnp.arange(box_len, dtype=jnp.int32) - box_len // 2
    pixels = jnp.arange(tile_len, dtype=jnp.int32)
    rows_fwd = phase_table(wide_freqs, jnp.arange(period, dtype=jnp.int32), period)
    cols_fwd = phase_table(wide_freqs, pixels, period)
    rows_inv = phase_table(box_freqs, pixels + margin, period)
    cols_inv = phase_table(box_freqs, pixels, period)
    return (rows_fwd, cols_fwd, rows_inv, cols_inv)

def selectors(shifts, box_len, max_shift):
    freq_width = box_len + 2 * max_shift
    columns = jnp.arange(freq_width, dtype=jnp.int32)[None, None, :]
    box_base = jnp.arange(box_len, dtype=jnp.int32)[None, :] + max_shift
    rows_at = box_base + shifts[:, 0:1]
    cols_at = box_base + shifts[:, 1:2]
    sel_rows = (rows_at[:, :, None] == columns).astype(jnp.float32)
    sel_cols = (cols_at[:, :, None] == columns).astype(jnp.float32)
    return (sel_rows, sel_cols)

def spectrum(window_mask, rows_fwd, cols_fwd, norm_scale):
    first_re = matmul(rows_fwd[0], window_mask)
    first_im = -matmul(rows_fwd[1], window_mask)
    spec_re = matmul(first_re, cols_fwd[0].T) + matmul(first_im, cols_fwd[1].T)
    spec_im = matmul(first_im, cols_fwd[0].T) - matmul(first_re, cols_fwd[1].T)
    return jnp.stack([spec_re, spec_im]) * norm_scale

def make_fields(spec, sel_rows, sel_cols, pupil_map, rows_inv, cols_inv):
    picked = einsum_hi('sij,cjl->csil', sel_rows, spec)
    picked = einsum_hi('csil,sml->csim', picked, sel_cols)
    lit_re = pupil_map[0] * picked[0] - pupil_map[1] * picked[1]
    lit_im = pupil_map[0] * picked[1] + pupil_map[1] * picked[0]
    mid_re = einsum_hi('kx,skl->sxl', rows_inv[0], lit_re) - einsum_hi('kx,skl->sxl', rows_inv[1], lit_im)
    mid_im = einsum_hi('kx,skl->sxl', rows_inv[0], lit_im) + einsum_hi('kx,skl->sxl', rows_inv[1], lit_re)
    field_re = einsum_hi('sxl,ly->sxy', mid_re, cols_inv[0]) - einsum_hi('sxl,ly->sxy', mid_im, cols_inv[1])
    field_im = einsum_hi('sxl,ly->sxy', mid_re, cols_inv[1]) + einsum_hi('sxl,ly->sxy', mid_im, cols_inv[0])
    return (field_re, field_im)

def spectral_grad(field_re, field_im, misfit, factor, sel_rows, sel_cols, pupil_map, rows_inv, cols_inv):
    hit_re = misfit[None] * field_re
    hit_im = misfit[None] * field_im
    half_re = einsum_hi('sxy,ly->sxl', hit_re, cols_inv[0]) + einsum_hi('sxy,ly->sxl', hit_im, cols_inv[1])
    half_im = einsum_hi('sxy,ly->sxl', hit_im, cols_inv[0]) - einsum_hi('sxy,ly->sxl', hit_re, cols_inv[1])
    box_re = einsum_hi('kx,sxl->skl', rows_inv[0], half_re) + einsum_hi('kx,sxl->skl', rows_inv[1], half_im)
    box_im = einsum_hi('kx,sxl->skl', rows_inv[0], half_im) - einsum_hi('kx,sxl->skl', rows_inv[1], half_re)
    weight_col = factor[:, None, None]
    back_re = (pupil_map[0] * box_re + pupil_map[1] * box_im) * weight_col
    back_im = (pupil_map[0] * box_im - pupil_map[1] * box_re) * weight_col
    stacked = jnp.stack([back_re, back_im])
    placed = einsum_hi('csim,sij->csjm', stacked, sel_rows)
    return einsum_hi('csjm,sml->cjl', placed, sel_cols)

def adjoint(grad_spec, rows_fwd, cols_fwd, norm_scale):
    vals_re = matmul(grad_spec[0], cols_fwd[0]) - matmul(grad_spec[1], cols_fwd[1])
    vals_im = matmul(grad_spec[0], cols_fwd[1]) + matmul(grad_spec[1], cols_fwd[0])
    return (matmul(rows_fwd[0].T, vals_re) - matmul(rows_fwd[1].T, vals_im)) * norm_scale

def assemble(windows, margin, tile_len):
    core = windows[:, margin:margin + tile_len]
    top_rim = windows[:, :margin]
    low_rim = windows[:, margin + tile_len:]
    empty = jnp.zeros_like(top_rim[:1])
    from_next = jnp.concatenate([top_rim[1:], empty], axis=0)
    from_prev = jnp.concatenate([empty, low_rim[:-1]], axis=0)
    core = core.at[:, tile_len - margin:].add(from_next)
    core = core.at[:, :margin].add(from_prev)
    return core.reshape(-1, tile_len)

def reference(mask_param, target_image, source_weights, source_shifts, pupil_map):
    tables = make_tables(WINDOW, CLIP_TILE, MARGIN, PUPIL_BOX, MAX_SHIFT)
    rows_fwd, cols_fwd, rows_inv, cols_inv = tables
    sel_rows, sel_cols = selectors(source_shifts, PUPIL_BOX, MAX_SHIFT)
    norm_scale = 1.0 / (WINDOW * CLIP_TILE)
    pixel_count = CLIP_ROWS * CLIP_TILE
    target_tiles = target_image.reshape(TILES_ALL, CLIP_TILE, CLIP_TILE)
    tile_ids = jnp.arange(TILES_ALL, dtype=jnp.int32)
    params = mask_param
    weights = source_weights

    def tile_image(padded, tile_id, weights, dose_total):
        window_mask = lax.dynamic_slice_in_dim(padded, tile_id * CLIP_TILE, WINDOW, 0)
        spec = spectrum(window_mask, rows_fwd, cols_fwd, norm_scale)
        field_re, field_im = make_fields(spec, sel_rows, sel_cols, pupil_map, rows_inv, cols_inv)
        powers = field_re * field_re + field_im * field_im
        intensity = einsum_hi('s,sxy->xy', weights, powers) / dose_total
        misfit = intensity - lax.dynamic_index_in_dim(target_tiles, tile_id, 0, keepdims=False)
        return (field_re, field_im, powers, intensity, misfit)
    for outer_step in range(OUTER_STEPS):
        for inner_step in range(INNER_STEPS):
            mask_field = jax.nn.sigmoid(params)
            padded = jnp.pad(mask_field, ((MARGIN, MARGIN), (0, 0)))
            dose_total = jnp.sum(weights)
            factor = 2.0 * weights / dose_total

            def window_grad(tile_id):
                field_re, field_im, powers, intensity, misfit = tile_image(padded, tile_id, weights, dose_total)
                grad_spec = spectral_grad(field_re, field_im, misfit, factor, sel_rows, sel_cols, pupil_map, rows_inv, cols_inv)
                return adjoint(grad_spec, rows_fwd, cols_fwd, norm_scale)
            windows = lax.map(window_grad, tile_ids)
            mask_grad = assemble(windows, MARGIN, CLIP_TILE) * (mask_field * (1.0 - mask_field))
            rms = jnp.sqrt(jnp.sum(mask_grad * mask_grad) / pixel_count + tiny_eps)
            params = params - mask_rate * mask_grad / rms
        mask_field = jax.nn.sigmoid(params)
        padded = jnp.pad(mask_field, ((MARGIN, MARGIN), (0, 0)))
        dose_total = jnp.sum(weights)

        def source_part(tile_id):
            field_re, field_im, powers, intensity, misfit = tile_image(padded, tile_id, weights, dose_total)
            return (einsum_hi('xy,sxy->s', misfit, powers) - jnp.sum(misfit * intensity)) / dose_total
        source_grad = lax.optimization_barrier(jnp.sum(lax.map(source_part, tile_ids), axis=0))
        spread = jnp.sqrt(jnp.sum(source_grad * source_grad) / SOURCES + tiny_eps)
        weights = weights * jnp.exp(-weight_rate * source_grad / spread)
    return (params, weights)
```

```python
import functools
import math

import jax
import jax.numpy as jnp
import ml_dtypes
import numpy as np
from jax import lax
from jax.experimental import pallas as pl
from jax.experimental.pallas import tpu as pltpu
from jax.sharding import PartitionSpec as P

MARGIN = 64
MAX_SHIFT = 16
MASK_RATE = 0.5
WEIGHT_RATE = 0.3
TINY_EPS = 1e-06
CHUNK = 8

bf16 = jnp.bfloat16
f32 = jnp.float32


def np_split(table):
    table = np.asarray(table, np.float64)
    high = table.astype(np.float32).astype(ml_dtypes.bfloat16)
    low = (table - high.astype(np.float64)).astype(np.float32).astype(ml_dtypes.bfloat16)
    return high, low


def phases(freqs, pixels, period):
    return 2.0 * math.pi * np.mod(np.outer(freqs, pixels), period) / period


def make_tables(tile_len, box_len, max_shift):
    period = tile_len + 2 * MARGIN
    grid = box_len + 2 * max_shift
    wide = np.arange(grid) - grid // 2
    pix = np.arange(tile_len)
    full = np.arange(period)
    points = np.arange(grid)
    box = np.arange(box_len)
    out = {}
    ang = phases(wide, pix, period)
    high, low = np_split(np.concatenate([np.cos(ang), -np.sin(ang)], 0).T / (period * tile_len))
    out["spec_cols"] = np.concatenate([high, low], 1)
    ang_rows = phases(wide, full, period)
    high, low = np_split(np.concatenate([np.cos(ang_rows), np.sin(ang_rows)], 0))
    out["spec_rows"] = np.concatenate([high, low], 0)
    ang = phases(points, points, grid)
    cos, sin = np.cos(ang), np.sin(ang)
    for name, table in (
        ("lane_fwd", np.block([[cos, sin], [-sin, cos]])),
        ("lane_back", np.block([[cos, -sin], [sin, cos]])),
    ):
        high, low = np_split(table)
        out[name] = np.block([[high, low], [high, np.zeros_like(low)]])
    ang = phases(points, box, grid)
    high, low = np_split(np.concatenate([np.cos(ang), np.sin(ang)], 0))
    out["row_fwd"] = np.concatenate([high, high, low], 1)
    high, low = np_split(np.concatenate([np.cos(ang).T, np.sin(ang).T], 0))
    out["row_back"] = np.concatenate([high, high, low], 1)
    def dirichlet(offset):
        theta = 2.0 * math.pi * ((pix + offset)[None, :] / period - points[:, None] / grid)
        orders = np.arange(1, box_len)
        return 1.0 + 2.0 * np.cos(orders[:, None, None] * theta[None]).sum(0)

    rows, cols = dirichlet(MARGIN), dirichlet(0)
    high, low = np_split(rows @ rows.T / grid)
    out["mix_rows"] = np.concatenate([high, high, low], 1)
    mix = cols @ cols.T / grid
    high, low = np_split(np.block([[mix, mix], [mix, mix]]))
    out["mix_cols"] = np.block([[high, low], [high, np.zeros_like(low)]])
    high, low = np_split(rows)
    out["target_rows"] = np.concatenate([high, low], 0)
    high, low = np_split(np.concatenate([cols, cols], 0).T)
    out["target_cols"] = np.concatenate([high, low], 1)
    ang = phases(wide, pix, period)
    cos, sin = np.cos(ang), np.sin(ang)
    high, low = np_split(np.block([[cos, sin], [-sin, cos]]))
    out["grad_cols"] = np.concatenate([high, high, low], 0)
    high, low = np_split(np.concatenate([np.cos(ang_rows).T, -np.sin(ang_rows).T], 1))
    out["grad_rows"] = np.concatenate([high, high, low], 1)
    return out


def split(value):
    high = value.astype(bf16)
    return high, (value - high.astype(f32)).astype(bf16)


def dot(left, right):
    return jnp.dot(left, right, preferred_element_type=f32)


def halves(value):
    width = value.shape[1] // 2
    return value[:, :width] + value[:, width:]


def lane_sign(rows, lanes, first):
    lane = lax.broadcasted_iota(jnp.int32, (rows, lanes), 1)
    return jnp.where(lane < lanes // 2, first, -first).astype(f32)


def swap(value):
    return pltpu.roll(value, value.shape[1] // 2, 1)


def sigmoid(value):
    return 1.0 / (1.0 + jnp.exp(-value))


def window_spectrum(window, t):
    grid = t["spec_cols"].shape[1] // 4
    high, low = split(window)
    cols = t["spec_cols"]
    mid = halves(dot(high, cols[...])) + dot(low, cols[:, : 2 * grid])
    mid_high, mid_low = split(mid)
    rows = t["spec_rows"]
    both = halves(dot(rows[: 2 * grid, :], jnp.concatenate([mid_high, mid_low], 1)))
    both = both + dot(rows[2 * grid :, :], mid_high)
    return both[:grid] + lane_sign(grid, 2 * grid, 1.0) * swap(both[grid:])


def lane_stage(blocks, table):
    rows = []
    for block in blocks:
        high, low = split(block)
        rows.append(jnp.concatenate([high, low], 1))
    return halves(dot(jnp.concatenate(rows, 0), table[...]))


def row_stage(blocks, table, sign):
    stacks = []
    for block in blocks:
        high, low = split(block)
        stacks.append(jnp.concatenate([high, low, high], 0))
    both = dot(table[...], jnp.concatenate(stacks, 1))
    width = blocks[0].shape[1]
    half = both.shape[0] // 2
    outs = []
    for i in range(len(blocks)):
        part = both[:, i * width : (i + 1) * width]
        outs.append(part[:half] + sign * swap(part[half:]))
    return outs


def place_pupils(shifts, roots, pupil_re, pupil_im, pr, pi):
    count = pr.shape[0]

    def one(s, carry):
        by = shifts[s, 1] + MAX_SHIFT
        pr[s] = pltpu.roll(pupil_re[...], by, 1) * roots[s]
        pi[s] = pltpu.roll(pupil_im[...], by, 1) * roots[s]
        return carry

    lax.fori_loop(0, count, one, 0, unroll=8)


def grid_fields(spec, shifts, t, pr, pi, plain, crossed, fields):
    count, box_len, lanes = pr.shape
    grid = lanes // 2
    plain[...] = spec
    crossed[...] = swap(spec)
    sign = lane_sign(grid, lanes, -1.0)

    def chunk(c, power):
        blocks = []
        for i in range(CHUNK):
            s = c * CHUNK + i
            at = shifts[s, 0] + MAX_SHIFT
            rows = pl.ds(at, box_len)
            blocks.append(pr[s] * plain[rows, :] + pi[s] * crossed[rows, :])
        mid = lane_stage(blocks, t["lane_fwd"])
        mids = [mid[i * box_len : (i + 1) * box_len] for i in range(CHUNK)]
        for i, field in enumerate(row_stage(mids, t["row_fwd"], sign)):
            fields[c * CHUNK + i] = field
            power = power + field * field
        return power

    return lax.fori_loop(0, count // CHUNK, chunk, jnp.zeros((grid, lanes), f32))


def grid_misfit(power, inv_dose, target, t):
    high, low = split(power)
    mid = halves(dot(jnp.concatenate([high, low], 1), t["mix_cols"][...]))
    high, low = split(mid)
    lit = dot(t["mix_rows"][...], jnp.concatenate([high, low, high], 0))
    return lit * inv_dose - target


def gather_back(misfit, shifts, scale, t, pr, pi, fields, acc_re, acc_im):
    count, box_len, lanes = pr.shape
    grid = lanes // 2
    acc_re[...] = jnp.zeros_like(acc_re)
    acc_im[...] = jnp.zeros_like(acc_im)
    sign = lane_sign(box_len, lanes, 1.0)

    def chunk(c, carry):
        blocks = [fields[c * CHUNK + i] * misfit for i in range(CHUNK)]
        mids = row_stage(blocks, t["row_back"], sign)
        hits = lane_stage(mids, t["lane_back"])
        for i in range(CHUNK):
            s = c * CHUNK + i
            rows = pl.ds(shifts[s, 0] + MAX_SHIFT, box_len)
            hit = hits[i * box_len : (i + 1) * box_len]
            acc_re[rows, :] += pr[s] * hit
            acc_im[rows, :] += pi[s] * hit
        return carry

    lax.fori_loop(0, count // CHUNK, chunk, 0)
    return (acc_re[...] + swap(acc_im[...])) * scale


def window_grads(backs, t):
    count = len(backs)
    grid = backs[0].shape[0]
    rows = []
    for back in backs:
        high, low = split(back)
        rows.append(jnp.concatenate([high, low, high], 1))
    mid = dot(jnp.concatenate(rows, 0), t["grad_cols"][...])
    width = mid.shape[1] // 2
    outs = []
    for k in range(count):
        part = mid[k * grid : (k + 1) * grid]
        high, low = split(jnp.concatenate([part[:, :width], part[:, width:]], 0))
        outs.append(dot(t["grad_rows"][...], jnp.concatenate([high, low, high], 0)))
    return outs


def updated_params(params, backs, t, tile, tiles):
    wins = window_grads(backs, t)
    tile_len = params[0].shape[0]
    grads, square = [], None
    for k in range(tiles):
        own = lax.rem(tile + tiles - k, tiles)
        has_prev = (own > 0).astype(f32)
        has_next = (own < tiles - 1).astype(f32)
        core = wins[k][MARGIN : MARGIN + tile_len]
        above = wins[(k + 1) % tiles][MARGIN + tile_len :] * has_prev
        below = wins[(k - 1) % tiles][:MARGIN] * has_next
        total = jnp.concatenate(
            [core[:MARGIN] + above, core[MARGIN:-MARGIN], core[-MARGIN:] + below], 0
        )
        mask = sigmoid(params[k])
        grad = total * (mask * (1.0 - mask))
        grads.append(grad)
        part = jnp.sum(grad * grad, axis=0, keepdims=True)
        square = part if square is None else square + part
    pixels = tiles * tile_len * tile_len
    rms = jnp.sqrt(jnp.sum(square, axis=1, keepdims=True) / pixels + TINY_EPS)
    rate = MASK_RATE / rms
    return [params[k] - grads[k] * rate for k in range(tiles)]


def tile_window(own, before, after, tile, tiles):
    has_prev = (tile > 0).astype(f32)
    has_next = (tile < tiles - 1).astype(f32)
    return jnp.concatenate(
        [sigmoid(before) * has_prev, sigmoid(own), sigmoid(after) * has_next], 0
    )


def target_kernel(names, target, *refs):
    t = dict(zip(names, refs))
    out = refs[len(names)]
    grid = out.shape[0]
    high, low = split(target[...])
    rows = t["target_rows"]
    both = dot(rows[...], high)
    mid = both[:grid] + both[grid:] + dot(rows[:grid, :], low)
    high, low = split(mid)
    cols = t["target_cols"]
    out[...] = halves(dot(high, cols[...])) + dot(low, cols[:, : 2 * grid])


def first_kernel(names, tiles, tile, shifts, roots, scal, pupil_re, pupil_im, target,
                 own, before, after, *refs):
    t = dict(zip(names, refs))
    back, pr, pi, plain, crossed, fields, acc_re, acc_im = refs[len(names):]
    here = tile[0]
    spec = window_spectrum(tile_window(own[...], before[...], after[...], here, tiles), t)
    place_pupils(shifts, roots, pupil_re, pupil_im, pr, pi)
    power = grid_fields(spec, shifts, t, pr, pi, plain, crossed, fields)
    misfit = grid_misfit(power, scal[0], target[...], t)
    back[...] = gather_back(misfit, shifts, scal[1], t, pr, pi, fields, acc_re, acc_im)


def next_kernel(names, tiles, tile, shifts, roots, scal, pupil_re, pupil_im, target, *refs):
    params = [ref[...] for ref in refs[:tiles]]
    backs = [ref[...] for ref in refs[tiles : 2 * tiles]]
    refs = refs[2 * tiles :]
    t = dict(zip(names, refs))
    outs = refs[len(names) : len(names) + tiles]
    back, pr, pi, plain, crossed, fields, acc_re, acc_im = refs[len(names) + tiles :]
    here = tile[0]
    params = updated_params(params, backs, t, here, tiles)
    for out, value in zip(outs, params):
        out[...] = value
    window = tile_window(params[0], params[1][-MARGIN:], params[-1][:MARGIN], here, tiles)
    spec = window_spectrum(window, t)
    place_pupils(shifts, roots, pupil_re, pupil_im, pr, pi)
    power = grid_fields(spec, shifts, t, pr, pi, plain, crossed, fields)
    misfit = grid_misfit(power, scal[0], target[...], t)
    back[...] = gather_back(misfit, shifts, scal[1], t, pr, pi, fields, acc_re, acc_im)


def last_kernel(names, tiles, tile, shifts, roots, scal, pupil_re, pupil_im, target, *refs):
    params = [ref[...] for ref in refs[:tiles]]
    backs = [ref[...] for ref in refs[tiles : 2 * tiles]]
    refs = refs[2 * tiles :]
    t = dict(zip(names, refs))
    final, terms, pr, pi, plain, crossed, fields = refs[len(names):]
    here = tile[0]
    params = updated_params(params, backs, t, here, tiles)
    final[...] = params[0]
    window = tile_window(params[0], params[1][-MARGIN:], params[-1][:MARGIN], here, tiles)
    spec = window_spectrum(window, t)
    place_pupils(shifts, roots, pupil_re, pupil_im, pr, pi)
    power = grid_fields(spec, shifts, t, pr, pi, plain, crossed, fields)
    misfit = grid_misfit(power, scal[0], target[...], t)

    def chunk(c, carry):
        rows = []
        for i in range(CHUNK):
            field = fields[c * CHUNK + i]
            rows.append(jnp.sum(field * field * misfit, axis=0, keepdims=True))
        terms[pl.ds(pl.multiple_of(c * CHUNK, CHUNK), CHUNK), :] = jnp.concatenate(rows, 0)
        return carry

    lax.fori_loop(0, fields.shape[0] // CHUNK, chunk, 0)


def weight_kernel(tiles, scale, tile, place, weights, *refs):
    terms = refs[:tiles]
    out, stack, new = refs[tiles:]
    for k in range(tiles):
        stack[k] = terms[k][...]
    here = tile[0]
    total = stack[lax.rem(here, tiles)]
    for k in range(1, tiles):
        total = total + stack[lax.rem(here + tiles - k, tiles)]
    weight = weights[...]
    dose = jnp.sum(weight, axis=0, keepdims=True)
    summed = jnp.sum(total, axis=1, keepdims=True) * scale
    mean = jnp.sum(summed, axis=0, keepdims=True) / dose
    grad = (summed / weight - mean) / dose
    count = weight.shape[0]
    spread = jnp.sqrt(jnp.sum(grad * grad, axis=0, keepdims=True) / count + TINY_EPS)
    new[...] = jnp.broadcast_to(weight * jnp.exp(-WEIGHT_RATE * grad / spread), new.shape)
    size = out.shape[0]
    out[...] = new[pl.ds(pl.multiple_of(place[0] * size, 8), size), :]


def ring(value, axis):
    peers = lax.axis_size(axis)
    got = [value]
    for k in range(1, peers):
        got.append(lax.ppermute(value, axis, [(i, (i + k) % peers) for i in range(peers)]))
    return got


def per_device(mask_param, target_image, source_weights, source_shifts, pupil_map):
    tile_len = mask_param.shape[1]
    box_len = pupil_map.shape[1]
    grid = box_len + 2 * MAX_SHIFT
    lanes = 2 * grid
    tiles = lax.axis_size("tile")
    peers = lax.axis_size("src")
    local = source_weights.shape[0]
    count = local * peers
    tables = make_tables(tile_len, box_len, MAX_SHIFT)

    tile = lax.axis_index("tile").astype(jnp.int32).reshape(1)
    place = lax.axis_index("src").astype(jnp.int32).reshape(1)

    packed = jnp.stack(
        [source_weights, source_shifts[:, 0].astype(f32), source_shifts[:, 1].astype(f32)]
    )
    slot = lax.broadcasted_iota(jnp.int32, (3, peers, local), 1)
    packed = jnp.where(slot == place[0], packed[:, None, :], 0.0).reshape(3, count)
    packed = sum(ring(packed, "src"))
    weights = packed[0]
    shifts = packed[1:].astype(jnp.int32).T
    dose = jnp.sum(weights)
    roots = jnp.sqrt(weights)
    scal = jnp.stack([1.0 / dose, 2.0 / (dose * (grid * grid) * ((tile_len + 2 * MARGIN) * tile_len))])

    down = [(i, (i + 1) % tiles) for i in range(tiles)]
    up = [(j, i) for i, j in down]
    before = lax.ppermute(mask_param[-MARGIN:], "tile", down)
    after = lax.ppermute(mask_param[:MARGIN], "tile", up)
    params = ring(mask_param, "tile")

    pad = ((0, 0), (0, grid - box_len))
    real, imag = jnp.pad(pupil_map[0], pad), jnp.pad(pupil_map[1], pad)
    pupil_re = jnp.concatenate([real, real], 1)
    pupil_im = jnp.concatenate([-imag, imag], 1)

    vmem = pl.BlockSpec(memory_space=pltpu.VMEM)
    smem = pl.BlockSpec(memory_space=pltpu.SMEM)
    params_of = pltpu.CompilerParams(vmem_limit_bytes=48 << 20)

    def struct(*shape):
        return jax.ShapeDtypeStruct(shape, f32)

    def pick(*names):
        return names, [jnp.asarray(tables[n]) for n in names]

    names, values = pick("target_rows", "target_cols")
    target = pl.pallas_call(
        functools.partial(target_kernel, names),
        out_shape=struct(grid, lanes),
        in_specs=[vmem] * (1 + len(names)),
        out_specs=vmem,
        compiler_params=params_of,
        cost_estimate=pl.CostEstimate(flops=4 << 24, bytes_accessed=1 << 20, transcendentals=0),
        name="target_terms",
    )(target_image, *values)

    core_scratch = [
        pltpu.VMEM((count, box_len, lanes), f32),
        pltpu.VMEM((count, box_len, lanes), f32),
        pltpu.VMEM((grid, lanes), f32),
        pltpu.VMEM((grid, lanes), f32),
        pltpu.VMEM((count, grid, lanes), f32),
    ]
    sums = [pltpu.VMEM((grid, lanes), f32)] * 2
    shared = (tile, shifts, roots, scal, pupil_re, pupil_im, target)
    shared_specs = [smem] * 4 + [vmem] * 3
    cost = pl.CostEstimate(flops=1 << 32, bytes_accessed=4 << 20, transcendentals=0)

    fwd = ("spec_cols", "spec_rows", "lane_fwd", "row_fwd", "mix_cols", "mix_rows")
    names, values = pick(*fwd, "lane_back", "row_back")
    back = pl.pallas_call(
        functools.partial(first_kernel, names, tiles),
        out_shape=struct(grid, lanes),
        in_specs=shared_specs + [vmem] * (3 + len(names)),
        out_specs=vmem,
        scratch_shapes=core_scratch + sums,
        compiler_params=params_of,
        cost_estimate=cost,
        name="first_step",
    )(*shared, mask_param, before, after, *values)

    backs = ring(back, "tile")
    names, values = pick(*fwd, "lane_back", "row_back", "grad_cols", "grad_rows")
    outs = pl.pallas_call(
        functools.partial(next_kernel, names, tiles),
        out_shape=[struct(tile_len, tile_len)] * tiles + [struct(grid, lanes)],
        in_specs=shared_specs + [vmem] * (2 * tiles + len(names)),
        out_specs=[vmem] * (tiles + 1),
        scratch_shapes=core_scratch + sums,
        compiler_params=params_of,
        cost_estimate=cost,
        name="next_step",
    )(*shared, *params, *backs, *values)
    params, back = outs[:tiles], outs[tiles]

    backs = ring(back, "tile")
    names, values = pick(*fwd, "grad_cols", "grad_rows")
    final, terms = pl.pallas_call(
        functools.partial(last_kernel, names, tiles),
        out_shape=[struct(tile_len, tile_len), struct(count, lanes)],
        in_specs=shared_specs + [vmem] * (2 * tiles + len(names)),
        out_specs=[vmem] * 2,
        scratch_shapes=core_scratch,
        compiler_params=params_of,
        cost_estimate=cost,
        name="last_step",
    )(*shared, *params, *backs, *values)

    terms = ring(terms, "tile")
    out = pl.pallas_call(
        functools.partial(weight_kernel, tiles, 1.0 / (grid * grid)),
        out_shape=struct(local, lanes),
        in_specs=[smem] * 2 + [vmem] * (1 + tiles),
        out_specs=vmem,
        scratch_shapes=[pltpu.VMEM((tiles, count, lanes), f32), pltpu.VMEM((count, lanes), f32)],
        compiler_params=params_of,
        name="weight_step",
    )(tile, place, weights[:, None], *terms)
    return final, out[:, 0]


def solution(mesh):
    in_specs = (
        P(("group", "tile"), None),
        P(("group", "tile"), None),
        P(("group", "src")),
        P("src", None),
        P(),
    )
    out_specs = (P(("group", "tile"), None), P(("group", "src")))
    return jax.shard_map(
        per_device, mesh=mesh, in_specs=in_specs, out_specs=out_specs, check_vma=False
    )
```

```python
import functools
import math

import jax
import jax.numpy as jnp
import ml_dtypes
import numpy as np
from jax import lax
from jax.experimental import pallas as pl
from jax.experimental.pallas import tpu as pltpu
from jax.sharding import PartitionSpec as P

MARGIN = 64
MAX_SHIFT = 16
MASK_RATE = 0.5
WEIGHT_RATE = 0.3
TINY_EPS = 1e-06
CHUNK = 16

bf16 = jnp.bfloat16
f32 = jnp.float32


def np_split(table):
    table = np.asarray(table, np.float64)
    high = table.astype(np.float32).astype(ml_dtypes.bfloat16)
    low = (table - high.astype(np.float64)).astype(np.float32).astype(ml_dtypes.bfloat16)
    return high, low


def phases(freqs, pixels, period):
    return 2.0 * math.pi * np.mod(np.outer(freqs, pixels), period) / period


def make_tables(tile_len, box_len, max_shift):
    period = tile_len + 2 * MARGIN
    grid = box_len + 2 * max_shift
    wide = np.arange(grid) - grid // 2
    pix = np.arange(tile_len)
    full = np.arange(period)
    points = np.arange(grid)
    box = np.arange(box_len)
    out = {}
    ang = phases(wide, pix, period)
    high, low = np_split(np.concatenate([np.cos(ang), -np.sin(ang)], 0).T / (period * tile_len))
    out["spec_cols"] = np.concatenate([high, low], 1)
    ang_rows = phases(wide, full, period)
    high, low = np_split(np.concatenate([np.cos(ang_rows), np.sin(ang_rows)], 0))
    out["spec_rows"] = np.concatenate([high, low], 0)
    ang = phases(points, points, grid)
    cos, sin = np.cos(ang), np.sin(ang)
    for name, table in (
        ("lane_fwd", np.block([[cos, sin], [-sin, cos]])),
        ("lane_back", np.block([[cos, -sin], [sin, cos]])),
    ):
        high, low = np_split(table)
        out[name] = np.block([[high, low], [high, np.zeros_like(low)]])
    ang = phases(points, box, grid)
    high, low = np_split(np.concatenate([np.cos(ang), np.sin(ang)], 1))
    out["row_fwd"] = np.concatenate([high, high, low], 1)
    high, low = np_split(np.concatenate([np.cos(ang).T, np.sin(ang).T], 0))
    out["row_back"] = np.concatenate([high, high, low], 1)
    def dirichlet(offset):
        theta = 2.0 * math.pi * ((pix + offset)[None, :] / period - points[:, None] / grid)
        orders = np.arange(1, box_len)
        return 1.0 + 2.0 * np.cos(orders[:, None, None] * theta[None]).sum(0)

    rows, cols = dirichlet(MARGIN), dirichlet(0)
    high, low = np_split(rows @ rows.T / grid)
    out["mix_rows"] = np.concatenate([high, high, low], 1)
    mix = cols @ cols.T / grid
    high, low = np_split(np.block([[mix, mix], [mix, mix]]))
    out["mix_cols"] = np.block([[high, low], [high, np.zeros_like(low)]])
    high, low = np_split(rows)
    out["target_rows"] = np.concatenate([high, low], 0)
    high, low = np_split(np.concatenate([cols, cols], 0).T)
    out["target_cols"] = np.concatenate([high, low], 1)
    ang = phases(wide, pix, period)
    cos, sin = np.cos(ang), np.sin(ang)
    high, low = np_split(np.block([[cos, sin], [-sin, cos]]))
    out["grad_cols"] = np.concatenate([high, high, low], 0)
    high, low = np_split(np.concatenate([np.cos(ang_rows).T, -np.sin(ang_rows).T], 1))
    out["grad_rows"] = np.concatenate([high, high, low], 1)
    return out


def split(value):
    high = value.astype(bf16)
    return high, (value - high.astype(f32)).astype(bf16)


def dot(left, right):
    return jnp.dot(left, right, preferred_element_type=f32)


def halves(value):
    width = value.shape[1] // 2
    return value[:, :width] + value[:, width:]


def lane_sign(rows, lanes, first):
    lane = lax.broadcasted_iota(jnp.int32, (rows, lanes), 1)
    return jnp.where(lane < lanes // 2, first, -first).astype(f32)


def swap(value):
    return pltpu.roll(value, value.shape[1] // 2, 1)


def half_tanh(value):
    return jnp.tanh(0.5 * value)


def sigmoid(value):
    return 0.5 * half_tanh(value) + 0.5


def window_spectrum(window, t):
    grid = t["spec_cols"].shape[1] // 4
    high, low = split(window)
    cols = t["spec_cols"]
    mid = halves(dot(high, cols[...])) + dot(low, cols[:, : 2 * grid])
    mid_high, mid_low = split(mid)
    rows = t["spec_rows"]
    both = halves(dot(rows[: 2 * grid, :], jnp.concatenate([mid_high, mid_low], 1)))
    both = both + dot(rows[2 * grid :, :], mid_high)
    return both[:grid] + lane_sign(grid, 2 * grid, 1.0) * swap(both[grid:])


def skewed(count, first, second, carry):
    chunks = count // CHUNK
    first(0)

    def body(c, carry):
        carry = second(c - 1, carry)
        first(c)
        return carry

    carry = lax.fori_loop(1, chunks, body, carry)
    return second(chunks - 1, carry)


def place_pupils(shifts, roots, pupil_re, pupil_im, pr, pi):
    count = pr.shape[0]

    def one(s, carry):
        by = shifts[2, s] + MAX_SHIFT
        pr[s] = pltpu.roll(pupil_re[...], by, 1) * roots[3, s]
        pi[s] = pltpu.roll(pupil_im[...], by, 1) * roots[3, s]
        return carry

    lax.fori_loop(0, count, one, 0, unroll=8)


def grid_fields(spec, shifts, t, pr, pi, work):
    plain, crossed, fields, stage = work
    count, box_len, lanes = pr.shape
    grid = lanes // 2
    plain[...] = spec
    crossed[...] = swap(spec)
    sign = lane_sign(box_len, lanes, -1.0)

    def first(c):
        rows = []
        for i in range(CHUNK):
            s = c * CHUNK + i
            at = pl.ds(shifts[1, s] + MAX_SHIFT, box_len)
            high, low = split(pr[s] * plain[at, :] + pi[s] * crossed[at, :])
            rows.append(jnp.concatenate([high, low], 1))
        mid = halves(dot(jnp.concatenate(rows, 0), t["lane_fwd"][...]))
        for i in range(CHUNK):
            part = mid[i * box_len : (i + 1) * box_len]
            at = slice(i * lanes, (i + 1) * lanes)
            high, low = split(part)
            stage[:box_len, at] = high
            stage[2 * box_len : 3 * box_len, at] = low
            high, low = split(sign * swap(part))
            stage[box_len : 2 * box_len, at] = high
            stage[3 * box_len :, at] = low

    def second(c, power):
        value = stage[...]
        out = dot(t["row_fwd"][...], jnp.concatenate([value, value[: 2 * box_len]], 0))
        for i in range(CHUNK):
            field = out[:, i * lanes : (i + 1) * lanes]
            fields[c * CHUNK + i] = field
            power = power + field * field
        return power

    return skewed(count, first, second, jnp.zeros((grid, lanes), f32))


def grid_misfit(power, inv_dose, target, t):
    high, low = split(power)
    mid = halves(dot(jnp.concatenate([high, low], 1), t["mix_cols"][...]))
    high, low = split(mid)
    lit = dot(t["mix_rows"][...], jnp.concatenate([high, low, high], 0))
    return lit * inv_dose - target


def gather_back(misfit, shifts, scale, t, pr, pi, fields, stage, sums):
    count, box_len, lanes = pr.shape
    for ref in sums:
        ref[...] = jnp.zeros_like(ref)
    sign = lane_sign(box_len, lanes, 1.0)

    def first(c):
        stacks = []
        for i in range(CHUNK):
            high, low = split(fields[c * CHUNK + i] * misfit)
            stacks.append(jnp.concatenate([high, low, high], 0))
        both = dot(t["row_back"][...], jnp.concatenate(stacks, 1))
        for i in range(CHUNK):
            part = both[:, i * lanes : (i + 1) * lanes]
            part = part[:box_len] + sign * swap(part[box_len:])
            at = slice(i * box_len, (i + 1) * box_len)
            high, low = split(part)
            stage[at, :lanes] = high
            stage[at, lanes:] = low

    def second(c, carry):
        hits = halves(dot(stage[...], t["lane_back"][...]))
        for i in range(CHUNK):
            s = c * CHUNK + i
            rows = pl.ds(shifts[1, s] + MAX_SHIFT, box_len)
            hit = hits[i * box_len : (i + 1) * box_len]
            one, two = sums[2 * (i % 2)], sums[2 * (i % 2) + 1]
            one[rows, :] += pr[s] * hit
            two[rows, :] += pi[s] * hit
        return carry

    skewed(count, first, second, 0)
    return (sums[0][...] + sums[2][...] + swap(sums[1][...] + sums[3][...])) * scale


def tile_of(k, tile, tiles):
    return lax.rem(tile + tiles - k, tiles)


def mask_grads(params, ids, backs, t, tile, tiles, zed, wins, grads):
    grid = backs[0].shape[0]
    tile_len = wins.shape[2]
    rows = []
    for back in backs:
        high, low = split(back[...])
        rows.append(jnp.concatenate([high, low, high], 1))
    mid = dot(jnp.concatenate(rows, 0), t["grad_cols"][...])
    wins[0, MARGIN + tile_len :, :] = jnp.zeros((MARGIN, tile_len), f32)
    wins[tiles + 1, :MARGIN, :] = jnp.zeros((MARGIN, tile_len), f32)
    for k in range(tiles):
        part = mid[k * grid : (k + 1) * grid]
        high, low = split(jnp.concatenate([part[:, :tile_len], part[:, tile_len:]], 0))
        out = dot(t["grad_rows"][...], jnp.concatenate([high, low, high], 0))
        wins[tile_of(k, tile, tiles) + 1] = out
    square = jnp.zeros((8, tile_len), f32)
    for k in range(tiles):
        own = ids[k]
        for low_row, high_row, near, shift in (
            (0, MARGIN, 0, tile_len),
            (MARGIN, tile_len - MARGIN, 1, 0),
            (tile_len - MARGIN, tile_len, 2, -tile_len),
        ):
            total = wins[own + 1, MARGIN + low_row : MARGIN + high_row, :]
            if near != 1:
                at = MARGIN + low_row + shift
                total = total + wins[own + near, at : at + MARGIN, :]
            lean = half_tanh(params(k, low_row, high_row))
            grad = total * (1.0 - lean * lean)
            grads[own, low_row:high_row, :] = grad
            square = square + jnp.sum((grad * grad).reshape(-1, 8, tile_len), axis=0)
    total = jnp.sum(jnp.sum(square, axis=0, keepdims=True), axis=1, keepdims=True)
    pixels = tiles * tile_len * tile_len
    return MASK_RATE / jnp.sqrt(total / pixels + TINY_EPS)


def edge_rows(tile, tiles, tile_len):
    above = pl.multiple_of(jnp.maximum(tile * tile_len - MARGIN, 0), MARGIN)
    below = jnp.minimum((tile + 1) * tile_len, tiles * tile_len - MARGIN)
    below = pl.multiple_of(below, MARGIN)
    return above, below, (tile > 0).astype(f32), (tile < tiles - 1).astype(f32)


def target_kernel(names, target, *refs):
    t = dict(zip(names, refs))
    out = refs[len(names)]
    grid = out.shape[0]
    high, low = split(target[...])
    rows = t["target_rows"]
    both = dot(rows[...], high)
    mid = both[:grid] + both[grid:] + dot(rows[:grid, :], low)
    high, low = split(mid)
    cols = t["target_cols"]
    out[...] = halves(dot(high, cols[...])) + dot(low, cols[:, : 2 * grid])


def pack_kernel(place, weights, shifts, out):
    local = weights.shape[1]
    out[...] = jnp.zeros_like(out)
    out[0:1, :local] = weights[...]
    out[1:3, :local] = shifts[...].astype(f32)
    out[3:4, :local] = jnp.sqrt(weights[...])
    out[...] = pltpu.roll(out[...], place[0] * local, 1)


def doses(info, scale):
    dose = jnp.sum(info[0:1, :], axis=1, keepdims=True)
    return 1.0 / dose, scale / dose


def first_kernel(names, peers, tiles, scale, tile, pupil_re, pupil_im, target,
                 own, before, after, *refs):
    parts = refs[:peers]
    t = dict(zip(names, refs[peers:]))
    back, pr, pi, info, whole = refs[peers + len(names) : peers + len(names) + 5]
    (plain, crossed, fields, stage, hold, *sums, shifts, roots, sems) = refs[
        peers + len(names) + 5 :
    ]
    here = tile[0]
    total = parts[0][...]
    for part in parts[1:]:
        total = total + part[...]
    info[...] = total
    whole[...] = total.astype(jnp.int32)
    copies = (
        pltpu.make_async_copy(whole, shifts, sems.at[0]),
        pltpu.make_async_copy(info, roots, sems.at[1]),
    )
    for copy in copies:
        copy.start()
    has_prev = (here > 0).astype(f32)
    has_next = (here < tiles - 1).astype(f32)
    window = jnp.concatenate(
        [sigmoid(before[...]) * has_prev, sigmoid(own[...]), sigmoid(after[...]) * has_next], 0
    )
    spec = window_spectrum(window, t)
    for copy in copies:
        copy.wait()
    place_pupils(shifts, roots, pupil_re, pupil_im, pr, pi)
    power = grid_fields(spec, shifts, t, pr, pi, (plain, crossed, fields, stage))
    inv_dose, factor = doses(total, scale)
    misfit = grid_misfit(power, inv_dose, target[...], t)
    back[...] = gather_back(misfit, shifts, factor, t, pr, pi, fields, hold, sums)


def next_kernel(names, tiles, scale, tile, shifts, info, pr, pi, target, *refs):
    params, backs = refs[:tiles], refs[tiles : 2 * tiles]
    refs = refs[2 * tiles :]
    t = dict(zip(names, refs))
    new, back, plain, crossed, fields, stage, hold, *rest = refs[len(names) :]
    sums, (wins, grads) = rest[:4], rest[4:]
    here = tile[0]
    tile_len = params[0].shape[0]
    ids = entry_ids(here, tiles)
    rate = mask_grads(
        lambda k, low, high: params[k][low:high, :], ids, backs, t, here, tiles, None, wins, grads
    )
    for k in range(tiles):
        own = ids[k]
        at = pl.ds(pl.multiple_of(own * tile_len, tile_len), tile_len)
        new[at, :] = params[k][...] - grads[own] * rate
    above, below, has_prev, has_next = edge_rows(here, tiles, tile_len)
    own = pl.ds(pl.multiple_of(here * tile_len, tile_len), tile_len)
    window = jnp.concatenate(
        [
            sigmoid(new[pl.ds(above, MARGIN), :]) * has_prev,
            sigmoid(new[own, :]),
            sigmoid(new[pl.ds(below, MARGIN), :]) * has_next,
        ],
        0,
    )
    spec = window_spectrum(window, t)
    power = grid_fields(spec, shifts, t, pr, pi, (plain, crossed, fields, stage))
    inv_dose, factor = doses(info[...], scale)
    misfit = grid_misfit(power, inv_dose, target[...], t)
    back[...] = gather_back(misfit, shifts, factor, t, pr, pi, fields, hold, sums)


def last_kernel(names, tiles, tile, shifts, info, pr, pi, target, params, *refs):
    backs = refs[:tiles]
    refs = refs[tiles:]
    t = dict(zip(names, refs))
    final, row, plain, crossed, fields, stage, terms, wins, grads = refs[len(names) :]
    here = tile[0]
    tile_len = final.shape[0]
    rate = mask_grads(
        lambda k, low, high: params[k * tile_len + low : k * tile_len + high, :],
        list(range(tiles)), backs, t, here, tiles, None, wins, grads,
    )
    above, below, has_prev, has_next = edge_rows(here, tiles, tile_len)
    own = pl.ds(pl.multiple_of(here * tile_len, tile_len), tile_len)
    final[...] = params[own, :] - grads[here] * rate
    prev, follow = jnp.maximum(here - 1, 0), jnp.minimum(here + 1, tiles - 1)
    window = jnp.concatenate(
        [
            sigmoid(params[pl.ds(above, MARGIN), :] - grads[prev, tile_len - MARGIN :, :] * rate)
            * has_prev,
            sigmoid(final[...]),
            sigmoid(params[pl.ds(below, MARGIN), :] - grads[follow, :MARGIN, :] * rate)
            * has_next,
        ],
        0,
    )
    spec = window_spectrum(window, t)
    power = grid_fields(spec, shifts, t, pr, pi, (plain, crossed, fields, stage))
    inv_dose, _ = doses(info[...], 1.0)
    misfit = grid_misfit(power, inv_dose, target[...], t)

    def chunk(c, carry):
        rows = []
        for i in range(CHUNK):
            field = fields[c * CHUNK + i]
            rows.append(jnp.sum(field * field * misfit, axis=0, keepdims=True))
        terms[pl.ds(pl.multiple_of(c * CHUNK, CHUNK), CHUNK), :] = jnp.concatenate(rows, 0)
        return carry

    count = fields.shape[0]
    lax.fori_loop(0, count // CHUNK, chunk, 0)
    high, low = split(terms[...])
    left = terms[...] - high.astype(f32) - low.astype(f32)
    ones = jnp.ones((8, terms.shape[1]), bf16)
    total = jnp.zeros((8, terms.shape[0]), f32)
    for part in (left.astype(bf16), low, high):
        total = total + lax.dot_general(
            ones, part, (((1,), (1,)), ((), ())), preferred_element_type=f32
        )
    row[...] = total


def weight_kernel(tiles, scale, tile, place, info, *refs):
    rows = refs[:tiles]
    out, stack = refs[tiles:]
    count = rows[0].shape[1]
    for k in range(tiles):
        stack[k] = rows[k][...]
    here = tile[0]
    total = stack[lax.rem(here, tiles)]
    for k in range(1, tiles):
        total = total + stack[tile_of(k, here, tiles)]
    summed = total[0:1] * scale
    weight = info[0:1, :count]
    dose = jnp.sum(weight, axis=1, keepdims=True)
    mean = jnp.sum(summed, axis=1, keepdims=True) / dose
    grad = (summed / weight - mean) / dose
    spread = jnp.sqrt(jnp.sum(grad * grad, axis=1, keepdims=True) / count + TINY_EPS)
    new = weight * jnp.exp(-WEIGHT_RATE * grad / spread)
    size = out.shape[1]
    lanes = info.shape[1]
    if count < lanes:
        new = jnp.concatenate([new, jnp.zeros((1, lanes - count), f32)], 1)
    new = pltpu.roll(jnp.broadcast_to(new, (8, lanes)), lanes - place[0] * size, 1)
    out[...] = new[0:1, :size]


def ring(value, axis):
    peers = lax.axis_size(axis)
    return [value] + [
        lax.ppermute(value, axis, [(i, (i + k) % peers) for i in range(peers)])
        for k in range(1, peers)
    ]


def mates(value):
    return lax.ppermute(value, "tile", [(i, i ^ 1) for i in range(lax.axis_size("tile"))])


def far_steps(tiles):
    return range(2, tiles, 2)


def entry_ids(tile, tiles):
    even = [tile] + [tile_of(k, tile, tiles) for k in far_steps(tiles)]
    return even + [one + 1 - 2 * lax.rem(one, 2) for one in even]


def per_device(mask_param, target_image, source_weights, source_shifts, pupil_map):
    tile_len = mask_param.shape[1]
    box_len = pupil_map.shape[1]
    grid = box_len + 2 * MAX_SHIFT
    lanes = 2 * grid
    tiles = lax.axis_size("tile")
    peers = lax.axis_size("src")
    local = source_weights.shape[0]
    count = local * peers
    assert tiles % 2 == 0 and count <= 128 and count % CHUNK == 0
    tables = make_tables(tile_len, box_len, MAX_SHIFT)

    tile = lax.axis_index("tile").astype(jnp.int32).reshape(1)
    place = lax.axis_index("src").astype(jnp.int32).reshape(1)

    vmem = pl.BlockSpec(memory_space=pltpu.VMEM)
    smem = pl.BlockSpec(memory_space=pltpu.SMEM)
    params_of = pltpu.CompilerParams(vmem_limit_bytes=48 << 20)

    def struct(*shape, kind=f32):
        return jax.ShapeDtypeStruct(shape, kind)

    def pick(*names):
        return names, [jnp.asarray(tables[n]) for n in names]

    def cost(flops):
        return pl.CostEstimate(flops=flops, bytes_accessed=1 << 20, transcendentals=0)

    down = [(i, (i + 1) % tiles) for i in range(tiles)]
    up = [(j, i) for i, j in down]
    before = lax.ppermute(mask_param[-MARGIN:], "tile", down)
    after = lax.ppermute(mask_param[:MARGIN], "tile", up)

    packed = pl.pallas_call(
        pack_kernel,
        out_shape=struct(8, 128),
        in_specs=[smem, vmem, vmem],
        out_specs=vmem,
        compiler_params=params_of,
        name="pack_sources",
    )(place, source_weights[None], source_shifts.T)
    packed = ring(packed, "src")

    pad = ((0, 0), (0, grid - box_len))
    real, imag = jnp.pad(pupil_map[0], pad), jnp.pad(pupil_map[1], pad)
    pupil_re = jnp.concatenate([real, real], 1)
    pupil_im = jnp.concatenate([-imag, imag], 1)

    names, values = pick("target_rows", "target_cols")
    target = pl.pallas_call(
        functools.partial(target_kernel, names),
        out_shape=struct(grid, lanes),
        in_specs=[vmem] * (1 + len(names)),
        out_specs=vmem,
        compiler_params=params_of,
        cost_estimate=cost(1 << 26),
        name="target_terms",
    )(target_image, *values)

    before, after, packed, source = lax.optimization_barrier((before, after, packed, mask_param))
    far = [
        lax.ppermute(source, "tile", [(i, (i + k) % tiles) for i in range(tiles)])
        for k in far_steps(tiles)
    ]
    mate = mates(source)

    work = [
        pltpu.VMEM((grid, lanes), f32),
        pltpu.VMEM((grid, lanes), f32),
        pltpu.VMEM((count, grid, lanes), f32),
        pltpu.VMEM((4 * box_len, CHUNK * lanes), bf16),
    ]
    hold = [pltpu.VMEM((CHUNK * box_len, 2 * lanes), bf16)]
    hold = hold + [pltpu.VMEM((grid, lanes), f32)] * 4
    steps = [
        pltpu.VMEM((tiles + 2, tile_len + 2 * MARGIN, tile_len), f32),
        pltpu.VMEM((tiles, tile_len, tile_len), f32),
    ]
    period = tile_len + 2 * MARGIN
    scale = 0.5 / (grid * grid * period * tile_len)
    source_len = struct(count, box_len, lanes)

    fwd = ("spec_cols", "spec_rows", "lane_fwd", "row_fwd", "mix_cols", "mix_rows")
    names, values = pick(*fwd, "lane_back", "row_back")
    back, pr, pi, info, whole = pl.pallas_call(
        functools.partial(first_kernel, names, peers, tiles, scale),
        out_shape=[struct(grid, lanes), source_len, source_len, struct(8, 128),
                   struct(8, 128, kind=jnp.int32)],
        in_specs=[smem] + [vmem] * (6 + peers + len(names)),
        out_specs=[vmem] * 5,
        scratch_shapes=work + hold + [
            pltpu.SMEM((8, 128), jnp.int32),
            pltpu.SMEM((8, 128), f32),
            pltpu.SemaphoreType.DMA((2,)),
        ],
        compiler_params=params_of,
        cost_estimate=cost(1 << 32),
        name="first_step",
    )(tile, pupil_re, pupil_im, target, mask_param, before, after, *packed, *values)

    shared = (tile, whole, info, pr, pi, target)
    shared_specs = [smem, smem] + [vmem] * 4

    backs = ring(back, "tile")
    entries = [mask_param, *far, mate, *[mates(one) for one in far]]
    names, values = pick(*fwd, "lane_back", "row_back", "grad_cols", "grad_rows")
    params, back = pl.pallas_call(
        functools.partial(next_kernel, names, tiles, scale),
        out_shape=[struct(tiles * tile_len, tile_len), struct(grid, lanes)],
        in_specs=shared_specs + [vmem] * (2 * tiles + len(names)),
        out_specs=[vmem] * 2,
        scratch_shapes=work + hold + steps,
        compiler_params=params_of,
        cost_estimate=cost(1 << 32),
        name="next_step",
    )(*shared, *entries, *backs, *values)

    backs = ring(back, "tile")
    names, values = pick(*fwd, "grad_cols", "grad_rows")
    final, row = pl.pallas_call(
        functools.partial(last_kernel, names, tiles),
        out_shape=[struct(tile_len, tile_len), struct(8, count)],
        in_specs=shared_specs + [vmem] * (1 + tiles + len(names)),
        out_specs=[vmem] * 2,
        scratch_shapes=work + [pltpu.VMEM((count, lanes), f32)] + steps,
        compiler_params=params_of,
        cost_estimate=cost(1 << 32),
        name="last_step",
    )(*shared, params, *backs, *values)

    rows = ring(row, "tile")
    out = pl.pallas_call(
        functools.partial(weight_kernel, tiles, 1.0 / (grid * grid)),
        out_shape=struct(1, local),
        in_specs=[smem] * 2 + [vmem] * (1 + tiles),
        out_specs=vmem,
        scratch_shapes=[pltpu.VMEM((tiles, 8, count), f32)],
        compiler_params=params_of,
        name="weight_step",
    )(tile, place, info, *rows)
    return final, out.reshape(local)


def solution(mesh):
    in_specs = (
        P(("group", "tile"), None),
        P(("group", "tile"), None),
        P(("group", "src")),
        P("src", None),
        P(),
    )
    out_specs = (P(("group", "tile"), None), P(("group", "src")))
    return jax.shard_map(
        per_device, mesh=mesh, in_specs=in_specs, out_specs=out_specs, check_vma=False
    )
```

```python
import functools
import math

import jax
import jax.numpy as jnp
import ml_dtypes
import numpy as np
from jax import lax
from jax.experimental import pallas as pl
from jax.experimental.pallas import tpu as pltpu
from jax.sharding import PartitionSpec as P

MARGIN = 64
MAX_SHIFT = 16
MASK_RATE = 0.5
WEIGHT_RATE = 0.3
TINY_EPS = 1e-06
CHUNK = 16

bf16 = jnp.bfloat16
f32 = jnp.float32


def np_split(table):
    table = np.asarray(table, np.float64)
    high = table.astype(np.float32).astype(ml_dtypes.bfloat16)
    low = (table - high.astype(np.float64)).astype(np.float32).astype(ml_dtypes.bfloat16)
    return high, low


def phases(freqs, pixels, period):
    return 2.0 * math.pi * np.mod(np.outer(freqs, pixels), period) / period


def make_tables(tile_len, box_len, max_shift):
    period = tile_len + 2 * MARGIN
    grid = box_len + 2 * max_shift
    wide = np.arange(grid) - grid // 2
    pix = np.arange(tile_len)
    full = np.arange(period)
    points = np.arange(grid)
    box = np.arange(box_len)
    out = {}
    ang = phases(wide, pix, period)
    high, low = np_split(np.concatenate([np.cos(ang), -np.sin(ang)], 0).T / (period * tile_len))
    out["spec_cols"] = np.concatenate([high, low], 1)
    ang_rows = phases(wide, full, period)
    high, low = np_split(np.concatenate([np.cos(ang_rows), np.sin(ang_rows)], 0))
    out["spec_rows"] = np.concatenate([high, low], 0)
    ang = phases(points, points, grid)
    cos, sin = np.cos(ang), np.sin(ang)
    for name, table in (
        ("lane_fwd", np.block([[cos, sin], [-sin, cos]])),
        ("lane_back", np.block([[cos, -sin], [sin, cos]])),
    ):
        high, low = np_split(table)
        out[name] = np.block([[high, low], [high, np.zeros_like(low)]])
    ang = phases(points, box, grid)
    high, low = np_split(np.concatenate([np.cos(ang), np.sin(ang)], 1))
    out["row_fwd"] = np.concatenate([high, high, low], 1)
    high, low = np_split(np.concatenate([np.cos(ang).T, np.sin(ang).T], 0))
    out["row_back"] = np.concatenate([high, high, low], 1)
    def dirichlet(offset):
        theta = 2.0 * math.pi * ((pix + offset)[None, :] / period - points[:, None] / grid)
        orders = np.arange(1, box_len)
        return 1.0 + 2.0 * np.cos(orders[:, None, None] * theta[None]).sum(0)

    rows, cols = dirichlet(MARGIN), dirichlet(0)
    high, low = np_split(rows @ rows.T / grid)
    out["mix_rows"] = np.concatenate([high, high, low], 1)
    mix = cols @ cols.T / grid
    high, low = np_split(np.block([[mix, mix], [mix, mix]]))
    out["mix_cols"] = np.block([[high, low], [high, np.zeros_like(low)]])
    high, low = np_split(rows)
    out["target_rows"] = np.concatenate([high, low], 0)
    high, low = np_split(np.concatenate([cols, cols], 0).T)
    out["target_cols"] = np.concatenate([high, low], 1)
    ang = phases(wide, pix, period)
    cos, sin = np.cos(ang), np.sin(ang)
    high, low = np_split(np.block([[cos, sin], [-sin, cos]]))
    out["grad_cols"] = np.concatenate([high, high, low], 0)
    high, low = np_split(np.concatenate([np.cos(ang_rows).T, -np.sin(ang_rows).T], 1))
    out["grad_rows"] = np.concatenate([high, high, low], 1)
    return out


def pack_tables(tables):
    wide = [n for n in tables if tables[n].shape[1] > 256]
    narrow = sorted((n for n in tables if n not in wide), key=lambda n: -tables[n].shape[0])
    place, heights = {}, [0, 0]
    for n in wide:
        place[n] = (heights[0], 0)
        heights = [heights[0] + tables[n].shape[0]] * 2
    for n in narrow:
        side = int(heights[1] < heights[0])
        place[n] = (heights[side], 256 * side)
        heights[side] += tables[n].shape[0]
    whole = np.zeros((max(heights), 512), ml_dtypes.bfloat16)
    spots = {}
    for n, (row, col) in place.items():
        rows, cols = tables[n].shape
        whole[row : row + rows, col : col + cols] = tables[n]
        spots[n] = (slice(row, row + rows), slice(col, col + cols))
    return whole, spots


def split(value):
    high = value.astype(bf16)
    return high, (value - high.astype(f32)).astype(bf16)


def dot(left, right):
    return jnp.dot(left, right, preferred_element_type=f32)


def halves(value):
    width = value.shape[1] // 2
    return value[:, :width] + value[:, width:]


def lane_sign(rows, lanes, first):
    lane = lax.broadcasted_iota(jnp.int32, (rows, lanes), 1)
    return jnp.where(lane < lanes // 2, first, -first).astype(f32)


def swap(value):
    return pltpu.roll(value, value.shape[1] // 2, 1)


def half_tanh(value):
    return jnp.tanh(0.5 * value)


def sigmoid(value):
    return 0.5 * half_tanh(value) + 0.5


def window_spectrum(window, t):
    grid = t["spec_cols"].shape[1] // 4
    high, low = split(window)
    cols = t["spec_cols"]
    mid = halves(dot(high, cols[...])) + dot(low, cols[:, : 2 * grid])
    mid_high, mid_low = split(mid)
    rows = t["spec_rows"]
    both = halves(dot(rows[: 2 * grid, :], jnp.concatenate([mid_high, mid_low], 1)))
    both = both + dot(rows[2 * grid :, :], mid_high)
    return both[:grid] + lane_sign(grid, 2 * grid, 1.0) * swap(both[grid:])


def skewed(count, stages, first, second, carry):
    chunks = count // CHUNK
    first(0, stages[0])
    for c in range(1, chunks):
        first(c, stages[c % 2])
        carry = second(c - 1, stages[(c - 1) % 2], carry)
    return second(chunks - 1, stages[(chunks - 1) % 2], carry)


def placed_pupils(shifts, roots, pupil_re, pupil_im, pr, pi):
    def make(s):
        by = shifts[2, s] + MAX_SHIFT
        real = pltpu.roll(pupil_re[...] * roots[3, s], by, 1)
        imag = pltpu.roll(pupil_im[...] * roots[3, s], by, 1)
        pr[s], pi[s] = real, imag
        return real, imag

    return make


def grid_fields(spec, shifts, t, pupils, work):
    plain, crossed, fields, *stages = work
    count, grid, lanes = fields.shape
    box_len = t["row_fwd"].shape[1] // 6
    plain[...] = spec
    crossed[...] = swap(spec)
    sign = lane_sign(box_len, lanes, -1.0)

    def first(c, stage):
        rows = []
        for i in range(CHUNK):
            s = c * CHUNK + i
            at = pl.ds(shifts[1, s] + MAX_SHIFT, box_len)
            real, imag = pupils(s)
            high, low = split(real * plain[at, :] + imag * crossed[at, :])
            rows.append(jnp.concatenate([high, low], 1))
        stage[...] = halves(dot(jnp.concatenate(rows, 0), t["lane_fwd"][...]))

    def second(c, stage, power):
        stacks = []
        for i in range(CHUNK):
            part = stage[i * box_len : (i + 1) * box_len, :]
            high, low = split(jnp.concatenate([part, sign * swap(part)], 0))
            stacks.append(jnp.concatenate([high, low, high], 0))
        out = dot(t["row_fwd"][...], jnp.concatenate(stacks, 1))
        for i in range(CHUNK):
            field = out[:, i * lanes : (i + 1) * lanes]
            fields[c * CHUNK + i] = field
            power = power + field * field
        return power

    return skewed(count, stages, first, second, jnp.zeros((grid, lanes), f32))


def grid_misfit(power, inv_dose, target, t):
    high, low = split(power)
    mid = halves(dot(jnp.concatenate([high, low], 1), t["mix_cols"][...]))
    high, low = split(mid)
    lit = dot(t["mix_rows"][...], jnp.concatenate([high, low, high], 0))
    return lit * inv_dose - target


def gather_back(misfit, shifts, scale, t, pr, pi, fields, stages, sums):
    count, box_len, lanes = pr.shape
    for ref in sums:
        ref[...] = jnp.zeros_like(ref)
    sign = lane_sign(box_len, lanes, 1.0)

    def first(c, stage):
        stacks = []
        for i in range(CHUNK):
            high, low = split(fields[c * CHUNK + i] * misfit)
            stacks.append(jnp.concatenate([high, low, high], 0))
        both = dot(t["row_back"][...], jnp.concatenate(stacks, 1))
        for i in range(CHUNK):
            part = both[:, i * lanes : (i + 1) * lanes]
            stage[i * box_len : (i + 1) * box_len, :] = part[:box_len] + sign * swap(
                part[box_len:]
            )

    def second(c, stage, carry):
        high, low = split(stage[...])
        hits = halves(dot(jnp.concatenate([high, low], 1), t["lane_back"][...]))
        for i in range(CHUNK):
            s = c * CHUNK + i
            rows = pl.ds(shifts[1, s] + MAX_SHIFT, box_len)
            hit = hits[i * box_len : (i + 1) * box_len]
            one, two = sums[2 * (i % 2)], sums[2 * (i % 2) + 1]
            one[rows, :] += pr[s] * hit
            two[rows, :] += pi[s] * hit
        return carry

    skewed(count, stages, first, second, 0)
    return (sums[0][...] + sums[2][...] + swap(sums[1][...] + sums[3][...])) * scale


def tile_of(k, tile, tiles):
    return lax.rem(tile + tiles - k, tiles)


def mask_grads(params, ids, backs, t, tile, tiles, wins, grads):
    grid = backs[0].shape[0]
    tile_len = wins.shape[2]
    rows = []
    for back in backs:
        high, low = split(back[...])
        rows.append(jnp.concatenate([high, low, high], 1))
    mid = dot(jnp.concatenate(rows, 0), t["grad_cols"][...])
    wins[0, MARGIN + tile_len :, :] = jnp.zeros((MARGIN, tile_len), f32)
    wins[tiles + 1, :MARGIN, :] = jnp.zeros((MARGIN, tile_len), f32)
    for k in range(tiles):
        part = mid[k * grid : (k + 1) * grid]
        high, low = split(jnp.concatenate([part[:, :tile_len], part[:, tile_len:]], 0))
        out = dot(t["grad_rows"][...], jnp.concatenate([high, low, high], 0))
        wins[tile_of(k, tile, tiles) + 1] = out
    square = jnp.zeros((8, tile_len), f32)
    for k in range(tiles):
        own = ids[k]
        for low_row, high_row, near, shift in (
            (0, MARGIN, 0, tile_len),
            (MARGIN, tile_len - MARGIN, 1, 0),
            (tile_len - MARGIN, tile_len, 2, -tile_len),
        ):
            total = wins[own + 1, MARGIN + low_row : MARGIN + high_row, :]
            if near != 1:
                at = MARGIN + low_row + shift
                total = total + wins[own + near, at : at + MARGIN, :]
            lean = half_tanh(params(k, low_row, high_row))
            grad = total * (1.0 - lean * lean)
            grads[own, low_row:high_row, :] = grad
            square = square + jnp.sum((grad * grad).reshape(-1, 8, tile_len), axis=0)
    total = jnp.sum(jnp.sum(square, axis=0, keepdims=True), axis=1, keepdims=True)
    pixels = tiles * tile_len * tile_len
    return MASK_RATE / jnp.sqrt(total / pixels + TINY_EPS)


def edge_rows(tile, tiles, tile_len):
    above = pl.multiple_of(jnp.maximum(tile * tile_len - MARGIN, 0), MARGIN)
    below = jnp.minimum((tile + 1) * tile_len, tiles * tile_len - MARGIN)
    below = pl.multiple_of(below, MARGIN)
    return above, below, (tile > 0).astype(f32), (tile < tiles - 1).astype(f32)


def start_all(pairs, sems):
    copies = [pltpu.make_async_copy(a, b, sems.at[i]) for i, (a, b) in enumerate(pairs)]
    for copy in copies:
        copy.start()
    return copies


def open_kernel(place, mask, weights, shifts, own, top, low, packed, hold_w, hold_s, sems):
    rows, local = mask.shape[0], weights.shape[1]
    copies = start_all(
        (
            (weights, hold_w),
            (shifts, hold_s),
            (mask.at[pl.ds(0, MARGIN), :], top),
            (mask.at[pl.ds(rows - MARGIN, MARGIN), :], low),
            (mask, own),
        ),
        sems,
    )
    copies[0].wait()
    copies[1].wait()
    packed[...] = jnp.zeros_like(packed)
    packed[0:1, :local] = hold_w[...]
    packed[1:3, :local] = hold_s[...].astype(f32)
    packed[3:4, :local] = jnp.sqrt(hold_w[...])
    packed[...] = pltpu.roll(packed[...], place[0] * local, 1)
    for copy in copies[2:]:
        copy.wait()


def target_kernel(spots, target, pupil, whole, out, pupil_re, pupil_im):
    grid, size = out.shape[0], pupil.shape[1]
    pupil_re[...] = jnp.zeros_like(pupil_re)
    pupil_im[...] = jnp.zeros_like(pupil_im)
    pupil_re[:, :size] = pupil[0]
    pupil_re[:, grid : grid + size] = pupil[0]
    pupil_im[:, :size] = -pupil[1]
    pupil_im[:, grid : grid + size] = pupil[1]
    rows, cols = whole.at[spots["target_rows"]], whole.at[spots["target_cols"]]
    high, low = split(target[...])
    both = dot(rows[...], high)
    mid = both[:grid] + both[grid:] + dot(rows[:grid, :], low)
    high, low = split(mid)
    out[...] = halves(dot(high, cols[...])) + dot(low, cols[:, : 2 * grid])


def doses(info, scale):
    dose = jnp.sum(info[0:1, :], axis=1, keepdims=True)
    return 1.0 / dose, scale / dose


def first_kernel(spots, peers, tiles, scale, tile, table, pupil_re, pupil_im, target,
                 own, before, after, *refs):
    parts = refs[:peers]
    t = {n: table.at[spot] for n, spot in spots.items()}
    back, pr, pi, info, whole = refs[peers : peers + 5]
    *work, s0, s1, s2, s3, shifts, roots, sems = refs[peers + 5 :]
    here = tile[0]
    total = parts[0][...]
    for part in parts[1:]:
        total = total + part[...]
    info[...] = total
    whole[...] = total.astype(jnp.int32)
    copies = (
        pltpu.make_async_copy(whole, shifts, sems.at[0]),
        pltpu.make_async_copy(info, roots, sems.at[1]),
    )
    for copy in copies:
        copy.start()
    has_prev = (here > 0).astype(f32)
    has_next = (here < tiles - 1).astype(f32)
    window = jnp.concatenate(
        [sigmoid(before[...]) * has_prev, sigmoid(own[...]), sigmoid(after[...]) * has_next], 0
    )
    spec = window_spectrum(window, t)
    for copy in copies:
        copy.wait()
    pupils = placed_pupils(shifts, roots, pupil_re, pupil_im, pr, pi)
    power = grid_fields(spec, shifts, t, pupils, work)
    inv_dose, factor = doses(total, scale)
    misfit = grid_misfit(power, inv_dose, target[...], t)
    sums = (s0, s1, s2, s3)
    back[...] = gather_back(misfit, shifts, factor, t, pr, pi, work[2], work[3:], sums)


def next_kernel(spots, tiles, scale, tile, table, shifts, info, pr, pi, target, *refs):
    params, backs = refs[:tiles], refs[tiles : 2 * tiles]
    t = {n: table.at[spot] for n, spot in spots.items()}
    new, back, *work, s0, s1, s2, s3, wins, grads = refs[2 * tiles :]
    here = tile[0]
    tile_len = params[0].shape[0]
    ids = entry_ids(here, tiles)
    rate = mask_grads(
        lambda k, low, high: params[k][low:high, :], ids, backs, t, here, tiles, wins, grads
    )
    for k in range(tiles):
        own = ids[k]
        at = pl.ds(pl.multiple_of(own * tile_len, tile_len), tile_len)
        new[at, :] = params[k][...] - grads[own] * rate
    above, below, has_prev, has_next = edge_rows(here, tiles, tile_len)
    own = pl.ds(pl.multiple_of(here * tile_len, tile_len), tile_len)
    window = jnp.concatenate(
        [
            sigmoid(new[pl.ds(above, MARGIN), :]) * has_prev,
            sigmoid(new[own, :]),
            sigmoid(new[pl.ds(below, MARGIN), :]) * has_next,
        ],
        0,
    )
    spec = window_spectrum(window, t)
    power = grid_fields(spec, shifts, t, lambda s: (pr[s], pi[s]), work)
    inv_dose, factor = doses(info[...], scale)
    misfit = grid_misfit(power, inv_dose, target[...], t)
    sums = (s0, s1, s2, s3)
    back[...] = gather_back(misfit, shifts, factor, t, pr, pi, work[2], work[3:], sums)


def last_kernel(spots, tiles, tile, table, shifts, info, pr, pi, target, params, *refs):
    backs = refs[:tiles]
    t = {n: table.at[spot] for n, spot in spots.items()}
    final, row, *work, terms, wins, grads = refs[tiles:]
    fields = work[2]
    here = tile[0]
    tile_len = final.shape[0]
    rate = mask_grads(
        lambda k, low, high: params[k * tile_len + low : k * tile_len + high, :],
        list(range(tiles)), backs, t, here, tiles, wins, grads,
    )
    above, below, has_prev, has_next = edge_rows(here, tiles, tile_len)
    own = pl.ds(pl.multiple_of(here * tile_len, tile_len), tile_len)
    final[...] = params[own, :] - grads[here] * rate
    prev, follow = jnp.maximum(here - 1, 0), jnp.minimum(here + 1, tiles - 1)
    window = jnp.concatenate(
        [
            sigmoid(params[pl.ds(above, MARGIN), :] - grads[prev, tile_len - MARGIN :, :] * rate)
            * has_prev,
            sigmoid(final[...]),
            sigmoid(params[pl.ds(below, MARGIN), :] - grads[follow, :MARGIN, :] * rate)
            * has_next,
        ],
        0,
    )
    spec = window_spectrum(window, t)
    power = grid_fields(spec, shifts, t, lambda s: (pr[s], pi[s]), work)
    inv_dose, _ = doses(info[...], 1.0)
    misfit = grid_misfit(power, inv_dose, target[...], t)

    def chunk(c, carry):
        rows = []
        for i in range(CHUNK):
            field = fields[c * CHUNK + i]
            rows.append(jnp.sum(field * field * misfit, axis=0, keepdims=True))
        terms[pl.ds(pl.multiple_of(c * CHUNK, CHUNK), CHUNK), :] = jnp.concatenate(rows, 0)
        return carry

    count = fields.shape[0]
    lax.fori_loop(0, count // CHUNK, chunk, 0)
    high, low = split(terms[...])
    left = terms[...] - high.astype(f32) - low.astype(f32)
    ones = jnp.ones((8, terms.shape[1]), bf16)
    total = jnp.zeros((8, terms.shape[0]), f32)
    for part in (left.astype(bf16), low, high):
        total = total + lax.dot_general(
            ones, part, (((1,), (1,)), ((), ())), preferred_element_type=f32
        )
    row[...] = total


def weight_kernel(tiles, scale, tile, place, info, *refs):
    rows = refs[:tiles]
    out, stack = refs[tiles:]
    count = rows[0].shape[1]
    for k in range(tiles):
        stack[k] = rows[k][...]
    here = tile[0]
    total = stack[lax.rem(here, tiles)]
    for k in range(1, tiles):
        total = total + stack[tile_of(k, here, tiles)]
    summed = total[0:1] * scale
    weight = info[0:1, :count]
    dose = jnp.sum(weight, axis=1, keepdims=True)
    mean = jnp.sum(summed, axis=1, keepdims=True) / dose
    grad = (summed / weight - mean) / dose
    spread = jnp.sqrt(jnp.sum(grad * grad, axis=1, keepdims=True) / count + TINY_EPS)
    new = weight * jnp.exp(-WEIGHT_RATE * grad / spread)
    size = out.shape[1]
    lanes = info.shape[1]
    if count < lanes:
        new = jnp.concatenate([new, jnp.zeros((1, lanes - count), f32)], 1)
    new = pltpu.roll(jnp.broadcast_to(new, (8, lanes)), lanes - place[0] * size, 1)
    out[...] = new[0:1, :size]


def ring(value, axis):
    peers = lax.axis_size(axis)
    return [value] + [
        lax.ppermute(value, axis, [(i, (i + k) % peers) for i in range(peers)])
        for k in range(1, peers)
    ]


def mates(value):
    return lax.ppermute(value, "tile", [(i, i ^ 1) for i in range(lax.axis_size("tile"))])


def far_steps(tiles):
    return range(2, tiles, 2)


def entry_ids(tile, tiles):
    even = [tile] + [tile_of(k, tile, tiles) for k in far_steps(tiles)]
    return even + [one + 1 - 2 * lax.rem(one, 2) for one in even]


def per_device(mask_param, target_image, source_weights, source_shifts, pupil_map):
    tile_len = mask_param.shape[1]
    box_len = pupil_map.shape[1]
    grid = box_len + 2 * MAX_SHIFT
    lanes = 2 * grid
    tiles = lax.axis_size("tile")
    peers = lax.axis_size("src")
    local = source_weights.shape[0]
    count = local * peers
    assert tiles % 2 == 0 and count <= 128 and count % CHUNK == 0
    tables = make_tables(tile_len, box_len, MAX_SHIFT)

    tile = lax.axis_index("tile").astype(jnp.int32).reshape(1)
    place = lax.axis_index("src").astype(jnp.int32).reshape(1)

    vmem = pl.BlockSpec(memory_space=pltpu.VMEM)
    smem = pl.BlockSpec(memory_space=pltpu.SMEM)
    left = pl.BlockSpec(memory_space=pltpu.HBM)
    params_of = pltpu.CompilerParams(vmem_limit_bytes=32 << 20)

    def struct(*shape, kind=f32):
        return jax.ShapeDtypeStruct(shape, kind)

    def cost(flops):
        return pl.CostEstimate(flops=flops, bytes_accessed=1 << 20, transcendentals=0)

    own, top, low, packed = pl.pallas_call(
        open_kernel,
        out_shape=[struct(tile_len, tile_len), struct(MARGIN, tile_len),
                   struct(MARGIN, tile_len), struct(8, 128)],
        in_specs=[smem, left, left, left],
        out_specs=[vmem] * 4,
        scratch_shapes=[
            pltpu.VMEM((1, local), f32),
            pltpu.VMEM((2, local), jnp.int32),
            pltpu.SemaphoreType.DMA((5,)),
        ],
        name="open_step",
    )(place, mask_param, source_weights[None], source_shifts.T)
    packed = ring(packed, "src")
    down = [(i, (i + 1) % tiles) for i in range(tiles)]
    up = [(j, i) for i, j in down]
    before = lax.ppermute(low, "tile", down)
    after = lax.ppermute(top, "tile", up)

    whole, spots = pack_tables(tables)
    table = jnp.asarray(whole)
    target, pupil_re, pupil_im = pl.pallas_call(
        functools.partial(target_kernel, spots),
        out_shape=[struct(grid, lanes), struct(box_len, lanes), struct(box_len, lanes)],
        in_specs=[vmem] * 3,
        out_specs=[vmem] * 3,
        compiler_params=params_of,
        cost_estimate=cost(1 << 26),
        name="target_terms",
    )(target_image, pupil_map, table)

    before, after, packed, source = lax.optimization_barrier((before, after, packed, own))
    far = [
        lax.ppermute(source, "tile", [(i, (i + k) % tiles) for i in range(tiles)])
        for k in far_steps(tiles)
    ]
    mate = mates(source)

    work = [
        pltpu.VMEM((grid, lanes), f32),
        pltpu.VMEM((grid, lanes), f32),
        pltpu.VMEM((count, grid, lanes), f32),
        pltpu.VMEM((CHUNK * box_len, lanes), f32),
        pltpu.VMEM((CHUNK * box_len, lanes), f32),
    ]
    hold = [pltpu.VMEM((grid, lanes), f32)] * 4
    steps = [
        pltpu.VMEM((tiles + 2, tile_len + 2 * MARGIN, tile_len), f32),
        pltpu.VMEM((tiles, tile_len, tile_len), f32),
    ]
    period = tile_len + 2 * MARGIN
    scale = 0.5 / (grid * grid * period * tile_len)
    source_len = struct(count, box_len, lanes)

    back, pr, pi, info, whole = pl.pallas_call(
        functools.partial(first_kernel, spots, peers, tiles, scale),
        out_shape=[struct(grid, lanes), source_len, source_len, struct(8, 128),
                   struct(8, 128, kind=jnp.int32)],
        in_specs=[smem] + [vmem] * (7 + peers),
        out_specs=[vmem] * 5,
        scratch_shapes=work + hold + [
            pltpu.SMEM((8, 128), jnp.int32),
            pltpu.SMEM((8, 128), f32),
            pltpu.SemaphoreType.DMA((2,)),
        ],
        compiler_params=params_of,
        cost_estimate=cost(1 << 32),
        name="first_step",
    )(tile, table, pupil_re, pupil_im, target, own, before, after, *packed)

    shared = (tile, table, whole, info, pr, pi, target)
    shared_specs = [smem, vmem, smem] + [vmem] * 4

    back, far = lax.optimization_barrier((back, far))
    backs = ring(back, "tile")
    entries = [own, *far, mate, *[mates(one) for one in far]]
    params, back = pl.pallas_call(
        functools.partial(next_kernel, spots, tiles, scale),
        out_shape=[struct(tiles * tile_len, tile_len), struct(grid, lanes)],
        in_specs=shared_specs + [vmem] * (2 * tiles),
        out_specs=[vmem] * 2,
        scratch_shapes=work + hold + steps,
        compiler_params=params_of,
        cost_estimate=cost(1 << 32),
        name="next_step",
    )(*shared, *entries, *backs)

    backs = ring(back, "tile")
    final, row = pl.pallas_call(
        functools.partial(last_kernel, spots, tiles),
        out_shape=[struct(tile_len, tile_len), struct(8, count)],
        in_specs=shared_specs + [vmem] * (1 + tiles),
        out_specs=[vmem] * 2,
        scratch_shapes=work + [pltpu.VMEM((count, lanes), f32)] + steps,
        compiler_params=params_of,
        cost_estimate=cost(1 << 32),
        name="last_step",
    )(*shared, params, *backs)

    rows = ring(row, "tile")
    out = pl.pallas_call(
        functools.partial(weight_kernel, tiles, 1.0 / (grid * grid)),
        out_shape=struct(1, local),
        in_specs=[smem] * 2 + [vmem] * (1 + tiles),
        out_specs=vmem,
        scratch_shapes=[pltpu.VMEM((tiles, 8, count), f32)],
        compiler_params=params_of,
        name="weight_step",
    )(tile, place, info, *rows)
    return final, out.reshape(local)


def solution(mesh):
    in_specs = (
        P(("group", "tile"), None),
        P(("group", "tile"), None),
        P(("group", "src")),
        P("src", None),
        P(),
    )
    out_specs = (P(("group", "tile"), None), P(("group", "src")))
    return jax.shard_map(
        per_device, mesh=mesh, in_specs=in_specs, out_specs=out_specs, check_vma=False
    )
```

```python
import functools
import math

import jax
import jax.numpy as jnp
import ml_dtypes
import numpy as np
from jax import lax
from jax.experimental import pallas as pl
from jax.experimental.pallas import tpu as pltpu
from jax.sharding import PartitionSpec as P


MARGIN = 64
MAX_SHIFT = 16
MASK_RATE = 0.5
WEIGHT_RATE = 0.3
TINY_EPS = 1e-06
CHUNK = 16


bf16 = jnp.bfloat16
f32 = jnp.float32


def np_split(table):
    table = np.asarray(table, np.float64)
    high = table.astype(np.float32).astype(ml_dtypes.bfloat16)
    low = (table - high.astype(np.float64)).astype(np.float32).astype(ml_dtypes.bfloat16)
    return high, low


def phases(freqs, pixels, period):
    return 2.0 * math.pi * np.mod(np.outer(freqs, pixels), period) / period


def make_tables(tile_len, box_len, max_shift):
    period = tile_len + 2 * MARGIN
    grid = box_len + 2 * max_shift
    wide = np.arange(grid) - grid // 2
    pix = np.arange(tile_len)
    full = np.arange(period)
    points = np.arange(grid)
    box = np.arange(box_len)
    out = {}
    ang = phases(wide, pix, period)
    high, low = np_split(np.concatenate([np.cos(ang), -np.sin(ang)], 0).T / (period * tile_len))
    out["spec_cols"] = np.concatenate([high, low], 1)
    ang_rows = phases(wide, full, period)
    high, low = np_split(np.concatenate([np.cos(ang_rows), np.sin(ang_rows)], 0))
    out["spec_rows"] = np.concatenate([high, low], 0)
    ang = phases(points, points, grid)
    cos, sin = np.cos(ang), np.sin(ang)
    for name, table in (
        ("lane_fwd", np.block([[cos, sin], [-sin, cos]])),
        ("lane_back", np.block([[cos, -sin], [sin, cos]])),
    ):
        high, low = np_split(table)
        out[name] = np.block([[high, low], [high, np.zeros_like(low)]])
    ang = phases(points, box, grid)
    high, low = np_split(np.concatenate([np.cos(ang), np.sin(ang)], 1))
    out["row_fwd"] = np.concatenate([high, high, low], 1)
    high, low = np_split(np.concatenate([np.cos(ang).T, np.sin(ang).T], 0))
    out["row_back"] = np.concatenate([high, high, low], 1)

    def dirichlet(offset):
        theta = 2.0 * math.pi * ((pix + offset)[None, :] / period - points[:, None] / grid)
        orders = np.arange(1, box_len)
        return 1.0 + 2.0 * np.cos(orders[:, None, None] * theta[None]).sum(0)

    rows, cols = dirichlet(MARGIN), dirichlet(0)
    high, low = np_split(rows @ rows.T / grid)
    out["mix_rows"] = np.concatenate([high, high, low], 1)
    mix = cols @ cols.T / grid
    high, low = np_split(np.block([[mix, mix], [mix, mix]]))
    out["mix_cols"] = np.block([[high, low], [high, np.zeros_like(low)]])
    high, low = np_split(rows)
    out["target_rows"] = np.concatenate([high, low], 0)
    high, low = np_split(np.concatenate([cols, cols], 0).T)
    out["target_cols"] = np.concatenate([high, low], 1)
    ang = phases(wide, pix, period)
    cos, sin = np.cos(ang), np.sin(ang)
    high, low = np_split(np.block([[cos, sin], [-sin, cos]]))
    out["grad_cols"] = np.concatenate([high, high, low], 0)
    high, low = np_split(np.concatenate([np.cos(ang_rows).T, -np.sin(ang_rows).T], 1))
    out["grad_rows"] = np.concatenate([high, high, low], 1)
    return out


def pack_tables(tables):
    wide = [n for n in tables if tables[n].shape[1] > 256]
    narrow = sorted((n for n in tables if n not in wide), key=lambda n: -tables[n].shape[0])
    place, heights = {}, [0, 0]
    for n in wide:
        place[n] = (heights[0], 0)
        heights = [heights[0] + tables[n].shape[0]] * 2
    for n in narrow:
        side = int(heights[1] < heights[0])
        place[n] = (heights[side], 256 * side)
        heights[side] += tables[n].shape[0]
    whole = np.zeros((max(heights), 512), ml_dtypes.bfloat16)
    spots = {}
    for n, (row, col) in place.items():
        rows, cols = tables[n].shape
        whole[row : row + rows, col : col + cols] = tables[n]
        spots[n] = (slice(row, row + rows), slice(col, col + cols))
    return whole, spots


def split(value):
    high = value.astype(bf16)
    return high, (value - high.astype(f32)).astype(bf16)


def dot(left, right):
    return jnp.dot(left, right, preferred_element_type=f32)


def halves(value):
    width = value.shape[1] // 2
    return value[:, :width] + value[:, width:]


def lane_sign(rows, lanes, first):
    lane = lax.broadcasted_iota(jnp.int32, (rows, lanes), 1)
    return jnp.where(lane < lanes // 2, first, -first).astype(f32)


def swap(value):
    return pltpu.roll(value, value.shape[1] // 2, 1)


def half_tanh(value):
    return jnp.tanh(0.5 * value)


def sigmoid(value):
    return 0.5 * half_tanh(value) + 0.5


def window_spectrum(window, t):
    grid = t["spec_cols"].shape[1] // 4
    high, low = split(window)
    cols = t["spec_cols"]
    mid = halves(dot(high, cols[...])) + dot(low, cols[:, : 2 * grid])
    mid_high, mid_low = split(mid)
    rows = t["spec_rows"]
    both = halves(dot(rows[: 2 * grid, :], jnp.concatenate([mid_high, mid_low], 1)))
    both = both + dot(rows[2 * grid :, :], mid_high)
    return both[:grid] + lane_sign(grid, 2 * grid, 1.0) * swap(both[grid:])


def skewed(count, stages, first, second, carry):
    chunks = count // CHUNK
    first(0, stages[0])
    for c in range(1, chunks):
        first(c, stages[c % 2])
        carry = second(c - 1, stages[(c - 1) % 2], carry)
    return second(chunks - 1, stages[(chunks - 1) % 2], carry)


def placed_pupils(shifts, roots, pupil_re, pupil_im, pr, pi):
    def make(s):
        by = shifts[2, s] + MAX_SHIFT
        real = pltpu.roll(pupil_re[...] * roots[3, s], by, 1)
        imag = pltpu.roll(pupil_im[...] * roots[3, s], by, 1)
        pr[s], pi[s] = real, imag
        return real, imag

    return make


def grid_fields(spec, shifts, t, pupils, work):
    plain, crossed, fields, *stages = work
    count, grid, lanes = fields.shape
    box_len = t["row_fwd"].shape[1] // 6
    plain[...] = spec
    crossed[...] = swap(spec)
    sign = lane_sign(box_len, lanes, -1.0)

    def first(c, stage):
        rows = []
        for i in range(CHUNK):
            s = c * CHUNK + i
            at = pl.ds(shifts[1, s] + MAX_SHIFT, box_len)
            real, imag = pupils(s)
            high, low = split(real * plain[at, :] + imag * crossed[at, :])
            rows.append(jnp.concatenate([high, low], 1))
        stage[...] = halves(dot(jnp.concatenate(rows, 0), t["lane_fwd"][...]))

    def second(c, stage, power):
        stacks = []
        for i in range(CHUNK):
            part = stage[i * box_len : (i + 1) * box_len, :]
            high, low = split(jnp.concatenate([part, sign * swap(part)], 0))
            stacks.append(jnp.concatenate([high, low, high], 0))
        out = dot(t["row_fwd"][...], jnp.concatenate(stacks, 1))
        for i in range(CHUNK):
            field = out[:, i * lanes : (i + 1) * lanes]
            fields[c * CHUNK + i] = field
            power = power + field * field
        return power

    return skewed(count, stages, first, second, jnp.zeros((grid, lanes), f32))


def grid_misfit(power, inv_dose, target, t):
    high, low = split(power)
    mid = halves(dot(jnp.concatenate([high, low], 1), t["mix_cols"][...]))
    high, low = split(mid)
    lit = dot(t["mix_rows"][...], jnp.concatenate([high, low, high], 0))
    return lit * inv_dose - target


def gather_back(misfit, shifts, scale, t, pr, pi, fields, stages, sums):
    count, box_len, lanes = pr.shape
    for ref in sums:
        ref[...] = jnp.zeros_like(ref)
    sign = lane_sign(box_len, lanes, 1.0)

    def first(c, stage):
        stacks = []
        for i in range(CHUNK):
            high, low = split(fields[c * CHUNK + i] * misfit)
            stacks.append(jnp.concatenate([high, low, high], 0))
        both = dot(t["row_back"][...], jnp.concatenate(stacks, 1))
        for i in range(CHUNK):
            part = both[:, i * lanes : (i + 1) * lanes]
            stage[i * box_len : (i + 1) * box_len, :] = part[:box_len] + sign * swap(
                part[box_len:]
            )

    def second(c, stage, carry):
        high, low = split(stage[...])
        hits = halves(dot(jnp.concatenate([high, low], 1), t["lane_back"][...]))
        for i in range(CHUNK):
            s = c * CHUNK + i
            rows = pl.ds(shifts[1, s] + MAX_SHIFT, box_len)
            hit = hits[i * box_len : (i + 1) * box_len]
            one, two = sums[2 * (i % 2)], sums[2 * (i % 2) + 1]
            one[rows, :] += pr[s] * hit
            two[rows, :] += pi[s] * hit
        return carry

    skewed(count, stages, first, second, 0)
    return (sums[0][...] + sums[2][...] + swap(sums[1][...] + sums[3][...])) * scale


def tile_of(k, tile):
    return lax.bitwise_xor(tile, jnp.int32(k))


def mask_grads(params, ids, backs, t, tile, tiles, wins, grads):
    grid = backs[0].shape[0]
    tile_len = wins.shape[2]
    rows = []
    for back in backs:
        high, low = split(back[...])
        rows.append(jnp.concatenate([high, low, high], 1))
    mid = dot(jnp.concatenate(rows, 0), t["grad_cols"][...])
    wins[0, MARGIN + tile_len :, :] = jnp.zeros((MARGIN, tile_len), f32)
    wins[tiles + 1, :MARGIN, :] = jnp.zeros((MARGIN, tile_len), f32)
    for k in range(tiles):
        part = mid[k * grid : (k + 1) * grid]
        high, low = split(jnp.concatenate([part[:, :tile_len], part[:, tile_len:]], 0))
        out = dot(t["grad_rows"][...], jnp.concatenate([high, low, high], 0))
        wins[tile_of(k, tile) + 1] = out
    square = jnp.zeros((8, tile_len), f32)
    for k in range(tiles):
        own = ids[k]
        for low_row, high_row, near, shift in (
            (0, MARGIN, 0, tile_len),
            (MARGIN, tile_len - MARGIN, 1, 0),
            (tile_len - MARGIN, tile_len, 2, -tile_len),
        ):
            total = wins[own + 1, MARGIN + low_row : MARGIN + high_row, :]
            if near != 1:
                at = MARGIN + low_row + shift
                total = total + wins[own + near, at : at + MARGIN, :]
            lean = half_tanh(params(k, low_row, high_row))
            grad = total * (1.0 - lean * lean)
            grads[own, low_row:high_row, :] = grad
            square = square + jnp.sum((grad * grad).reshape(-1, 8, tile_len), axis=0)
    total = jnp.sum(jnp.sum(square, axis=0, keepdims=True), axis=1, keepdims=True)
    pixels = tiles * tile_len * tile_len
    return MASK_RATE / jnp.sqrt(total / pixels + TINY_EPS)


def edge_rows(tile, tiles, tile_len):
    above = pl.multiple_of(jnp.maximum(tile * tile_len - MARGIN, 0), MARGIN)
    below = jnp.minimum((tile + 1) * tile_len, tiles * tile_len - MARGIN)
    below = pl.multiple_of(below, MARGIN)
    return above, below, (tile > 0).astype(f32), (tile < tiles - 1).astype(f32)


def start_all(pairs, sems):
    copies = [pltpu.make_async_copy(a, b, sems.at[i]) for i, (a, b) in enumerate(pairs)]
    for copy in copies:
        copy.start()
    return copies


def pack_kernel(place, weights, shifts, packed, hold_w, hold_s, sems):
    local = weights.shape[1]
    for copy in start_all(((weights, hold_w), (shifts, hold_s)), sems):
        copy.wait()
    packed[...] = jnp.zeros_like(packed)
    packed[0:1, :local] = hold_w[...]
    packed[1:3, :local] = hold_s[...].astype(f32)
    packed[3:4, :local] = jnp.sqrt(hold_w[...])
    packed[...] = pltpu.roll(packed[...], place[0] * local, 1)


def edge_kernel(tile, mask, edge, sems):
    at = pl.multiple_of(lax.rem(tile[0], 2) * (mask.shape[0] - MARGIN), MARGIN)
    for copy in start_all(((mask.at[pl.ds(at, MARGIN), :], edge),), sems):
        copy.wait()


def target_kernel(spots, target, pupil, whole, out, pupil_re, pupil_im):
    grid, size = out.shape[0], pupil.shape[1]
    pupil_re[...] = jnp.zeros_like(pupil_re)
    pupil_im[...] = jnp.zeros_like(pupil_im)
    pupil_re[:, :size] = pupil[0]
    pupil_re[:, grid : grid + size] = pupil[0]
    pupil_im[:, :size] = -pupil[1]
    pupil_im[:, grid : grid + size] = pupil[1]
    rows, cols = whole.at[spots["target_rows"]], whole.at[spots["target_cols"]]
    high, low = split(target[...])
    both = dot(rows[...], high)
    mid = both[:grid] + both[grid:] + dot(rows[:grid, :], low)
    high, low = split(mid)
    out[...] = halves(dot(high, cols[...])) + dot(low, cols[:, : 2 * grid])


def doses(info, scale):
    dose = jnp.sum(info[0:1, :], axis=1, keepdims=True)
    return 1.0 / dose, scale / dose


def first_kernel(spots, peers, tiles, scale, tile, table, pupil_re, pupil_im, target,
                 own, mate, cross, *refs):
    parts = refs[:peers]
    t = {n: table.at[spot] for n, spot in spots.items()}
    back, pr, pi, info, whole = refs[peers : peers + 5]
    *work, s0, s1, s2, s3, shifts, roots, sems = refs[peers + 5 :]
    here = tile[0]
    total = parts[0][...]
    for part in parts[1:]:
        total = total + part[...]
    info[...] = total
    whole[...] = total.astype(jnp.int32)
    copies = (
        pltpu.make_async_copy(whole, shifts, sems.at[0]),
        pltpu.make_async_copy(info, roots, sems.at[1]),
    )
    for copy in copies:
        copy.start()
    has_prev = (here > 0).astype(f32)
    has_next = (here < tiles - 1).astype(f32)
    odd = lax.rem(here, 2) > 0
    before = jnp.where(odd, mate[-MARGIN:, :], cross[...])
    after = jnp.where(odd, cross[...], mate[:MARGIN, :])
    window = jnp.concatenate(
        [sigmoid(before) * has_prev, sigmoid(own[...]), sigmoid(after) * has_next], 0
    )
    spec = window_spectrum(window, t)
    for copy in copies:
        copy.wait()
    pupils = placed_pupils(shifts, roots, pupil_re, pupil_im, pr, pi)
    power = grid_fields(spec, shifts, t, pupils, work)
    inv_dose, factor = doses(total, scale)
    misfit = grid_misfit(power, inv_dose, target[...], t)
    sums = (s0, s1, s2, s3)
    back[...] = gather_back(misfit, shifts, factor, t, pr, pi, work[2], work[3:], sums)


def next_kernel(spots, tiles, scale, tile, table, shifts, info, pr, pi, target, *refs):
    params, backs = refs[:tiles], refs[tiles : 2 * tiles]
    t = {n: table.at[spot] for n, spot in spots.items()}
    new, back, *work, s0, s1, s2, s3, wins, grads = refs[2 * tiles :]
    here = tile[0]
    tile_len = params[0].shape[0]
    ids = [tile_of(k, here) for k in range(tiles)]
    rate = mask_grads(
        lambda k, low, high: params[k][low:high, :], ids, backs, t, here, tiles, wins, grads
    )
    for k in range(tiles):
        own = ids[k]
        at = pl.ds(pl.multiple_of(own * tile_len, tile_len), tile_len)
        new[at, :] = params[k][...] - grads[own] * rate
    above, below, has_prev, has_next = edge_rows(here, tiles, tile_len)
    own = pl.ds(pl.multiple_of(here * tile_len, tile_len), tile_len)
    window = jnp.concatenate(
        [
            sigmoid(new[pl.ds(above, MARGIN), :]) * has_prev,
            sigmoid(new[own, :]),
            sigmoid(new[pl.ds(below, MARGIN), :]) * has_next,
        ],
        0,
    )
    spec = window_spectrum(window, t)
    power = grid_fields(spec, shifts, t, lambda s: (pr[s], pi[s]), work)
    inv_dose, factor = doses(info[...], scale)
    misfit = grid_misfit(power, inv_dose, target[...], t)
    sums = (s0, s1, s2, s3)
    back[...] = gather_back(misfit, shifts, factor, t, pr, pi, work[2], work[3:], sums)


def last_kernel(spots, tiles, tile, table, shifts, info, pr, pi, target, params, *refs):
    backs = refs[:tiles]
    t = {n: table.at[spot] for n, spot in spots.items()}
    final, row, *work, terms, wins, grads = refs[tiles:]
    fields = work[2]
    here = tile[0]
    tile_len = final.shape[0]
    rate = mask_grads(
        lambda k, low, high: params[k * tile_len + low : k * tile_len + high, :],
        list(range(tiles)), backs, t, here, tiles, wins, grads,
    )
    above, below, has_prev, has_next = edge_rows(here, tiles, tile_len)
    own = pl.ds(pl.multiple_of(here * tile_len, tile_len), tile_len)
    final[...] = params[own, :] - grads[here] * rate
    prev, follow = jnp.maximum(here - 1, 0), jnp.minimum(here + 1, tiles - 1)
    window = jnp.concatenate(
        [
            sigmoid(params[pl.ds(above, MARGIN), :] - grads[prev, tile_len - MARGIN :, :] * rate)
            * has_prev,
            sigmoid(final[...]),
            sigmoid(params[pl.ds(below, MARGIN), :] - grads[follow, :MARGIN, :] * rate)
            * has_next,
        ],
        0,
    )
    spec = window_spectrum(window, t)
    power = grid_fields(spec, shifts, t, lambda s: (pr[s], pi[s]), work)
    inv_dose, _ = doses(info[...], 1.0)
    misfit = grid_misfit(power, inv_dose, target[...], t)

    def chunk(c, carry):
        rows = []
        for i in range(CHUNK):
            field = fields[c * CHUNK + i]
            rows.append(jnp.sum(field * field * misfit, axis=0, keepdims=True))
        terms[pl.ds(pl.multiple_of(c * CHUNK, CHUNK), CHUNK), :] = jnp.concatenate(rows, 0)
        return carry

    count = fields.shape[0]
    lax.fori_loop(0, count // CHUNK, chunk, 0)
    high, low = split(terms[...])
    left = terms[...] - high.astype(f32) - low.astype(f32)
    ones = jnp.ones((8, terms.shape[1]), bf16)
    total = jnp.zeros((8, terms.shape[0]), f32)
    for part in (left.astype(bf16), low, high):
        total = total + lax.dot_general(
            ones, part, (((1,), (1,)), ((), ())), preferred_element_type=f32
        )
    row[...] = total


def weight_kernel(tiles, scale, tile, place, info, *refs):
    rows = refs[:tiles]
    out, stack = refs[tiles:]
    count = rows[0].shape[1]
    for k in range(tiles):
        stack[k] = rows[k][...]
    here = tile[0]
    total = stack[here]
    for k in range(1, tiles):
        total = total + stack[tile_of(k, here)]
    summed = total[0:1] * scale
    weight = info[0:1, :count]
    dose = jnp.sum(weight, axis=1, keepdims=True)
    mean = jnp.sum(summed, axis=1, keepdims=True) / dose
    grad = (summed / weight - mean) / dose
    spread = jnp.sqrt(jnp.sum(grad * grad, axis=1, keepdims=True) / count + TINY_EPS)
    new = weight * jnp.exp(-WEIGHT_RATE * grad / spread)
    size = out.shape[1]
    lanes = info.shape[1]
    if count < lanes:
        new = jnp.concatenate([new, jnp.zeros((1, lanes - count), f32)], 1)
    new = pltpu.roll(jnp.broadcast_to(new, (8, lanes)), lanes - place[0] * size, 1)
    out[...] = new[0:1, :size]


def crossed(value, axis, k):
    return lax.ppermute(value, axis, [(i, i ^ k) for i in range(lax.axis_size(axis))])


def all_of(value, axis):
    return [value] + [crossed(value, axis, k) for k in range(1, lax.axis_size(axis))]


def per_device(mask_param, target_image, source_weights, source_shifts, pupil_map):
    tile_len = mask_param.shape[1]
    box_len = pupil_map.shape[1]
    grid = box_len + 2 * MAX_SHIFT
    lanes = 2 * grid
    tiles = lax.axis_size("tile")
    peers = lax.axis_size("src")
    local = source_weights.shape[0]
    count = local * peers
    assert tiles & (tiles - 1) == 0 and peers & (peers - 1) == 0 and count <= 128 and count % CHUNK == 0
    tables = make_tables(tile_len, box_len, MAX_SHIFT)

    tile = lax.axis_index("tile").astype(jnp.int32).reshape(1)
    place = lax.axis_index("src").astype(jnp.int32).reshape(1)

    vmem = pl.BlockSpec(memory_space=pltpu.VMEM)
    smem = pl.BlockSpec(memory_space=pltpu.SMEM)
    left = pl.BlockSpec(memory_space=pltpu.HBM)
    params_of = pltpu.CompilerParams(vmem_limit_bytes=32 << 20)

    def struct(*shape, kind=f32):
        return jax.ShapeDtypeStruct(shape, kind)

    def cost(flops):
        return pl.CostEstimate(flops=flops, bytes_accessed=1 << 20, transcendentals=0)

    packed = pl.pallas_call(
        pack_kernel,
        out_shape=struct(8, 128),
        in_specs=[smem, left, left],
        out_specs=vmem,
        scratch_shapes=[
            pltpu.VMEM((1, local), f32),
            pltpu.VMEM((2, local), jnp.int32),
            pltpu.SemaphoreType.DMA((2,)),
        ],
        name="pack_sources",
    )(place, source_weights[None], source_shifts.T)
    packed = all_of(packed, "src")

    edge = pl.pallas_call(
        edge_kernel,
        out_shape=struct(MARGIN, tile_len),
        in_specs=[smem, left],
        out_specs=vmem,
        scratch_shapes=[pltpu.SemaphoreType.DMA((1,))],
        name="edge_rows",
    )(tile, mask_param)
    pairs = [(i, (i + 1) % tiles) for i in range(1, tiles, 2)]
    cross = lax.ppermute(edge, "tile", pairs + [(j, i) for i, j in pairs])
    mate = crossed(mask_param, "tile", 1)
    far = [crossed(mask_param, "tile", k) for k in range(2, tiles, 2)]

    whole, spots = pack_tables(tables)
    table = jnp.asarray(whole)
    target, pupil_re, pupil_im = pl.pallas_call(
        functools.partial(target_kernel, spots),
        out_shape=[struct(grid, lanes), struct(box_len, lanes), struct(box_len, lanes)],
        in_specs=[vmem] * 3,
        out_specs=[vmem] * 3,
        compiler_params=params_of,
        cost_estimate=cost(1 << 26),
        name="target_terms",
    )(target_image, pupil_map, table)

    work = [
        pltpu.VMEM((grid, lanes), f32),
        pltpu.VMEM((grid, lanes), f32),
        pltpu.VMEM((count, grid, lanes), f32),
        pltpu.VMEM((CHUNK * box_len, lanes), f32),
        pltpu.VMEM((CHUNK * box_len, lanes), f32),
    ]
    hold = [pltpu.VMEM((grid, lanes), f32)] * 4
    steps = [
        pltpu.VMEM((tiles + 2, tile_len + 2 * MARGIN, tile_len), f32),
        pltpu.VMEM((tiles, tile_len, tile_len), f32),
    ]
    period = tile_len + 2 * MARGIN
    scale = 0.5 / (grid * grid * period * tile_len)
    source_len = struct(count, box_len, lanes)

    back, pr, pi, info, whole = pl.pallas_call(
        functools.partial(first_kernel, spots, peers, tiles, scale),
        out_shape=[struct(grid, lanes), source_len, source_len, struct(8, 128),
                   struct(8, 128, kind=jnp.int32)],
        in_specs=[smem] + [vmem] * (7 + peers),
        out_specs=[vmem] * 5,
        scratch_shapes=work + hold + [
            pltpu.SMEM((8, 128), jnp.int32),
            pltpu.SMEM((8, 128), f32),
            pltpu.SemaphoreType.DMA((2,)),
        ],
        compiler_params=params_of,
        cost_estimate=cost(1 << 32),
        name="first_step",
    )(tile, table, pupil_re, pupil_im, target, mask_param, mate, cross, *packed)

    shared = (tile, table, whole, info, pr, pi, target)
    shared_specs = [smem, vmem, smem] + [vmem] * 4

    back, far = lax.optimization_barrier((back, far))
    backs = all_of(back, "tile")
    entries = [mask_param, mate]
    for one in far:
        entries += [one, crossed(one, "tile", 1)]
    params, back = pl.pallas_call(
        functools.partial(next_kernel, spots, tiles, scale),
        out_shape=[struct(tiles * tile_len, tile_len), struct(grid, lanes)],
        in_specs=shared_specs + [vmem] * (2 * tiles),
        out_specs=[vmem] * 2,
        scratch_shapes=work + hold + steps,
        compiler_params=params_of,
        cost_estimate=cost(1 << 32),
        name="next_step",
    )(*shared, *entries, *backs)

    backs = all_of(back, "tile")
    final, row = pl.pallas_call(
        functools.partial(last_kernel, spots, tiles),
        out_shape=[struct(tile_len, tile_len), struct(8, count)],
        in_specs=shared_specs + [vmem] * (1 + tiles),
        out_specs=[vmem] * 2,
        scratch_shapes=work + [pltpu.VMEM((count, lanes), f32)] + steps,
        compiler_params=params_of,
        cost_estimate=cost(1 << 32),
        name="last_step",
    )(*shared, params, *backs)

    rows = all_of(row, "tile")
    out = pl.pallas_call(
        functools.partial(weight_kernel, tiles, 1.0 / (grid * grid)),
        out_shape=struct(1, local),
        in_specs=[smem] * 2 + [vmem] * (1 + tiles),
        out_specs=vmem,
        scratch_shapes=[pltpu.VMEM((tiles, 8, count), f32)],
        compiler_params=params_of,
        name="weight_step",
    )(tile, place, info, *rows)
    return final, out.reshape(local)


def solution(mesh):
    in_specs = (
        P(("group", "tile"), None),
        P(("group", "tile"), None),
        P(("group", "src")),
        P("src", None),
        P(),
    )
    out_specs = (P(("group", "tile"), None), P(("group", "src")))
    return jax.shard_map(
        per_device, mesh=mesh, in_specs=in_specs, out_specs=out_specs, check_vma=False
    )
```

```python
import functools
import math

import jax
import jax.numpy as jnp
import ml_dtypes
import numpy as np
from jax import lax
from jax.experimental import pallas as pl
from jax.experimental.pallas import tpu as pltpu
from jax.sharding import PartitionSpec as P


MARGIN = 64
MAX_SHIFT = 16
MASK_RATE = 0.5
WEIGHT_RATE = 0.3
TINY_EPS = 1e-06
CHUNK = 16
GROUP = 2


bf16 = jnp.bfloat16
f32 = jnp.float32


def np_split(table):
    table = np.asarray(table, np.float64)
    high = table.astype(np.float32).astype(ml_dtypes.bfloat16)
    low = (table - high.astype(np.float64)).astype(np.float32).astype(ml_dtypes.bfloat16)
    return high, low


def phases(freqs, pixels, period):
    return 2.0 * math.pi * np.mod(np.outer(freqs, pixels), period) / period


def make_tables(tile_len, box_len, max_shift):
    period = tile_len + 2 * MARGIN
    grid = box_len + 2 * max_shift
    wide = np.arange(grid) - grid // 2
    pix = np.arange(tile_len)
    full = np.arange(period)
    points = np.arange(grid)
    box = np.arange(box_len)
    out = {}
    ang = phases(wide, pix, period)
    high, low = np_split(np.concatenate([np.cos(ang), -np.sin(ang)], 0).T / (period * tile_len))
    out["spec_cols"] = np.concatenate([high, low], 1)
    ang_rows = phases(wide, full, period)
    high, low = np_split(np.concatenate([np.cos(ang_rows), np.sin(ang_rows)], 0))
    out["spec_rows"] = np.concatenate([high, low], 0)
    ang = phases(points, points, grid)
    cos, sin = np.cos(ang), np.sin(ang)
    for name, table in (
        ("lane_fwd", np.block([[cos, sin], [-sin, cos]])),
        ("lane_back", np.block([[cos, -sin], [sin, cos]])),
    ):
        high, low = np_split(table)
        out[name] = np.block([[high, low], [high, np.zeros_like(low)]])
    ang = phases(points, box, grid)
    high, low = np_split(np.concatenate([np.cos(ang), np.sin(ang)], 1))
    out["row_fwd"] = np.concatenate([high, high, low], 1)
    high, low = np_split(np.concatenate([np.cos(ang).T, np.sin(ang).T], 0))
    out["row_back"] = np.concatenate([high, high, low], 1)

    def dirichlet(offset):
        theta = 2.0 * math.pi * ((pix + offset)[None, :] / period - points[:, None] / grid)
        orders = np.arange(1, box_len)
        return 1.0 + 2.0 * np.cos(orders[:, None, None] * theta[None]).sum(0)

    rows, cols = dirichlet(MARGIN), dirichlet(0)
    high, low = np_split(rows @ rows.T / grid)
    out["mix_rows"] = np.concatenate([high, high, low], 1)
    mix = cols @ cols.T / grid
    high, low = np_split(np.block([[mix, mix], [mix, mix]]))
    out["mix_cols"] = np.block([[high, low], [high, np.zeros_like(low)]])
    high, low = np_split(rows)
    out["target_rows"] = np.concatenate([high, low], 0)
    high, low = np_split(np.concatenate([cols, cols], 0).T)
    out["target_cols"] = np.concatenate([high, low], 1)
    ang = phases(wide, pix, period)
    cos, sin = np.cos(ang), np.sin(ang)
    high, low = np_split(np.block([[cos, sin], [-sin, cos]]))
    out["grad_cols"] = np.concatenate([high, high, low], 0)
    high, low = np_split(np.concatenate([np.cos(ang_rows).T, -np.sin(ang_rows).T], 1))
    out["grad_rows"] = np.concatenate([high, high, low], 1)
    return out


def pack_tables(tables):
    wide = [n for n in tables if tables[n].shape[1] > 256]
    narrow = sorted((n for n in tables if n not in wide), key=lambda n: -tables[n].shape[0])
    place, heights = {}, [0, 0]
    for n in wide:
        place[n] = (heights[0], 0)
        heights = [heights[0] + tables[n].shape[0]] * 2
    for n in narrow:
        side = int(heights[1] < heights[0])
        place[n] = (heights[side], 256 * side)
        heights[side] += tables[n].shape[0]
    whole = np.zeros((max(heights), 512), ml_dtypes.bfloat16)
    spots = {}
    for n, (row, col) in place.items():
        rows, cols = tables[n].shape
        whole[row : row + rows, col : col + cols] = tables[n]
        spots[n] = (slice(row, row + rows), slice(col, col + cols))
    return whole, spots


def split(value):
    high = value.astype(bf16)
    return high, (value - high.astype(f32)).astype(bf16)


def dot(left, right):
    return jnp.dot(left, right, preferred_element_type=f32)


def halves(value):
    width = value.shape[1] // 2
    return value[:, :width] + value[:, width:]


def lane_sign(rows, lanes, first):
    lane = lax.broadcasted_iota(jnp.int32, (rows, lanes), 1)
    return jnp.where(lane < lanes // 2, first, -first).astype(f32)


def swap(value):
    return pltpu.roll(value, value.shape[1] // 2, 1)


def half_tanh(value):
    return jnp.tanh(0.5 * value)


def sigmoid(value):
    return 0.5 * half_tanh(value) + 0.5


def window_spectrum(window, t):
    grid = t["spec_cols"].shape[1] // 4
    high, low = split(window)
    cols = t["spec_cols"]
    mid = halves(dot(high, cols[...])) + dot(low, cols[:, : 2 * grid])
    mid_high, mid_low = split(mid)
    rows = t["spec_rows"]
    both = halves(dot(rows[: 2 * grid, :], jnp.concatenate([mid_high, mid_low], 1)))
    both = both + dot(rows[2 * grid :, :], mid_high)
    return both[:grid] + lane_sign(grid, 2 * grid, 1.0) * swap(both[grid:])


def skewed(count, stages, first, second, carry):
    chunks = count // CHUNK
    first(0, stages[0])
    for c in range(1, chunks):
        first(c, stages[c % 2])
        carry = second(c - 1, stages[(c - 1) % 2], carry)
    return second(chunks - 1, stages[(chunks - 1) % 2], carry)


def turn_pupils(pupil, turned_re, turned_im):
    count, size, lanes = turned_re.shape
    grid = lanes // 2
    turned_re[0] = jnp.zeros((size, lanes), f32)
    turned_im[0] = jnp.zeros((size, lanes), f32)
    turned_re[0, :, :size] = pupil[0]
    turned_re[0, :, grid : grid + size] = pupil[0]
    turned_im[0, :, :size] = -pupil[1]
    turned_im[0, :, grid : grid + size] = pupil[1]
    real, imag = turned_re[0], turned_im[0]
    for by in range(1, count):
        turned_re[by] = pltpu.roll(real, by, 1)
        turned_im[by] = pltpu.roll(imag, by, 1)


def placed_pupils(shifts, roots, turned_re, turned_im, pr, pi):
    def make(s):
        by = shifts[2, s] + MAX_SHIFT
        real, imag = turned_re[by] * roots[3, s], turned_im[by] * roots[3, s]
        pr[s], pi[s] = real, imag
        return real, imag

    return make


def grid_fields(spec, shifts, t, pupils, work, squares=False):
    plain, crossed, fields, *stages = work
    count, grid, lanes = fields.shape
    box_len = t["row_fwd"].shape[1] // 6
    plain[...] = spec
    crossed[...] = swap(spec)
    sign = lane_sign(box_len, lanes, -1.0)

    def first(c, stage):
        rows = []
        for i in range(CHUNK):
            s = c * CHUNK + i
            at = pl.ds(shifts[1, s] + MAX_SHIFT, box_len)
            real, imag = pupils(s)
            high, low = split(real * plain[at, :] + imag * crossed[at, :])
            rows.append(jnp.concatenate([high, low], 1))
        stage[...] = halves(dot(jnp.concatenate(rows, 0), t["lane_fwd"][...]))

    def second(c, stage, power):
        for base in range(0, CHUNK, GROUP):
            stacks = []
            for i in range(base, base + GROUP):
                part = stage[i * box_len : (i + 1) * box_len, :]
                high, low = split(jnp.concatenate([part, sign * swap(part)], 0))
                stacks.append(jnp.concatenate([high, low, high], 0))
            out = dot(t["row_fwd"][...], jnp.concatenate(stacks, 1))
            for i in range(GROUP):
                field = out[:, i * lanes : (i + 1) * lanes]
                square = field * field
                fields[c * CHUNK + base + i] = square if squares else field
                power = power + square
        return power

    return skewed(count, stages, first, second, jnp.zeros((grid, lanes), f32))


def grid_misfit(power, inv_dose, target, t):
    high, low = split(power)
    mid = halves(dot(jnp.concatenate([high, low], 1), t["mix_cols"][...]))
    high, low = split(mid)
    lit = dot(t["mix_rows"][...], jnp.concatenate([high, low, high], 0))
    return lit * inv_dose - target


def gather_back(misfit, shifts, scale, t, pr, pi, fields, stages, sums):
    count, box_len, lanes = pr.shape
    for ref in sums:
        ref[...] = jnp.zeros_like(ref)
    sign = lane_sign(box_len, lanes, 1.0)

    def first(c, stage):
        for base in range(0, CHUNK, GROUP):
            stacks = []
            for i in range(base, base + GROUP):
                high, low = split(fields[c * CHUNK + i] * misfit)
                stacks.append(jnp.concatenate([high, low, high], 0))
            both = dot(t["row_back"][...], jnp.concatenate(stacks, 1))
            for i in range(GROUP):
                part = both[:, i * lanes : (i + 1) * lanes]
                at = (base + i) * box_len
                stage[at : at + box_len, :] = part[:box_len] + sign * swap(part[box_len:])

    def second(c, stage, carry):
        high, low = split(stage[...])
        hits = halves(dot(jnp.concatenate([high, low], 1), t["lane_back"][...]))
        for i in range(CHUNK):
            s = c * CHUNK + i
            rows = pl.ds(shifts[1, s] + MAX_SHIFT, box_len)
            hit = hits[i * box_len : (i + 1) * box_len]
            one, two = sums[2 * (i % 2)], sums[2 * (i % 2) + 1]
            one[rows, :] += pr[s] * hit
            two[rows, :] += pi[s] * hit
        return carry

    skewed(count, stages, first, second, 0)
    return (sums[0][...] + sums[2][...] + swap(sums[1][...] + sums[3][...])) * scale


def tile_of(k, tile):
    return lax.bitwise_xor(tile, jnp.int32(k))


def mask_grads(params, ids, backs, t, tile, tiles, wins, grads):
    grid = backs[0].shape[0]
    tile_len = wins.shape[2]
    rows = []
    for back in backs:
        high, low = split(back[...])
        rows.append(jnp.concatenate([high, low, high], 1))
    mid = dot(jnp.concatenate(rows, 0), t["grad_cols"][...])
    wins[0, MARGIN + tile_len :, :] = jnp.zeros((MARGIN, tile_len), f32)
    wins[tiles + 1, :MARGIN, :] = jnp.zeros((MARGIN, tile_len), f32)
    for k in range(tiles):
        part = mid[k * grid : (k + 1) * grid]
        high, low = split(jnp.concatenate([part[:, :tile_len], part[:, tile_len:]], 0))
        out = dot(t["grad_rows"][...], jnp.concatenate([high, low, high], 0))
        wins[tile_of(k, tile) + 1] = out
    square = jnp.zeros((8, tile_len), f32)
    for k in range(tiles):
        own = ids[k]
        for low_row, high_row, near, shift in (
            (0, MARGIN, 0, tile_len),
            (MARGIN, tile_len - MARGIN, 1, 0),
            (tile_len - MARGIN, tile_len, 2, -tile_len),
        ):
            total = wins[own + 1, MARGIN + low_row : MARGIN + high_row, :]
            if near != 1:
                at = MARGIN + low_row + shift
                total = total + wins[own + near, at : at + MARGIN, :]
            lean = half_tanh(params(k, low_row, high_row))
            grad = total * (1.0 - lean * lean)
            grads[own, low_row:high_row, :] = grad
            square = square + jnp.sum((grad * grad).reshape(-1, 8, tile_len), axis=0)
    total = jnp.sum(jnp.sum(square, axis=0, keepdims=True), axis=1, keepdims=True)
    pixels = tiles * tile_len * tile_len
    return MASK_RATE / jnp.sqrt(total / pixels + TINY_EPS)


def edge_rows(tile, tiles, tile_len):
    above = pl.multiple_of(jnp.maximum(tile * tile_len - MARGIN, 0), MARGIN)
    below = jnp.minimum((tile + 1) * tile_len, tiles * tile_len - MARGIN)
    below = pl.multiple_of(below, MARGIN)
    return above, below, (tile > 0).astype(f32), (tile < tiles - 1).astype(f32)


def start_all(pairs, sems):
    copies = [pltpu.make_async_copy(a, b, sems.at[i]) for i, (a, b) in enumerate(pairs)]
    for copy in copies:
        copy.start()
    return copies


def pack_kernel(tile, place, weights, shifts, mask, packed, edge, hold_w, hold_s, sems):
    local = weights.shape[1]
    at = pl.multiple_of(lax.rem(tile[0], 2) * (mask.shape[0] - MARGIN), MARGIN)
    copies = start_all(
        ((weights, hold_w), (shifts, hold_s), (mask.at[pl.ds(at, MARGIN), :], edge)), sems
    )
    for copy in copies:
        copy.wait()
    packed[...] = jnp.zeros_like(packed)
    packed[0:1, :local] = hold_w[...]
    packed[1:3, :local] = hold_s[...].astype(f32)
    packed[3:4, :local] = jnp.sqrt(hold_w[...])
    packed[...] = pltpu.roll(packed[...], place[0] * local, 1)


def target_terms(target, t):
    rows, cols = t["target_rows"], t["target_cols"]
    grid = rows.shape[0] // 2
    high, low = split(target)
    both = dot(rows[...], high)
    mid = both[:grid] + both[grid:] + dot(rows[:grid, :], low)
    high, low = split(mid)
    return halves(dot(high, cols[...])) + dot(low, cols[:, : 2 * grid])


def doses(info, scale):
    dose = jnp.sum(info[0:1, :], axis=1, keepdims=True)
    return 1.0 / dose, scale / dose


def first_kernel(spots, peers, tiles, scale, tile, table, pupil, goal,
                 own, mate, cross, *refs):
    parts = refs[:peers]
    t = {n: table.at[spot] for n, spot in spots.items()}
    back, pr, pi, info, whole, target = refs[peers : peers + 6]
    *work, s0, s1, s2, s3, turned_re, turned_im, shifts, roots, sems = refs[peers + 6 :]
    here = tile[0]
    total = parts[0][...]
    for part in parts[1:]:
        total = total + part[...]
    info[...] = total
    whole[...] = total.astype(jnp.int32)
    copies = (
        pltpu.make_async_copy(whole, shifts, sems.at[0]),
        pltpu.make_async_copy(info, roots, sems.at[1]),
    )
    for copy in copies:
        copy.start()
    has_prev = (here > 0).astype(f32)
    has_next = (here < tiles - 1).astype(f32)
    odd = lax.rem(here, 2) > 0
    before = jnp.where(odd, mate[-MARGIN:, :], cross[...])
    after = jnp.where(odd, cross[...], mate[:MARGIN, :])
    window = jnp.concatenate(
        [sigmoid(before) * has_prev, sigmoid(own[...]), sigmoid(after) * has_next], 0
    )
    spec = window_spectrum(window, t)
    target[...] = target_terms(goal[...], t)
    turn_pupils(pupil, turned_re, turned_im)
    for copy in copies:
        copy.wait()
    pupils = placed_pupils(shifts, roots, turned_re, turned_im, pr, pi)
    power = grid_fields(spec, shifts, t, pupils, work)
    inv_dose, factor = doses(total, scale)
    misfit = grid_misfit(power, inv_dose, target[...], t)
    sums = (s0, s1, s2, s3)
    back[...] = gather_back(misfit, shifts, factor, t, pr, pi, work[2], work[3:], sums)


def next_kernel(spots, tiles, scale, tile, table, shifts, info, pr, pi, target, *refs):
    params, backs = refs[:tiles], refs[tiles : 2 * tiles]
    t = {n: table.at[spot] for n, spot in spots.items()}
    new, back, *work, s0, s1, s2, s3, wins, grads = refs[2 * tiles :]
    here = tile[0]
    tile_len = params[0].shape[0]
    ids = [tile_of(k, here) for k in range(tiles)]
    rate = mask_grads(
        lambda k, low, high: params[k][low:high, :], ids, backs, t, here, tiles, wins, grads
    )
    for k in range(tiles):
        own = ids[k]
        at = pl.ds(pl.multiple_of(own * tile_len, tile_len), tile_len)
        new[at, :] = params[k][...] - grads[own] * rate
    above, below, has_prev, has_next = edge_rows(here, tiles, tile_len)
    own = pl.ds(pl.multiple_of(here * tile_len, tile_len), tile_len)
    window = jnp.concatenate(
        [
            sigmoid(new[pl.ds(above, MARGIN), :]) * has_prev,
            sigmoid(new[own, :]),
            sigmoid(new[pl.ds(below, MARGIN), :]) * has_next,
        ],
        0,
    )
    spec = window_spectrum(window, t)
    power = grid_fields(spec, shifts, t, lambda s: (pr[s], pi[s]), work)
    inv_dose, factor = doses(info[...], scale)
    misfit = grid_misfit(power, inv_dose, target[...], t)
    sums = (s0, s1, s2, s3)
    back[...] = gather_back(misfit, shifts, factor, t, pr, pi, work[2], work[3:], sums)


def last_kernel(spots, tiles, tile, table, shifts, info, pr, pi, target, params, *refs):
    backs = refs[:tiles]
    t = {n: table.at[spot] for n, spot in spots.items()}
    final, row, *work, terms, wins, grads = refs[tiles:]
    fields = work[2]
    here = tile[0]
    tile_len = final.shape[0]
    rate = mask_grads(
        lambda k, low, high: params[k * tile_len + low : k * tile_len + high, :],
        list(range(tiles)), backs, t, here, tiles, wins, grads,
    )
    above, below, has_prev, has_next = edge_rows(here, tiles, tile_len)
    own = pl.ds(pl.multiple_of(here * tile_len, tile_len), tile_len)
    final[...] = params[own, :] - grads[here] * rate
    prev, follow = jnp.maximum(here - 1, 0), jnp.minimum(here + 1, tiles - 1)
    window = jnp.concatenate(
        [
            sigmoid(params[pl.ds(above, MARGIN), :] - grads[prev, tile_len - MARGIN :, :] * rate)
            * has_prev,
            sigmoid(final[...]),
            sigmoid(params[pl.ds(below, MARGIN), :] - grads[follow, :MARGIN, :] * rate)
            * has_next,
        ],
        0,
    )
    spec = window_spectrum(window, t)
    power = grid_fields(spec, shifts, t, lambda s: (pr[s], pi[s]), work, squares=True)
    inv_dose, _ = doses(info[...], 1.0)
    misfit = grid_misfit(power, inv_dose, target[...], t)

    def chunk(c, carry):
        rows = []
        for i in range(CHUNK):
            rows.append(jnp.sum(fields[c * CHUNK + i] * misfit, axis=0, keepdims=True))
        terms[pl.ds(pl.multiple_of(c * CHUNK, CHUNK), CHUNK), :] = jnp.concatenate(rows, 0)
        return carry

    count = fields.shape[0]
    lax.fori_loop(0, count // CHUNK, chunk, 0)
    high, low = split(terms[...])
    left = terms[...] - high.astype(f32) - low.astype(f32)
    ones = jnp.ones((8, terms.shape[1]), bf16)
    total = jnp.zeros((8, terms.shape[0]), f32)
    for part in (left.astype(bf16), low, high):
        total = total + lax.dot_general(
            ones, part, (((1,), (1,)), ((), ())), preferred_element_type=f32
        )
    row[...] = total


def weight_kernel(tiles, scale, tile, place, info, *refs):
    rows = refs[:tiles]
    out, stack = refs[tiles:]
    count = rows[0].shape[1]
    for k in range(tiles):
        stack[k] = rows[k][...]
    here = tile[0]
    total = stack[here]
    for k in range(1, tiles):
        total = total + stack[tile_of(k, here)]
    summed = total[0:1] * scale
    weight = info[0:1, :count]
    dose = jnp.sum(weight, axis=1, keepdims=True)
    mean = jnp.sum(summed, axis=1, keepdims=True) / dose
    grad = (summed / weight - mean) / dose
    spread = jnp.sqrt(jnp.sum(grad * grad, axis=1, keepdims=True) / count + TINY_EPS)
    new = weight * jnp.exp(-WEIGHT_RATE * grad / spread)
    size = out.shape[1]
    lanes = info.shape[1]
    if count < lanes:
        new = jnp.concatenate([new, jnp.zeros((1, lanes - count), f32)], 1)
    new = pltpu.roll(jnp.broadcast_to(new, (8, lanes)), lanes - place[0] * size, 1)
    out[...] = new[0:1, :size]


def crossed(value, axis, k):
    return lax.ppermute(value, axis, [(i, i ^ k) for i in range(lax.axis_size(axis))])


def all_of(value, axis):
    return [value] + [crossed(value, axis, k) for k in range(1, lax.axis_size(axis))]


def per_device(mask_param, target_image, source_weights, source_shifts, pupil_map):
    tile_len = mask_param.shape[1]
    box_len = pupil_map.shape[1]
    grid = box_len + 2 * MAX_SHIFT
    lanes = 2 * grid
    tiles = lax.axis_size("tile")
    peers = lax.axis_size("src")
    local = source_weights.shape[0]
    count = local * peers
    assert tiles & (tiles - 1) == 0 and peers & (peers - 1) == 0 and count <= 128 and count % CHUNK == 0
    tables = make_tables(tile_len, box_len, MAX_SHIFT)

    tile = lax.axis_index("tile").astype(jnp.int32).reshape(1)
    place = lax.axis_index("src").astype(jnp.int32).reshape(1)

    vmem = pl.BlockSpec(memory_space=pltpu.VMEM)
    smem = pl.BlockSpec(memory_space=pltpu.SMEM)
    left = pl.BlockSpec(memory_space=pltpu.HBM)
    params_of = pltpu.CompilerParams(vmem_limit_bytes=32 << 20)

    def struct(*shape, kind=f32):
        return jax.ShapeDtypeStruct(shape, kind)

    def cost(flops):
        return pl.CostEstimate(flops=flops, bytes_accessed=1 << 20, transcendentals=0)

    packed, edge = pl.pallas_call(
        pack_kernel,
        out_shape=[struct(8, 128), struct(MARGIN, tile_len)],
        in_specs=[smem, smem, left, left, left],
        out_specs=[vmem] * 2,
        scratch_shapes=[
            pltpu.VMEM((1, local), f32),
            pltpu.VMEM((2, local), jnp.int32),
            pltpu.SemaphoreType.DMA((3,)),
        ],
        name="pack_sources",
    )(tile, place, source_weights[None], source_shifts.T, mask_param)
    packed = all_of(packed, "src")

    pairs = [(i, (i + 1) % tiles) for i in range(1, tiles, 2)]
    cross = lax.ppermute(edge, "tile", pairs + [(j, i) for i, j in pairs])
    mate = crossed(mask_param, "tile", 1)
    far = [crossed(mask_param, "tile", k) for k in range(2, tiles, 2)]

    whole, spots = pack_tables(tables)
    table = jnp.asarray(whole)
    work = [
        pltpu.VMEM((grid, lanes), f32),
        pltpu.VMEM((grid, lanes), f32),
        pltpu.VMEM((count, grid, lanes), f32),
        pltpu.VMEM((CHUNK * box_len, lanes), f32),
        pltpu.VMEM((CHUNK * box_len, lanes), f32),
    ]
    hold = [pltpu.VMEM((grid, lanes), f32)] * 4
    steps = [
        pltpu.VMEM((tiles + 2, tile_len + 2 * MARGIN, tile_len), f32),
        pltpu.VMEM((tiles, tile_len, tile_len), f32),
    ]
    period = tile_len + 2 * MARGIN
    scale = 0.5 / (grid * grid * period * tile_len)
    source_len = struct(count, box_len, lanes)

    back, pr, pi, info, whole, target = pl.pallas_call(
        functools.partial(first_kernel, spots, peers, tiles, scale),
        out_shape=[struct(grid, lanes), source_len, source_len, struct(8, 128),
                   struct(8, 128, kind=jnp.int32), struct(grid, lanes)],
        in_specs=[smem] + [vmem] * (6 + peers),
        out_specs=[vmem] * 6,
        scratch_shapes=work + hold + [
            pltpu.VMEM((2 * MAX_SHIFT + 1, box_len, lanes), f32),
            pltpu.VMEM((2 * MAX_SHIFT + 1, box_len, lanes), f32),
            pltpu.SMEM((8, 128), jnp.int32),
            pltpu.SMEM((8, 128), f32),
            pltpu.SemaphoreType.DMA((2,)),
        ],
        compiler_params=params_of,
        cost_estimate=cost(1 << 32),
        name="first_step",
    )(tile, table, pupil_map, target_image, mask_param, mate, cross, *packed)

    shared = (tile, table, whole, info, pr, pi, target)
    shared_specs = [smem, vmem, smem] + [vmem] * 4

    back, far = lax.optimization_barrier((back, far))
    backs = all_of(back, "tile")
    entries = [mask_param, mate]
    for one in far:
        entries += [one, crossed(one, "tile", 1)]
    params, back = pl.pallas_call(
        functools.partial(next_kernel, spots, tiles, scale),
        out_shape=[struct(tiles * tile_len, tile_len), struct(grid, lanes)],
        in_specs=shared_specs + [vmem] * (2 * tiles),
        out_specs=[vmem] * 2,
        scratch_shapes=work + hold + steps,
        compiler_params=params_of,
        cost_estimate=cost(1 << 32),
        name="next_step",
    )(*shared, *entries, *backs)

    backs = all_of(back, "tile")
    final, row = pl.pallas_call(
        functools.partial(last_kernel, spots, tiles),
        out_shape=[struct(tile_len, tile_len), struct(8, count)],
        in_specs=shared_specs + [vmem] * (1 + tiles),
        out_specs=[vmem] * 2,
        scratch_shapes=work + [pltpu.VMEM((count, lanes), f32)] + steps,
        compiler_params=params_of,
        cost_estimate=cost(1 << 32),
        name="last_step",
    )(*shared, params, *backs)

    rows = all_of(row, "tile")
    out = pl.pallas_call(
        functools.partial(weight_kernel, tiles, 1.0 / (grid * grid)),
        out_shape=struct(1, local),
        in_specs=[smem] * 2 + [vmem] * (1 + tiles),
        out_specs=vmem,
        scratch_shapes=[pltpu.VMEM((tiles, 8, count), f32)],
        compiler_params=params_of,
        name="weight_step",
    )(tile, place, info, *rows)
    return final, out.reshape(local)


def solution(mesh):
    in_specs = (
        P(("group", "tile"), None),
        P(("group", "tile"), None),
        P(("group", "src")),
        P("src", None),
        P(),
    )
    out_specs = (P(("group", "tile"), None), P(("group", "src")))
    return jax.shard_map(
        per_device, mesh=mesh, in_specs=in_specs, out_specs=out_specs, check_vma=False
    )
```

```python
import functools
import math

import jax
import jax.numpy as jnp
import ml_dtypes
import numpy as np
from jax import lax
from jax.experimental import pallas as pl
from jax.experimental.pallas import tpu as pltpu
from jax.sharding import PartitionSpec as P


MARGIN = 64
MAX_SHIFT = 16
MASK_RATE = 0.5
WEIGHT_RATE = 0.3
TINY_EPS = 1e-06
CHUNK = 16
GROUP = 2


bf16 = jnp.bfloat16
f32 = jnp.float32


def np_split(table):
    table = np.asarray(table, np.float64)
    high = table.astype(np.float32).astype(ml_dtypes.bfloat16)
    low = (table - high.astype(np.float64)).astype(np.float32).astype(ml_dtypes.bfloat16)
    return high, low


def phases(freqs, pixels, period):
    return 2.0 * math.pi * np.mod(np.outer(freqs, pixels), period) / period


def make_tables(tile_len, box_len, max_shift):
    period = tile_len + 2 * MARGIN
    grid = box_len + 2 * max_shift
    wide = np.arange(grid) - grid // 2
    pix = np.arange(tile_len)
    full = np.arange(period)
    points = np.arange(grid)
    box = np.arange(box_len)
    out = {}
    ang = phases(wide, pix, period)
    high, low = np_split(np.concatenate([np.cos(ang), -np.sin(ang)], 0).T / (period * tile_len))
    out["spec_cols"] = np.concatenate([high, low], 1)
    ang_rows = phases(wide, full, period)
    high, low = np_split(np.concatenate([np.cos(ang_rows), np.sin(ang_rows)], 0))
    out["spec_rows"] = np.concatenate([high, low], 0)
    ang = phases(points, points, grid)
    cos, sin = np.cos(ang), np.sin(ang)
    for name, table in (
        ("lane_fwd", np.block([[cos, sin], [-sin, cos]])),
        ("lane_back", np.block([[cos, -sin], [sin, cos]])),
    ):
        high, low = np_split(table)
        out[name] = np.block([[high, low], [high, np.zeros_like(low)]])
    ang = phases(points, box, grid)
    high, low = np_split(np.concatenate([np.cos(ang), np.sin(ang)], 1))
    out["row_fwd"] = np.concatenate([high, high, low], 1)
    high, low = np_split(np.concatenate([np.cos(ang).T, np.sin(ang).T], 0))
    out["row_back"] = np.concatenate([high, high, low], 1)

    def dirichlet(offset):
        theta = 2.0 * math.pi * ((pix + offset)[None, :] / period - points[:, None] / grid)
        orders = np.arange(1, box_len)
        return 1.0 + 2.0 * np.cos(orders[:, None, None] * theta[None]).sum(0)

    rows, cols = dirichlet(MARGIN), dirichlet(0)
    high, low = np_split(rows @ rows.T / grid)
    out["mix_rows"] = np.concatenate([high, high, low], 1)
    mix = cols @ cols.T / grid
    high, low = np_split(np.block([[mix, mix], [mix, mix]]))
    out["mix_cols"] = np.block([[high, low], [high, np.zeros_like(low)]])
    high, low = np_split(rows)
    out["target_rows"] = np.concatenate([high, low], 0)
    high, low = np_split(np.concatenate([cols, cols], 0).T)
    out["target_cols"] = np.concatenate([high, low], 1)
    ang = phases(wide, pix, period)
    cos, sin = np.cos(ang), np.sin(ang)
    high, low = np_split(np.block([[cos, sin], [-sin, cos]]))
    out["grad_cols"] = np.concatenate([high, high, low], 0)
    high, low = np_split(np.concatenate([np.cos(ang_rows).T, -np.sin(ang_rows).T], 1))
    out["grad_rows"] = np.concatenate([high, high, low], 1)
    return out


def pack_tables(tables):
    wide = [n for n in tables if tables[n].shape[1] > 256]
    narrow = sorted((n for n in tables if n not in wide), key=lambda n: -tables[n].shape[0])
    place, heights = {}, [0, 0]
    for n in wide:
        place[n] = (heights[0], 0)
        heights = [heights[0] + tables[n].shape[0]] * 2
    for n in narrow:
        side = int(heights[1] < heights[0])
        place[n] = (heights[side], 256 * side)
        heights[side] += tables[n].shape[0]
    whole = np.zeros((max(heights), 512), ml_dtypes.bfloat16)
    spots = {}
    for n, (row, col) in place.items():
        rows, cols = tables[n].shape
        whole[row : row + rows, col : col + cols] = tables[n]
        spots[n] = (slice(row, row + rows), slice(col, col + cols))
    return whole, spots


def split(value):
    high = value.astype(bf16)
    return high, (value - high.astype(f32)).astype(bf16)


def dot(left, right):
    return jnp.dot(left, right, preferred_element_type=f32)


def halves(value):
    width = value.shape[1] // 2
    return value[:, :width] + value[:, width:]


def lane_sign(rows, lanes, first):
    lane = lax.broadcasted_iota(jnp.int32, (rows, lanes), 1)
    return jnp.where(lane < lanes // 2, first, -first).astype(f32)


def swap(value):
    return pltpu.roll(value, value.shape[1] // 2, 1)


def half_tanh(value):
    return jnp.tanh(0.5 * value)


def sigmoid(value):
    return 0.5 * half_tanh(value) + 0.5


def window_spectrum(window, t):
    grid = t["spec_cols"].shape[1] // 4
    high, low = split(window)
    cols = t["spec_cols"]
    mid = halves(dot(high, cols[...])) + dot(low, cols[:, : 2 * grid])
    mid_high, mid_low = split(mid)
    rows = t["spec_rows"]
    both = halves(dot(rows[: 2 * grid, :], jnp.concatenate([mid_high, mid_low], 1)))
    both = both + dot(rows[2 * grid :, :], mid_high)
    return both[:grid] + lane_sign(grid, 2 * grid, 1.0) * swap(both[grid:])


def skewed(count, stages, first, second, carry):
    chunks = count // CHUNK
    first(0, stages[0])
    for c in range(1, chunks):
        first(c, stages[c % 2])
        carry = second(c - 1, stages[(c - 1) % 2], carry)
    return second(chunks - 1, stages[(chunks - 1) % 2], carry)


def turn_pupils(pupil, turned_re, turned_im):
    count, size, lanes = turned_re.shape
    grid = lanes // 2
    turned_re[0] = jnp.zeros((size, lanes), f32)
    turned_im[0] = jnp.zeros((size, lanes), f32)
    turned_re[0, :, :size] = pupil[0]
    turned_re[0, :, grid : grid + size] = pupil[0]
    turned_im[0, :, :size] = -pupil[1]
    turned_im[0, :, grid : grid + size] = pupil[1]
    real, imag = turned_re[0], turned_im[0]
    for by in range(1, count):
        turned_re[by] = pltpu.roll(real, by, 1)
        turned_im[by] = pltpu.roll(imag, by, 1)


def placed_pupils(shifts, roots, turned_re, turned_im, pr, pi):
    def make(s):
        by = shifts[2, s] + MAX_SHIFT
        real, imag = turned_re[by] * roots[3, s], turned_im[by] * roots[3, s]
        pr[s], pi[s] = real, imag
        return real, imag

    return make


def grid_fields(spec, shifts, t, pupils, work, squares=False):
    plain, crossed, fields, *stages = work
    count, grid, lanes = fields.shape
    box_len = t["row_fwd"].shape[1] // 6
    plain[...] = spec
    crossed[...] = swap(spec)
    sign = lane_sign(box_len, lanes, -1.0)

    def first(c, stage):
        rows = []
        for i in range(CHUNK):
            s = c * CHUNK + i
            at = pl.ds(shifts[1, s] + MAX_SHIFT, box_len)
            real, imag = pupils(s)
            high, low = split(real * plain[at, :] + imag * crossed[at, :])
            rows.append(jnp.concatenate([high, low], 1))
        stage[...] = halves(dot(jnp.concatenate(rows, 0), t["lane_fwd"][...]))

    def second(c, stage, power):
        for base in range(0, CHUNK, GROUP):
            stacks = []
            for i in range(base, base + GROUP):
                part = stage[i * box_len : (i + 1) * box_len, :]
                high, low = split(jnp.concatenate([part, sign * swap(part)], 0))
                stacks.append(jnp.concatenate([high, low, high], 0))
            out = dot(t["row_fwd"][...], jnp.concatenate(stacks, 1))
            for i in range(GROUP):
                field = out[:, i * lanes : (i + 1) * lanes]
                square = field * field
                fields[c * CHUNK + base + i] = square if squares else field
                power = power + square
        return power

    return skewed(count, stages, first, second, jnp.zeros((grid, lanes), f32))


def grid_misfit(power, inv_dose, target, t):
    high, low = split(power)
    mid = halves(dot(jnp.concatenate([high, low], 1), t["mix_cols"][...]))
    high, low = split(mid)
    lit = dot(t["mix_rows"][...], jnp.concatenate([high, low, high], 0))
    return lit * inv_dose - target


def gather_back(misfit, shifts, scale, t, pr, pi, fields, stages, sums):
    count, box_len, lanes = pr.shape
    for ref in sums:
        ref[...] = jnp.zeros_like(ref)
    sign = lane_sign(box_len, lanes, 1.0)

    def first(c, stage):
        for base in range(0, CHUNK, GROUP):
            stacks = []
            for i in range(base, base + GROUP):
                high, low = split(fields[c * CHUNK + i] * misfit)
                stacks.append(jnp.concatenate([high, low, high], 0))
            both = dot(t["row_back"][...], jnp.concatenate(stacks, 1))
            for i in range(GROUP):
                part = both[:, i * lanes : (i + 1) * lanes]
                at = (base + i) * box_len
                stage[at : at + box_len, :] = part[:box_len] + sign * swap(part[box_len:])

    def second(c, stage, carry):
        high, low = split(stage[...])
        hits = halves(dot(jnp.concatenate([high, low], 1), t["lane_back"][...]))
        for i in range(CHUNK):
            s = c * CHUNK + i
            rows = pl.ds(shifts[1, s] + MAX_SHIFT, box_len)
            hit = hits[i * box_len : (i + 1) * box_len]
            one, two = sums[2 * (i % 2)], sums[2 * (i % 2) + 1]
            one[rows, :] += pr[s] * hit
            two[rows, :] += pi[s] * hit
        return carry

    skewed(count, stages, first, second, 0)
    return (sums[0][...] + sums[2][...] + swap(sums[1][...] + sums[3][...])) * scale


def tile_of(k, tile):
    return lax.bitwise_xor(tile, jnp.int32(k))


def mask_grads(params, ids, backs, t, tile, tiles, wins, grads):
    grid = backs[0].shape[0]
    tile_len = wins.shape[2]
    rows = []
    for back in backs:
        high, low = split(back[...])
        rows.append(jnp.concatenate([high, low, high], 1))
    mid = dot(jnp.concatenate(rows, 0), t["grad_cols"][...])
    wins[0, MARGIN + tile_len :, :] = jnp.zeros((MARGIN, tile_len), f32)
    wins[tiles + 1, :MARGIN, :] = jnp.zeros((MARGIN, tile_len), f32)
    for k in range(tiles):
        part = mid[k * grid : (k + 1) * grid]
        high, low = split(jnp.concatenate([part[:, :tile_len], part[:, tile_len:]], 0))
        out = dot(t["grad_rows"][...], jnp.concatenate([high, low, high], 0))
        wins[tile_of(k, tile) + 1] = out
    square = jnp.zeros((8, tile_len), f32)
    for k in range(tiles):
        own = ids[k]
        for low_row, high_row, near, shift in (
            (0, MARGIN, 0, tile_len),
            (MARGIN, tile_len - MARGIN, 1, 0),
            (tile_len - MARGIN, tile_len, 2, -tile_len),
        ):
            total = wins[own + 1, MARGIN + low_row : MARGIN + high_row, :]
            if near != 1:
                at = MARGIN + low_row + shift
                total = total + wins[own + near, at : at + MARGIN, :]
            lean = half_tanh(params(k, low_row, high_row))
            grad = total * (1.0 - lean * lean)
            grads[own, low_row:high_row, :] = grad
            square = square + jnp.sum((grad * grad).reshape(-1, 8, tile_len), axis=0)
    total = jnp.sum(jnp.sum(square, axis=0, keepdims=True), axis=1, keepdims=True)
    pixels = tiles * tile_len * tile_len
    return MASK_RATE / jnp.sqrt(total / pixels + TINY_EPS)


def edge_rows(tile, tiles, tile_len):
    above = pl.multiple_of(jnp.maximum(tile * tile_len - MARGIN, 0), MARGIN)
    below = jnp.minimum((tile + 1) * tile_len, tiles * tile_len - MARGIN)
    below = pl.multiple_of(below, MARGIN)
    return above, below, (tile > 0).astype(f32), (tile < tiles - 1).astype(f32)


def start_all(pairs, sems):
    copies = [pltpu.make_async_copy(a, b, sems.at[i]) for i, (a, b) in enumerate(pairs)]
    for copy in copies:
        copy.start()
    return copies


def pack_kernel(tile, place, weights, shifts, mask, packed, edge, hold_w, hold_s, sems):
    at = pl.multiple_of(lax.rem(tile[0], 2) * (mask.shape[0] - MARGIN), MARGIN)
    copies = start_all(
        ((weights, hold_w), (shifts, hold_s), (mask.at[pl.ds(at, MARGIN), :], edge)), sems
    )
    for copy in copies:
        copy.wait()
    fill_sources(packed, hold_w, hold_s, place)


def fill_sources(packed, weights, shifts, place):
    local = weights.shape[1]
    packed[...] = jnp.zeros_like(packed)
    packed[0:1, :local] = weights[...]
    packed[1:3, :local] = shifts[...].astype(f32)
    packed[3:4, :local] = jnp.sqrt(weights[...])
    packed[...] = pltpu.roll(packed[...], place[0] * local, 1)


def target_terms(target, t):
    rows, cols = t["target_rows"], t["target_cols"]
    grid = rows.shape[0] // 2
    high, low = split(target)
    both = dot(rows[...], high)
    mid = both[:grid] + both[grid:] + dot(rows[:grid, :], low)
    high, low = split(mid)
    return halves(dot(high, cols[...])) + dot(low, cols[:, : 2 * grid])


def doses(info, scale):
    dose = jnp.sum(info[0:1, :], axis=1, keepdims=True)
    return 1.0 / dose, scale / dose


def first_kernel(spots, peers, tiles, scale, tile, place, table, pupil, goal, weights, turns,
                 own, mate, cross, *refs):
    parts = refs[: peers - 1]
    t = {n: table.at[spot] for n, spot in spots.items()}
    back, pr, pi, info, whole, target = refs[peers - 1 : peers + 5]
    *work, s0, s1, s2, s3, turned_re, turned_im, shifts, roots, sems = refs[peers + 5 :]
    here = tile[0]
    fill_sources(info, weights, turns, place)
    total = info[...]
    for part in parts:
        total = total + part[...]
    info[...] = total
    whole[...] = total.astype(jnp.int32)
    copies = (
        pltpu.make_async_copy(whole, shifts, sems.at[0]),
        pltpu.make_async_copy(info, roots, sems.at[1]),
    )
    for copy in copies:
        copy.start()
    has_prev = (here > 0).astype(f32)
    has_next = (here < tiles - 1).astype(f32)
    odd = lax.rem(here, 2) > 0
    before = jnp.where(odd, mate[-MARGIN:, :], cross[...])
    after = jnp.where(odd, cross[...], mate[:MARGIN, :])
    window = jnp.concatenate(
        [sigmoid(before) * has_prev, sigmoid(own[...]), sigmoid(after) * has_next], 0
    )
    spec = window_spectrum(window, t)
    target[...] = target_terms(goal[...], t)
    turn_pupils(pupil, turned_re, turned_im)
    for copy in copies:
        copy.wait()
    pupils = placed_pupils(shifts, roots, turned_re, turned_im, pr, pi)
    power = grid_fields(spec, shifts, t, pupils, work)
    inv_dose, factor = doses(total, scale)
    misfit = grid_misfit(power, inv_dose, target[...], t)
    sums = (s0, s1, s2, s3)
    back[...] = gather_back(misfit, shifts, factor, t, pr, pi, work[2], work[3:], sums)


def next_kernel(spots, tiles, scale, tile, table, shifts, info, pr, pi, target, *refs):
    params, backs = refs[:tiles], refs[tiles : 2 * tiles]
    t = {n: table.at[spot] for n, spot in spots.items()}
    new, back, *work, s0, s1, s2, s3, wins, grads = refs[2 * tiles :]
    here = tile[0]
    tile_len = params[0].shape[0]
    ids = [tile_of(k, here) for k in range(tiles)]
    rate = mask_grads(
        lambda k, low, high: params[k][low:high, :], ids, backs, t, here, tiles, wins, grads
    )
    for k in range(tiles):
        own = ids[k]
        at = pl.ds(pl.multiple_of(own * tile_len, tile_len), tile_len)
        new[at, :] = params[k][...] - grads[own] * rate
    above, below, has_prev, has_next = edge_rows(here, tiles, tile_len)
    own = pl.ds(pl.multiple_of(here * tile_len, tile_len), tile_len)
    window = jnp.concatenate(
        [
            sigmoid(new[pl.ds(above, MARGIN), :]) * has_prev,
            sigmoid(new[own, :]),
            sigmoid(new[pl.ds(below, MARGIN), :]) * has_next,
        ],
        0,
    )
    spec = window_spectrum(window, t)
    power = grid_fields(spec, shifts, t, lambda s: (pr[s], pi[s]), work)
    inv_dose, factor = doses(info[...], scale)
    misfit = grid_misfit(power, inv_dose, target[...], t)
    sums = (s0, s1, s2, s3)
    back[...] = gather_back(misfit, shifts, factor, t, pr, pi, work[2], work[3:], sums)


def last_kernel(spots, tiles, tile, table, shifts, info, pr, pi, target, params, *refs):
    backs = refs[:tiles]
    t = {n: table.at[spot] for n, spot in spots.items()}
    final, row, *work, terms, wins, grads = refs[tiles:]
    fields = work[2]
    here = tile[0]
    tile_len = final.shape[0]
    rate = mask_grads(
        lambda k, low, high: params[k * tile_len + low : k * tile_len + high, :],
        list(range(tiles)), backs, t, here, tiles, wins, grads,
    )
    above, below, has_prev, has_next = edge_rows(here, tiles, tile_len)
    own = pl.ds(pl.multiple_of(here * tile_len, tile_len), tile_len)
    final[...] = params[own, :] - grads[here] * rate
    prev, follow = jnp.maximum(here - 1, 0), jnp.minimum(here + 1, tiles - 1)
    window = jnp.concatenate(
        [
            sigmoid(params[pl.ds(above, MARGIN), :] - grads[prev, tile_len - MARGIN :, :] * rate)
            * has_prev,
            sigmoid(final[...]),
            sigmoid(params[pl.ds(below, MARGIN), :] - grads[follow, :MARGIN, :] * rate)
            * has_next,
        ],
        0,
    )
    spec = window_spectrum(window, t)
    power = grid_fields(spec, shifts, t, lambda s: (pr[s], pi[s]), work, squares=True)
    inv_dose, _ = doses(info[...], 1.0)
    misfit = grid_misfit(power, inv_dose, target[...], t)

    def chunk(c, carry):
        rows = []
        for i in range(CHUNK):
            rows.append(jnp.sum(fields[c * CHUNK + i] * misfit, axis=0, keepdims=True))
        terms[pl.ds(pl.multiple_of(c * CHUNK, CHUNK), CHUNK), :] = jnp.concatenate(rows, 0)
        return carry

    count = fields.shape[0]
    lax.fori_loop(0, count // CHUNK, chunk, 0)
    high, low = split(terms[...])
    left = terms[...] - high.astype(f32) - low.astype(f32)
    ones = jnp.ones((8, terms.shape[1]), bf16)
    total = jnp.zeros((8, terms.shape[0]), f32)
    for part in (left.astype(bf16), low, high):
        total = total + lax.dot_general(
            ones, part, (((1,), (1,)), ((), ())), preferred_element_type=f32
        )
    row[...] = total


def weight_kernel(tiles, scale, tile, place, info, *refs):
    rows = refs[:tiles]
    out, stack = refs[tiles:]
    count = rows[0].shape[1]
    for k in range(tiles):
        stack[k] = rows[k][...]
    here = tile[0]
    total = stack[here]
    for k in range(1, tiles):
        total = total + stack[tile_of(k, here)]
    summed = total[0:1] * scale
    weight = info[0:1, :count]
    dose = jnp.sum(weight, axis=1, keepdims=True)
    mean = jnp.sum(summed, axis=1, keepdims=True) / dose
    grad = (summed / weight - mean) / dose
    spread = jnp.sqrt(jnp.sum(grad * grad, axis=1, keepdims=True) / count + TINY_EPS)
    new = weight * jnp.exp(-WEIGHT_RATE * grad / spread)
    size = out.shape[1]
    lanes = info.shape[1]
    if count < lanes:
        new = jnp.concatenate([new, jnp.zeros((1, lanes - count), f32)], 1)
    new = pltpu.roll(jnp.broadcast_to(new, (8, lanes)), lanes - place[0] * size, 1)
    out[...] = new[0:1, :size]


def crossed(value, axis, k):
    return lax.ppermute(value, axis, [(i, i ^ k) for i in range(lax.axis_size(axis))])


def all_of(value, axis):
    return [value] + [crossed(value, axis, k) for k in range(1, lax.axis_size(axis))]


def per_device(mask_param, target_image, source_weights, source_shifts, pupil_map):
    tile_len = mask_param.shape[1]
    box_len = pupil_map.shape[1]
    grid = box_len + 2 * MAX_SHIFT
    lanes = 2 * grid
    tiles = lax.axis_size("tile")
    peers = lax.axis_size("src")
    local = source_weights.shape[0]
    count = local * peers
    assert tiles & (tiles - 1) == 0 and peers & (peers - 1) == 0 and count <= 128 and count % CHUNK == 0
    tables = make_tables(tile_len, box_len, MAX_SHIFT)

    tile = lax.axis_index("tile").astype(jnp.int32).reshape(1)
    place = lax.axis_index("src").astype(jnp.int32).reshape(1)

    vmem = pl.BlockSpec(memory_space=pltpu.VMEM)
    smem = pl.BlockSpec(memory_space=pltpu.SMEM)
    left = pl.BlockSpec(memory_space=pltpu.HBM)
    params_of = pltpu.CompilerParams(vmem_limit_bytes=32 << 20)

    def struct(*shape, kind=f32):
        return jax.ShapeDtypeStruct(shape, kind)

    def cost(flops):
        return pl.CostEstimate(flops=flops, bytes_accessed=1 << 20, transcendentals=0)

    packed, edge = pl.pallas_call(
        pack_kernel,
        out_shape=[struct(8, 128), struct(MARGIN, tile_len)],
        in_specs=[smem, smem, left, left, left],
        out_specs=[vmem] * 2,
        scratch_shapes=[
            pltpu.VMEM((1, local), f32),
            pltpu.VMEM((2, local), jnp.int32),
            pltpu.SemaphoreType.DMA((3,)),
        ],
        cost_estimate=cost(1 << 34),
        name="pack_sources",
    )(tile, place, source_weights[None], source_shifts.T, mask_param)
    packed = all_of(packed, "src")[1:]

    pairs = [(i, (i + 1) % tiles) for i in range(1, tiles, 2)]
    cross = lax.ppermute(edge, "tile", pairs + [(j, i) for i, j in pairs])
    mate = crossed(mask_param, "tile", 1)
    far = [crossed(mask_param, "tile", k) for k in range(2, tiles, 2)]

    whole, spots = pack_tables(tables)
    table = jnp.asarray(whole)
    work = [
        pltpu.VMEM((grid, lanes), f32),
        pltpu.VMEM((grid, lanes), f32),
        pltpu.VMEM((count, grid, lanes), f32),
        pltpu.VMEM((CHUNK * box_len, lanes), f32),
        pltpu.VMEM((CHUNK * box_len, lanes), f32),
    ]
    hold = [pltpu.VMEM((grid, lanes), f32)] * 4
    steps = [
        pltpu.VMEM((tiles + 2, tile_len + 2 * MARGIN, tile_len), f32),
        pltpu.VMEM((tiles, tile_len, tile_len), f32),
    ]
    period = tile_len + 2 * MARGIN
    scale = 0.5 / (grid * grid * period * tile_len)
    source_len = struct(count, box_len, lanes)

    back, pr, pi, info, whole, target = pl.pallas_call(
        functools.partial(first_kernel, spots, peers, tiles, scale),
        out_shape=[struct(grid, lanes), source_len, source_len, struct(8, 128),
                   struct(8, 128, kind=jnp.int32), struct(grid, lanes)],
        in_specs=[smem] * 2 + [vmem] * (7 + peers),
        out_specs=[vmem] * 6,
        scratch_shapes=work + hold + [
            pltpu.VMEM((2 * MAX_SHIFT + 1, box_len, lanes), f32),
            pltpu.VMEM((2 * MAX_SHIFT + 1, box_len, lanes), f32),
            pltpu.SMEM((8, 128), jnp.int32),
            pltpu.SMEM((8, 128), f32),
            pltpu.SemaphoreType.DMA((2,)),
        ],
        compiler_params=params_of,
        cost_estimate=cost(1 << 32),
        name="first_step",
    )(tile, place, table, pupil_map, target_image, source_weights[None], source_shifts.T,
      mask_param, mate, cross, *packed)

    shared = (tile, table, whole, info, pr, pi, target)
    shared_specs = [smem, vmem, smem] + [vmem] * 4

    back, far = lax.optimization_barrier((back, far))
    backs = all_of(back, "tile")
    entries = [mask_param, mate]
    for one in far:
        entries += [one, crossed(one, "tile", 1)]
    params, back = pl.pallas_call(
        functools.partial(next_kernel, spots, tiles, scale),
        out_shape=[struct(tiles * tile_len, tile_len), struct(grid, lanes)],
        in_specs=shared_specs + [vmem] * (2 * tiles),
        out_specs=[vmem] * 2,
        scratch_shapes=work + hold + steps,
        compiler_params=params_of,
        cost_estimate=cost(1 << 32),
        name="next_step",
    )(*shared, *entries, *backs)

    backs = all_of(back, "tile")
    final, row = pl.pallas_call(
        functools.partial(last_kernel, spots, tiles),
        out_shape=[struct(tile_len, tile_len), struct(8, count)],
        in_specs=shared_specs + [vmem] * (1 + tiles),
        out_specs=[vmem] * 2,
        scratch_shapes=work + [pltpu.VMEM((count, lanes), f32)] + steps,
        compiler_params=params_of,
        cost_estimate=cost(1 << 32),
        name="last_step",
    )(*shared, params, *backs)

    rows = all_of(row, "tile")
    out = pl.pallas_call(
        functools.partial(weight_kernel, tiles, 1.0 / (grid * grid)),
        out_shape=struct(1, local),
        in_specs=[smem] * 2 + [vmem] * (1 + tiles),
        out_specs=vmem,
        scratch_shapes=[pltpu.VMEM((tiles, 8, count), f32)],
        compiler_params=params_of,
        name="weight_step",
    )(tile, place, info, *rows)
    return final, out.reshape(local)


def solution(mesh):
    in_specs = (
        P(("group", "tile"), None),
        P(("group", "tile"), None),
        P(("group", "src")),
        P("src", None),
        P(),
    )
    out_specs = (P(("group", "tile"), None), P(("group", "src")))
    return jax.shard_map(
        per_device, mesh=mesh, in_specs=in_specs, out_specs=out_specs, check_vma=False
    )
```

```python
import functools
import math

import jax
import jax.numpy as jnp
import ml_dtypes
import numpy as np
from jax import lax
from jax.experimental import pallas as pl
from jax.experimental.pallas import tpu as pltpu
from jax.sharding import PartitionSpec as P


MARGIN = 64
MAX_SHIFT = 16
MASK_RATE = 0.5
WEIGHT_RATE = 0.3
TINY_EPS = 1e-06
CHUNK = 16
GROUP = 2


bf16 = jnp.bfloat16
f32 = jnp.float32


def np_split(table):
    table = np.asarray(table, np.float64)
    high = table.astype(np.float32).astype(ml_dtypes.bfloat16)
    low = (table - high.astype(np.float64)).astype(np.float32).astype(ml_dtypes.bfloat16)
    return high, low


def phases(freqs, pixels, period):
    return 2.0 * math.pi * np.mod(np.outer(freqs, pixels), period) / period


def make_tables(tile_len, box_len, max_shift):
    period = tile_len + 2 * MARGIN
    grid = box_len + 2 * max_shift
    wide = np.arange(grid) - grid // 2
    pix = np.arange(tile_len)
    full = np.arange(period)
    points = np.arange(grid)
    box = np.arange(box_len)
    out = {}
    ang = phases(wide, pix, period)
    high, low = np_split(np.concatenate([np.cos(ang), -np.sin(ang)], 0).T / (period * tile_len))
    out["spec_cols"] = np.concatenate([high, low], 1)
    ang_rows = phases(wide, full, period)
    high, low = np_split(np.concatenate([np.cos(ang_rows), np.sin(ang_rows)], 0))
    out["spec_rows"] = np.concatenate([high, low], 0)
    ang = phases(points, points, grid)
    cos, sin = np.cos(ang), np.sin(ang)
    for name, table in (
        ("lane_fwd", np.block([[cos, sin], [-sin, cos]])),
        ("lane_back", np.block([[cos, -sin], [sin, cos]])),
    ):
        high, low = np_split(table)
        out[name] = np.block([[high, low], [high, np.zeros_like(low)]])
    ang = phases(points, box, grid)
    high, low = np_split(np.concatenate([np.cos(ang), np.sin(ang)], 1))
    out["row_fwd"] = np.concatenate([high, high, low], 1)
    high, low = np_split(np.concatenate([np.cos(ang).T, np.sin(ang).T], 0))
    out["row_back"] = np.concatenate([high, high, low], 1)

    def dirichlet(offset):
        theta = 2.0 * math.pi * ((pix + offset)[None, :] / period - points[:, None] / grid)
        orders = np.arange(1, box_len)
        return 1.0 + 2.0 * np.cos(orders[:, None, None] * theta[None]).sum(0)

    rows, cols = dirichlet(MARGIN), dirichlet(0)
    high, low = np_split(rows @ rows.T / grid)
    out["mix_rows"] = np.concatenate([high, high, low], 1)
    mix = cols @ cols.T / grid
    high, low = np_split(np.block([[mix, mix], [mix, mix]]))
    out["mix_cols"] = np.block([[high, low], [high, np.zeros_like(low)]])
    high, low = np_split(rows)
    out["target_rows"] = np.concatenate([high, low], 0)
    high, low = np_split(np.concatenate([cols, cols], 0).T)
    out["target_cols"] = np.concatenate([high, low], 1)
    ang = phases(wide, pix, period)
    cos, sin = np.cos(ang), np.sin(ang)
    high, low = np_split(np.block([[cos, sin], [-sin, cos]]))
    out["grad_cols"] = np.concatenate([high, high, low], 0)
    high, low = np_split(np.concatenate([np.cos(ang_rows).T, -np.sin(ang_rows).T], 1))
    out["grad_rows"] = np.concatenate([high, high, low], 1)
    return out


def pack_tables(tables):
    wide = [n for n in tables if tables[n].shape[1] > 256]
    narrow = sorted((n for n in tables if n not in wide), key=lambda n: -tables[n].shape[0])
    place, heights = {}, [0, 0]
    for n in wide:
        place[n] = (heights[0], 0)
        heights = [heights[0] + tables[n].shape[0]] * 2
    for n in narrow:
        side = int(heights[1] < heights[0])
        place[n] = (heights[side], 256 * side)
        heights[side] += tables[n].shape[0]
    whole = np.zeros((max(heights), 512), ml_dtypes.bfloat16)
    spots = {}
    for n, (row, col) in place.items():
        rows, cols = tables[n].shape
        whole[row : row + rows, col : col + cols] = tables[n]
        spots[n] = (slice(row, row + rows), slice(col, col + cols))
    return whole, spots


def split(value):
    high = value.astype(bf16)
    return high, (value - high.astype(f32)).astype(bf16)


def dot(left, right):
    return jnp.dot(left, right, preferred_element_type=f32)


def halves(value):
    width = value.shape[1] // 2
    return value[:, :width] + value[:, width:]


def lane_sign(rows, lanes, first):
    lane = lax.broadcasted_iota(jnp.int32, (rows, lanes), 1)
    return jnp.where(lane < lanes // 2, first, -first).astype(f32)


def swap(value):
    return pltpu.roll(value, value.shape[1] // 2, 1)


def half_tanh(value):
    return jnp.tanh(0.5 * value)


def sigmoid(value):
    return 0.5 * half_tanh(value) + 0.5


def window_spectrum(window, t):
    grid = t["spec_cols"].shape[1] // 4
    high, low = split(window)
    cols = t["spec_cols"]
    mid = halves(dot(high, cols[...])) + dot(low, cols[:, : 2 * grid])
    mid_high, mid_low = split(mid)
    rows = t["spec_rows"]
    both = halves(dot(rows[: 2 * grid, :], jnp.concatenate([mid_high, mid_low], 1)))
    both = both + dot(rows[2 * grid :, :], mid_high)
    return both[:grid] + lane_sign(grid, 2 * grid, 1.0) * swap(both[grid:])


def skewed(count, stages, first, second, carry):
    chunks = count // CHUNK
    first(0, stages[0])
    for c in range(1, chunks):
        first(c, stages[c % 2])
        carry = second(c - 1, stages[(c - 1) % 2], carry)
    return second(chunks - 1, stages[(chunks - 1) % 2], carry)


def turn_pupils(pupil, turned_re, turned_im):
    count, size, lanes = turned_re.shape
    grid = lanes // 2
    turned_re[0] = jnp.zeros((size, lanes), f32)
    turned_im[0] = jnp.zeros((size, lanes), f32)
    turned_re[0, :, :size] = pupil[0]
    turned_re[0, :, grid : grid + size] = pupil[0]
    turned_im[0, :, :size] = -pupil[1]
    turned_im[0, :, grid : grid + size] = pupil[1]
    real, imag = turned_re[0], turned_im[0]
    for by in range(1, count):
        turned_re[by] = pltpu.roll(real, by, 1)
        turned_im[by] = pltpu.roll(imag, by, 1)


def placed_pupils(shifts, roots, turned_re, turned_im, pr, pi):
    def make(s):
        by = shifts[2, s] + MAX_SHIFT
        real, imag = turned_re[by] * roots[3, s], turned_im[by] * roots[3, s]
        pr[s], pi[s] = real, imag
        return real, imag

    return make


def grid_fields(spec, shifts, t, pupils, work, squares=False):
    plain, crossed, fields, *stages = work
    count, grid, lanes = fields.shape
    box_len = t["row_fwd"].shape[1] // 6
    if spec is not None:
        plain[...] = spec
        crossed[...] = swap(spec)
    sign = lane_sign(box_len, lanes, -1.0)

    def first(c, stage):
        rows = []
        for i in range(CHUNK):
            s = c * CHUNK + i
            at = pl.ds(shifts[1, s] + MAX_SHIFT, box_len)
            real, imag = pupils(s)
            high, low = split(real * plain[at, :] + imag * crossed[at, :])
            rows.append(jnp.concatenate([high, low], 1))
        stage[...] = halves(dot(jnp.concatenate(rows, 0), t["lane_fwd"][...]))

    def second(c, stage, power):
        for base in range(0, CHUNK, GROUP):
            stacks = []
            for i in range(base, base + GROUP):
                part = stage[i * box_len : (i + 1) * box_len, :]
                high, low = split(jnp.concatenate([part, sign * swap(part)], 0))
                stacks.append(jnp.concatenate([high, low, high], 0))
            out = dot(t["row_fwd"][...], jnp.concatenate(stacks, 1))
            for i in range(GROUP):
                field = out[:, i * lanes : (i + 1) * lanes]
                square = field * field
                fields[c * CHUNK + base + i] = square if squares else field
                power = power + square
        return power

    return skewed(count, stages, first, second, jnp.zeros((grid, lanes), f32))


def grid_misfit(power, inv_dose, target, t):
    high, low = split(power)
    mid = halves(dot(jnp.concatenate([high, low], 1), t["mix_cols"][...]))
    high, low = split(mid)
    lit = dot(t["mix_rows"][...], jnp.concatenate([high, low, high], 0))
    return lit * inv_dose - target


def gather_back(misfit, shifts, scale, t, pr, pi, fields, stages, sums):
    count, box_len, lanes = pr.shape
    for ref in sums:
        ref[...] = jnp.zeros_like(ref)
    sign = lane_sign(box_len, lanes, 1.0)

    def first(c, stage):
        for base in range(0, CHUNK, GROUP):
            stacks = []
            for i in range(base, base + GROUP):
                high, low = split(fields[c * CHUNK + i] * misfit)
                stacks.append(jnp.concatenate([high, low, high], 0))
            both = dot(t["row_back"][...], jnp.concatenate(stacks, 1))
            for i in range(GROUP):
                part = both[:, i * lanes : (i + 1) * lanes]
                at = (base + i) * box_len
                stage[at : at + box_len, :] = part[:box_len] + sign * swap(part[box_len:])

    def second(c, stage, carry):
        high, low = split(stage[...])
        hits = halves(dot(jnp.concatenate([high, low], 1), t["lane_back"][...]))
        for i in range(CHUNK):
            s = c * CHUNK + i
            rows = pl.ds(shifts[1, s] + MAX_SHIFT, box_len)
            hit = hits[i * box_len : (i + 1) * box_len]
            one, two = sums[2 * (i % 2)], sums[2 * (i % 2) + 1]
            one[rows, :] += pr[s] * hit
            two[rows, :] += pi[s] * hit
        return carry

    skewed(count, stages, first, second, 0)
    return (sums[0][...] + sums[2][...] + swap(sums[1][...] + sums[3][...])) * scale


def tile_of(k, tile):
    return lax.bitwise_xor(tile, jnp.int32(k))


def mask_grads(params, ids, backs, t, tile, tiles, wins, grads):
    grid = backs[0].shape[0]
    tile_len = wins.shape[2]
    rows = []
    for back in backs:
        high, low = split(back[...])
        rows.append(jnp.concatenate([high, low, high], 1))
    mid = dot(jnp.concatenate(rows, 0), t["grad_cols"][...])
    wins[0, MARGIN + tile_len :, :] = jnp.zeros((MARGIN, tile_len), f32)
    wins[tiles + 1, :MARGIN, :] = jnp.zeros((MARGIN, tile_len), f32)
    for k in range(tiles):
        part = mid[k * grid : (k + 1) * grid]
        high, low = split(jnp.concatenate([part[:, :tile_len], part[:, tile_len:]], 0))
        out = dot(t["grad_rows"][...], jnp.concatenate([high, low, high], 0))
        wins[tile_of(k, tile) + 1] = out
    square = jnp.zeros((8, tile_len), f32)
    for k in range(tiles):
        own = ids[k]
        for low_row, high_row, near, shift in (
            (0, MARGIN, 0, tile_len),
            (MARGIN, tile_len - MARGIN, 1, 0),
            (tile_len - MARGIN, tile_len, 2, -tile_len),
        ):
            total = wins[own + 1, MARGIN + low_row : MARGIN + high_row, :]
            if near != 1:
                at = MARGIN + low_row + shift
                total = total + wins[own + near, at : at + MARGIN, :]
            lean = half_tanh(params(k, low_row, high_row))
            grad = total * (1.0 - lean * lean)
            grads[own, low_row:high_row, :] = grad
            square = square + jnp.sum((grad * grad).reshape(-1, 8, tile_len), axis=0)
    total = jnp.sum(jnp.sum(square, axis=0, keepdims=True), axis=1, keepdims=True)
    pixels = tiles * tile_len * tile_len
    return MASK_RATE / jnp.sqrt(total / pixels + TINY_EPS)


def edge_rows(tile, tiles, tile_len):
    above = pl.multiple_of(jnp.maximum(tile * tile_len - MARGIN, 0), MARGIN)
    below = jnp.minimum((tile + 1) * tile_len, tiles * tile_len - MARGIN)
    below = pl.multiple_of(below, MARGIN)
    return above, below, (tile > 0).astype(f32), (tile < tiles - 1).astype(f32)


def start_all(pairs, sems):
    copies = [pltpu.make_async_copy(a, b, sems.at[i]) for i, (a, b) in enumerate(pairs)]
    for copy in copies:
        copy.start()
    return copies


def head_kernel(out):
    out[...] = jnp.zeros_like(out)


def pack_kernel(tile, place, head, weights, shifts, mask, packed, edge):
    at = pl.multiple_of(lax.rem(tile[0], 2) * (mask.shape[0] - MARGIN), MARGIN)
    edge[...] = mask[pl.ds(at, MARGIN), :]
    local = weights.shape[1]
    packed[...] = head[...]
    packed[0:1, :local] = weights[...]
    packed[1:3, :local] = shifts[...].astype(f32)
    packed[3:4, :local] = jnp.sqrt(weights[...])
    packed[...] = pltpu.roll(packed[...], place[0] * local, 1)


def target_terms(target, t):
    rows, cols = t["target_rows"], t["target_cols"]
    grid = rows.shape[0] // 2
    high, low = split(target)
    both = dot(rows[...], high)
    mid = both[:grid] + both[grid:] + dot(rows[:grid, :], low)
    high, low = split(mid)
    return halves(dot(high, cols[...])) + dot(low, cols[:, : 2 * grid])


def doses(info, scale):
    dose = jnp.sum(info[0:1, :], axis=1, keepdims=True)
    return 1.0 / dose, scale / dose


def ready_kernel(spots, tiles, tile, table, pupil, goal, own, mate, cross,
                 plain, crossed, target, turned_re, turned_im):
    t = {n: table.at[spot] for n, spot in spots.items()}
    here = tile[0]
    has_prev = (here > 0).astype(f32)
    has_next = (here < tiles - 1).astype(f32)
    odd = lax.rem(here, 2) > 0
    before = jnp.where(odd, mate[-MARGIN:, :], cross[...])
    after = jnp.where(odd, cross[...], mate[:MARGIN, :])
    window = jnp.concatenate(
        [sigmoid(before) * has_prev, sigmoid(own[...]), sigmoid(after) * has_next], 0
    )
    turn_pupils(pupil, turned_re, turned_im)
    spec = window_spectrum(window, t)
    plain[...] = spec
    crossed[...] = swap(spec)
    target[...] = target_terms(goal[...], t)


def first_kernel(spots, peers, scale, table, plain, crossed, target, turned_re, turned_im, *refs):
    parts = refs[:peers]
    t = {n: table.at[spot] for n, spot in spots.items()}
    back, pr, pi, info, whole = refs[peers : peers + 5]
    *work, s0, s1, s2, s3, shifts, roots, sems = refs[peers + 5 :]
    total = parts[0][...]
    for part in parts[1:]:
        total = total + part[...]
    info[...] = total
    whole[...] = total.astype(jnp.int32)
    for copy in start_all(((whole, shifts), (info, roots)), sems):
        copy.wait()
    pupils = placed_pupils(shifts, roots, turned_re, turned_im, pr, pi)
    work = [plain, crossed, *work]
    power = grid_fields(None, shifts, t, pupils, work)
    inv_dose, factor = doses(total, scale)
    misfit = grid_misfit(power, inv_dose, target[...], t)
    sums = (s0, s1, s2, s3)
    back[...] = gather_back(misfit, shifts, factor, t, pr, pi, work[2], work[3:], sums)


def next_kernel(spots, tiles, scale, tile, table, shifts, info, pr, pi, target, *refs):
    params, backs = refs[:tiles], refs[tiles : 2 * tiles]
    t = {n: table.at[spot] for n, spot in spots.items()}
    new, back, *work, s0, s1, s2, s3, wins, grads = refs[2 * tiles :]
    here = tile[0]
    tile_len = params[0].shape[0]
    ids = [tile_of(k, here) for k in range(tiles)]
    rate = mask_grads(
        lambda k, low, high: params[k][low:high, :], ids, backs, t, here, tiles, wins, grads
    )
    for k in range(tiles):
        own = ids[k]
        at = pl.ds(pl.multiple_of(own * tile_len, tile_len), tile_len)
        new[at, :] = params[k][...] - grads[own] * rate
    above, below, has_prev, has_next = edge_rows(here, tiles, tile_len)
    own = pl.ds(pl.multiple_of(here * tile_len, tile_len), tile_len)
    window = jnp.concatenate(
        [
            sigmoid(new[pl.ds(above, MARGIN), :]) * has_prev,
            sigmoid(new[own, :]),
            sigmoid(new[pl.ds(below, MARGIN), :]) * has_next,
        ],
        0,
    )
    spec = window_spectrum(window, t)
    power = grid_fields(spec, shifts, t, lambda s: (pr[s], pi[s]), work)
    inv_dose, factor = doses(info[...], scale)
    misfit = grid_misfit(power, inv_dose, target[...], t)
    sums = (s0, s1, s2, s3)
    back[...] = gather_back(misfit, shifts, factor, t, pr, pi, work[2], work[3:], sums)


def last_kernel(spots, tiles, tile, table, shifts, info, pr, pi, target, params, *refs):
    backs = refs[:tiles]
    t = {n: table.at[spot] for n, spot in spots.items()}
    final, row, *work, terms, wins, grads, fresh, sems = refs[tiles:]
    fields = work[2]
    here = tile[0]
    tile_len = fresh.shape[0]
    rate = mask_grads(
        lambda k, low, high: params[k * tile_len + low : k * tile_len + high, :],
        list(range(tiles)), backs, t, here, tiles, wins, grads,
    )
    above, below, has_prev, has_next = edge_rows(here, tiles, tile_len)
    own = pl.ds(pl.multiple_of(here * tile_len, tile_len), tile_len)
    fresh[...] = params[own, :] - grads[here] * rate
    (leave,) = start_all(((fresh, final),), sems)
    prev, follow = jnp.maximum(here - 1, 0), jnp.minimum(here + 1, tiles - 1)
    window = jnp.concatenate(
        [
            sigmoid(params[pl.ds(above, MARGIN), :] - grads[prev, tile_len - MARGIN :, :] * rate)
            * has_prev,
            sigmoid(fresh[...]),
            sigmoid(params[pl.ds(below, MARGIN), :] - grads[follow, :MARGIN, :] * rate)
            * has_next,
        ],
        0,
    )
    spec = window_spectrum(window, t)
    power = grid_fields(spec, shifts, t, lambda s: (pr[s], pi[s]), work, squares=True)
    inv_dose, _ = doses(info[...], 1.0)
    misfit = grid_misfit(power, inv_dose, target[...], t)

    def chunk(c, carry):
        rows = []
        for i in range(CHUNK):
            rows.append(jnp.sum(fields[c * CHUNK + i] * misfit, axis=0, keepdims=True))
        terms[pl.ds(pl.multiple_of(c * CHUNK, CHUNK), CHUNK), :] = jnp.concatenate(rows, 0)
        return carry

    count = fields.shape[0]
    lax.fori_loop(0, count // CHUNK, chunk, 0)
    high, low = split(terms[...])
    left = terms[...] - high.astype(f32) - low.astype(f32)
    ones = jnp.ones((8, terms.shape[1]), bf16)
    total = jnp.zeros((8, terms.shape[0]), f32)
    for part in (left.astype(bf16), low, high):
        total = total + lax.dot_general(
            ones, part, (((1,), (1,)), ((), ())), preferred_element_type=f32
        )
    row[...] = total
    leave.wait()


def weight_kernel(tiles, scale, tile, place, info, *refs):
    rows = refs[:tiles]
    out, stack = refs[tiles:]
    count = rows[0].shape[1]
    for k in range(tiles):
        stack[k] = rows[k][...]
    here = tile[0]
    total = stack[here]
    for k in range(1, tiles):
        total = total + stack[tile_of(k, here)]
    summed = total[0:1] * scale
    weight = info[0:1, :count]
    dose = jnp.sum(weight, axis=1, keepdims=True)
    mean = jnp.sum(summed, axis=1, keepdims=True) / dose
    grad = (summed / weight - mean) / dose
    spread = jnp.sqrt(jnp.sum(grad * grad, axis=1, keepdims=True) / count + TINY_EPS)
    new = weight * jnp.exp(-WEIGHT_RATE * grad / spread)
    size = out.shape[1]
    lanes = info.shape[1]
    if count < lanes:
        new = jnp.concatenate([new, jnp.zeros((1, lanes - count), f32)], 1)
    new = pltpu.roll(jnp.broadcast_to(new, (8, lanes)), lanes - place[0] * size, 1)
    out[...] = new[0:1, :size]


def crossed(value, axis, k):
    return lax.ppermute(value, axis, [(i, i ^ k) for i in range(lax.axis_size(axis))])


def all_of(value, axis):
    return [value] + [crossed(value, axis, k) for k in range(1, lax.axis_size(axis))]


def per_device(mask_param, target_image, source_weights, source_shifts, pupil_map):
    tile_len = mask_param.shape[1]
    box_len = pupil_map.shape[1]
    grid = box_len + 2 * MAX_SHIFT
    lanes = 2 * grid
    tiles = lax.axis_size("tile")
    peers = lax.axis_size("src")
    local = source_weights.shape[0]
    count = local * peers
    assert tiles & (tiles - 1) == 0 and peers & (peers - 1) == 0 and count <= 128 and count % CHUNK == 0
    tables = make_tables(tile_len, box_len, MAX_SHIFT)

    tile = lax.axis_index("tile").astype(jnp.int32).reshape(1)
    place = lax.axis_index("src").astype(jnp.int32).reshape(1)

    vmem = pl.BlockSpec(memory_space=pltpu.VMEM)
    smem = pl.BlockSpec(memory_space=pltpu.SMEM)
    left = pl.BlockSpec(memory_space=pltpu.HBM)
    params_of = pltpu.CompilerParams(vmem_limit_bytes=32 << 20)

    def struct(*shape, kind=f32):
        return jax.ShapeDtypeStruct(shape, kind)

    def cost(flops):
        return pl.CostEstimate(flops=flops, bytes_accessed=1 << 20, transcendentals=0)

    head = pl.pallas_call(
        head_kernel,
        out_shape=struct(8, 128),
        out_specs=vmem,
        compiler_params=params_of,
        cost_estimate=cost(1 << 34),
        name="head_step",
    )()
    packed, edge = pl.pallas_call(
        pack_kernel,
        out_shape=[struct(8, 128), struct(MARGIN, tile_len)],
        in_specs=[smem, smem] + [vmem] * 4,
        out_specs=[vmem] * 2,
        compiler_params=params_of,
        cost_estimate=cost(1 << 20),
        name="pack_sources",
    )(tile, place, head, source_weights[None], source_shifts.T, mask_param)
    packed = all_of(packed, "src")

    pairs = [(i, (i + 1) % tiles) for i in range(1, tiles, 2)]
    cross = lax.ppermute(edge, "tile", pairs + [(j, i) for i, j in pairs])
    mate = crossed(mask_param, "tile", 1)
    far = [crossed(mask_param, "tile", k) for k in range(2, tiles, 2)]

    whole, spots = pack_tables(tables)
    table = jnp.asarray(whole)
    work = [
        pltpu.VMEM((grid, lanes), f32),
        pltpu.VMEM((grid, lanes), f32),
        pltpu.VMEM((count, grid, lanes), f32),
        pltpu.VMEM((CHUNK * box_len, lanes), f32),
        pltpu.VMEM((CHUNK * box_len, lanes), f32),
    ]
    hold = [pltpu.VMEM((grid, lanes), f32)] * 4
    steps = [
        pltpu.VMEM((tiles + 2, tile_len + 2 * MARGIN, tile_len), f32),
        pltpu.VMEM((tiles, tile_len, tile_len), f32),
    ]
    period = tile_len + 2 * MARGIN
    scale = 0.5 / (grid * grid * period * tile_len)
    source_len = struct(count, box_len, lanes)

    plain, crossed_spec, target, *turned = pl.pallas_call(
        functools.partial(ready_kernel, spots, tiles),
        out_shape=[struct(grid, lanes)] * 3 + [struct(2 * MAX_SHIFT + 1, box_len, lanes)] * 2,
        in_specs=[smem] + [vmem] * 6,
        out_specs=[vmem] * 5,
        compiler_params=params_of,
        cost_estimate=cost(1 << 30),
        name="ready_step",
    )(tile, table, pupil_map, target_image, mask_param, mate, cross)

    back, pr, pi, info, whole = pl.pallas_call(
        functools.partial(first_kernel, spots, peers, scale),
        out_shape=[struct(grid, lanes), source_len, source_len, struct(8, 128),
                   struct(8, 128, kind=jnp.int32)],
        in_specs=[vmem] * (6 + peers),
        out_specs=[vmem] * 5,
        scratch_shapes=work[2:] + hold + [
            pltpu.SMEM((8, 128), jnp.int32),
            pltpu.SMEM((8, 128), f32),
            pltpu.SemaphoreType.DMA((2,)),
        ],
        compiler_params=params_of,
        cost_estimate=cost(1 << 32),
        name="first_step",
    )(table, plain, crossed_spec, target, *turned, *packed)

    shared = (tile, table, whole, info, pr, pi, target)
    shared_specs = [smem, vmem, smem] + [vmem] * 4

    back, far = lax.optimization_barrier((back, far))
    backs = all_of(back, "tile")
    entries = [mask_param, mate]
    for one in far:
        entries += [one, crossed(one, "tile", 1)]
    params, back = pl.pallas_call(
        functools.partial(next_kernel, spots, tiles, scale),
        out_shape=[struct(tiles * tile_len, tile_len), struct(grid, lanes)],
        in_specs=shared_specs + [vmem] * (2 * tiles),
        out_specs=[vmem] * 2,
        scratch_shapes=work + hold + steps,
        compiler_params=params_of,
        cost_estimate=cost(1 << 32),
        name="next_step",
    )(*shared, *entries, *backs)

    backs = all_of(back, "tile")
    final, row = pl.pallas_call(
        functools.partial(last_kernel, spots, tiles),
        out_shape=[struct(tile_len, tile_len), struct(8, count)],
        in_specs=shared_specs + [vmem] * (1 + tiles),
        out_specs=[left, vmem],
        scratch_shapes=work + [pltpu.VMEM((count, lanes), f32)] + steps + [
            pltpu.VMEM((tile_len, tile_len), f32),
            pltpu.SemaphoreType.DMA((1,)),
        ],
        compiler_params=params_of,
        cost_estimate=cost(1 << 32),
        name="last_step",
    )(*shared, params, *backs)

    rows = all_of(row, "tile")
    out = pl.pallas_call(
        functools.partial(weight_kernel, tiles, 1.0 / (grid * grid)),
        out_shape=struct(1, local),
        in_specs=[smem] * 2 + [vmem] * (1 + tiles),
        out_specs=vmem,
        scratch_shapes=[pltpu.VMEM((tiles, 8, count), f32)],
        compiler_params=params_of,
        name="weight_step",
    )(tile, place, info, *rows)
    return final, out.reshape(local)


def solution(mesh):
    in_specs = (
        P(("group", "tile"), None),
        P(("group", "tile"), None),
        P(("group", "src")),
        P("src", None),
        P(),
    )
    out_specs = (P(("group", "tile"), None), P(("group", "src")))
    return jax.shard_map(
        per_device, mesh=mesh, in_specs=in_specs, out_specs=out_specs, check_vma=False
    )
```

```python
import functools
import math

import jax
import jax.numpy as jnp
import ml_dtypes
import numpy as np
from jax import lax
from jax.experimental import pallas as pl
from jax.experimental.pallas import tpu as pltpu
from jax.sharding import PartitionSpec as P


MARGIN = 64
MAX_SHIFT = 16
MASK_RATE = 0.5
WEIGHT_RATE = 0.3
TINY_EPS = 1e-06
CHUNK = 16
GROUP = 2


bf16 = jnp.bfloat16
f32 = jnp.float32


def np_split(table):
    table = np.asarray(table, np.float64)
    high = table.astype(np.float32).astype(ml_dtypes.bfloat16)
    low = (table - high.astype(np.float64)).astype(np.float32).astype(ml_dtypes.bfloat16)
    return high, low


def phases(freqs, pixels, period):
    return 2.0 * math.pi * np.mod(np.outer(freqs, pixels), period) / period


def make_tables(tile_len, box_len, max_shift):
    period = tile_len + 2 * MARGIN
    grid = box_len + 2 * max_shift
    wide = np.arange(grid) - grid // 2
    pix = np.arange(tile_len)
    full = np.arange(period)
    points = np.arange(grid)
    box = np.arange(box_len)
    out = {}
    ang = phases(wide, pix, period)
    high, low = np_split(np.concatenate([np.cos(ang), -np.sin(ang)], 0).T / (period * tile_len))
    out["spec_cols"] = np.concatenate([high, low], 1)
    ang_rows = phases(wide, full, period)
    high, low = np_split(np.concatenate([np.cos(ang_rows), np.sin(ang_rows)], 0))
    out["spec_rows"] = np.concatenate([high, low], 0)
    ang = phases(points, points, grid)
    cos, sin = np.cos(ang), np.sin(ang)
    for name, table in (
        ("lane_fwd", np.block([[cos, sin], [-sin, cos]])),
        ("lane_back", np.block([[cos, -sin], [sin, cos]])),
    ):
        high, low = np_split(table)
        out[name] = np.block([[high, low], [high, np.zeros_like(low)]])
    ang = phases(points, box, grid)
    high, low = np_split(np.concatenate([np.cos(ang), np.sin(ang)], 1))
    out["row_fwd"] = np.concatenate([high, high, low], 1)
    high, low = np_split(np.concatenate([np.cos(ang).T, np.sin(ang).T], 0))
    out["row_back"] = np.concatenate([high, high, low], 1)

    def dirichlet(offset):
        theta = 2.0 * math.pi * ((pix + offset)[None, :] / period - points[:, None] / grid)
        orders = np.arange(1, box_len)
        return 1.0 + 2.0 * np.cos(orders[:, None, None] * theta[None]).sum(0)

    rows, cols = dirichlet(MARGIN), dirichlet(0)
    high, low = np_split(rows @ rows.T / grid)
    out["mix_rows"] = np.concatenate([high, high, low], 1)
    mix = cols @ cols.T / grid
    high, low = np_split(np.block([[mix, mix], [mix, mix]]))
    out["mix_cols"] = np.block([[high, low], [high, np.zeros_like(low)]])
    high, low = np_split(rows)
    out["target_rows"] = np.concatenate([high, low], 0)
    high, low = np_split(np.concatenate([cols, cols], 0).T)
    out["target_cols"] = np.concatenate([high, low], 1)
    ang = phases(wide, pix, period)
    cos, sin = np.cos(ang), np.sin(ang)
    high, low = np_split(np.block([[cos, -sin], [-sin, -cos]]))
    out["grad_cols"] = np.concatenate([high, high, low], 0)
    ang = phases(full, np.arange(grid // 2), period)
    high, low = np_split(np.concatenate([np.cos(ang), np.sin(ang)], 1))
    out["grad_rows"] = np.concatenate([high, high, low], 1)
    return out


def pack_tables(tables):
    wide = [n for n in tables if tables[n].shape[1] > 256]
    narrow = sorted((n for n in tables if n not in wide), key=lambda n: -tables[n].shape[0])
    place, heights = {}, [0, 0]
    for n in wide:
        place[n] = (heights[0], 0)
        heights = [heights[0] + tables[n].shape[0]] * 2
    for n in narrow:
        side = int(heights[1] < heights[0])
        place[n] = (heights[side], 256 * side)
        heights[side] += tables[n].shape[0]
    whole = np.zeros((max(heights), 512), ml_dtypes.bfloat16)
    spots = {}
    for n, (row, col) in place.items():
        rows, cols = tables[n].shape
        whole[row : row + rows, col : col + cols] = tables[n]
        spots[n] = (slice(row, row + rows), slice(col, col + cols))
    return whole, spots


def split(value):
    high = value.astype(bf16)
    return high, (value - high.astype(f32)).astype(bf16)


def dot(left, right):
    return jnp.dot(left, right, preferred_element_type=f32)


def halves(value):
    width = value.shape[1] // 2
    return value[:, :width] + value[:, width:]


def lane_sign(rows, lanes, first):
    lane = lax.broadcasted_iota(jnp.int32, (rows, lanes), 1)
    return jnp.where(lane < lanes // 2, first, -first).astype(f32)


def swap(value):
    return pltpu.roll(value, value.shape[1] // 2, 1)


def half_tanh(value):
    return jnp.tanh(0.5 * value)


def sigmoid(value):
    return 0.5 * half_tanh(value) + 0.5


def window_spectrum(window, t):
    grid = t["spec_cols"].shape[1] // 4
    high, low = split(window)
    cols = t["spec_cols"]
    mid = halves(dot(high, cols[...])) + dot(low, cols[:, : 2 * grid])
    mid_high, mid_low = split(mid)
    rows = t["spec_rows"]
    both = halves(dot(rows[: 2 * grid, :], jnp.concatenate([mid_high, mid_low], 1)))
    both = both + dot(rows[2 * grid :, :], mid_high)
    return both[:grid] + lane_sign(grid, 2 * grid, 1.0) * swap(both[grid:])


def skewed(count, stages, first, second, carry):
    chunks = count // CHUNK
    first(0, stages[0])
    for c in range(1, chunks):
        first(c, stages[c % 2])
        carry = second(c - 1, stages[(c - 1) % 2], carry)
    return second(chunks - 1, stages[(chunks - 1) % 2], carry)


def turn_pupils(pupil, turned_re, turned_im):
    count, size, lanes = turned_re.shape
    grid = lanes // 2
    turned_re[0] = jnp.zeros((size, lanes), f32)
    turned_im[0] = jnp.zeros((size, lanes), f32)
    turned_re[0, :, :size] = pupil[0]
    turned_re[0, :, grid : grid + size] = pupil[0]
    turned_im[0, :, :size] = -pupil[1]
    turned_im[0, :, grid : grid + size] = pupil[1]
    real, imag = turned_re[0], turned_im[0]
    for by in range(1, count):
        turned_re[by] = pltpu.roll(real, by, 1)
        turned_im[by] = pltpu.roll(imag, by, 1)


def placed_pupils(shifts, roots, turned_re, turned_im, pr, pi):
    def make(s):
        by = shifts[2, s] + MAX_SHIFT
        real, imag = turned_re[by] * roots[3, s], turned_im[by] * roots[3, s]
        pr[s], pi[s] = real, imag
        return real, imag

    return make


def grid_fields(spec, shifts, t, pupils, work, squares=False):
    plain, crossed, fields, *stages = work
    count, grid, lanes = fields.shape
    box_len = t["row_fwd"].shape[1] // 6
    if spec is not None:
        plain[...] = spec
        crossed[...] = swap(spec)
    sign = lane_sign(box_len, lanes, -1.0)

    def first(c, stage):
        rows = []
        for i in range(CHUNK):
            s = c * CHUNK + i
            at = pl.ds(shifts[1, s] + MAX_SHIFT, box_len)
            real, imag = pupils(s)
            high, low = split(real * plain[at, :] + imag * crossed[at, :])
            rows.append(jnp.concatenate([high, low], 1))
        stage[...] = halves(dot(jnp.concatenate(rows, 0), t["lane_fwd"][...]))

    def second(c, stage, power):
        for base in range(0, CHUNK, GROUP):
            stacks = []
            for i in range(base, base + GROUP):
                part = stage[i * box_len : (i + 1) * box_len, :]
                high, low = split(jnp.concatenate([part, sign * swap(part)], 0))
                stacks.append(jnp.concatenate([high, low, high], 0))
            out = dot(t["row_fwd"][...], jnp.concatenate(stacks, 1))
            for i in range(GROUP):
                field = out[:, i * lanes : (i + 1) * lanes]
                square = field * field
                fields[c * CHUNK + base + i] = square if squares else field
                power = power + square
        return power

    return skewed(count, stages, first, second, jnp.zeros((grid, lanes), f32))


def grid_misfit(power, inv_dose, target, t):
    high, low = split(power)
    mid = halves(dot(jnp.concatenate([high, low], 1), t["mix_cols"][...]))
    high, low = split(mid)
    lit = dot(t["mix_rows"][...], jnp.concatenate([high, low, high], 0))
    return lit * inv_dose - target


def gather_back(misfit, shifts, scale, t, pr, pi, fields, stages, sums):
    count, box_len, lanes = pr.shape
    grid = lanes // 2
    for ref in sums:
        ref[...] = jnp.zeros_like(ref)
    sign = lane_sign(box_len, lanes, 1.0)

    def first(c, stage):
        for base in range(0, CHUNK, GROUP):
            stacks = []
            for i in range(base, base + GROUP):
                high, low = split(fields[c * CHUNK + i] * misfit)
                stacks.append(jnp.concatenate([high, low, high], 0))
            both = dot(t["row_back"][...], jnp.concatenate(stacks, 1))
            for i in range(GROUP):
                part = both[:, i * lanes : (i + 1) * lanes]
                at = (base + i) * box_len
                stage[at : at + box_len, :] = part[:box_len] + sign * swap(part[box_len:])

    def second(c, stage, carry):
        high, low = split(stage[...])
        hits = halves(dot(jnp.concatenate([high, low], 1), t["lane_back"][...]))
        for i in range(CHUNK):
            s = c * CHUNK + i
            rows = pl.ds(shifts[1, s] + MAX_SHIFT, box_len)
            hit = hits[i * box_len : (i + 1) * box_len]
            one, two = sums[2 * (i % 2)], sums[2 * (i % 2) + 1]
            one[rows, :] += pr[s] * hit
            two[rows, :] += pi[s] * hit
        return carry

    skewed(count, stages, first, second, 0)
    whole, turned = sums[0], sums[1]
    whole[...] = (whole[...] + sums[2][...] + swap(turned[...] + sums[3][...])) * scale
    middle = grid // 2
    turned[0:1, :] = jnp.zeros((1, lanes), f32)
    for a in range(1, middle):
        turned[a : a + 1, :] = whole[middle - a : middle - a + 1, :]
    ahead, behind = whole[middle:, :], turned[:middle, :]
    return jnp.concatenate([ahead + behind, ahead - behind], 0)


def tile_of(k, tile):
    return lax.bitwise_xor(tile, jnp.int32(k))


def fill_windows(backs, t, tile, tiles, wins):
    half = backs[0].shape[0] // 2
    tile_len = wins.shape[2]
    stacks = []
    for rows in (slice(0, half), slice(half, 2 * half)):
        parts = []
        for back in backs:
            high, low = split(back[rows, :])
            parts.append(jnp.concatenate([high, low, high], 1))
        stacks.append(jnp.concatenate(parts, 0))
    even = dot(stacks[0], t["grad_cols"][:, :tile_len])
    odd = dot(stacks[1], t["grad_cols"][:, tile_len:])
    wins[0, MARGIN + tile_len :, :] = jnp.zeros((MARGIN, tile_len), f32)
    wins[tiles + 1, :MARGIN, :] = jnp.zeros((MARGIN, tile_len), f32)
    for k in range(tiles):
        at = slice(k * half, (k + 1) * half)
        high, low = split(jnp.concatenate([even[at], odd[at]], 0))
        out = dot(t["grad_rows"][...], jnp.concatenate([high, low, high], 0))
        wins[tile_of(k, tile) + 1] = out


def pieces(tile_len):
    return (
        (0, MARGIN, 0, tile_len),
        (MARGIN, tile_len - MARGIN, 1, 0),
        (tile_len - MARGIN, tile_len, 2, -tile_len),
    )


def piece_total(own, piece, wins):
    low, high, near, shift = piece
    total = wins[own + 1, MARGIN + low : MARGIN + high, :]
    if near != 1:
        at = MARGIN + low + shift
        total = total + wins[own + near, at : at + MARGIN, :]
    return total


def squares_of(grad):
    return jnp.sum((grad * grad).reshape(-1, 8, grad.shape[1]), axis=0)


def step_rate(square, tiles):
    tile_len = square.shape[1]
    total = jnp.sum(jnp.sum(square, axis=0, keepdims=True), axis=1, keepdims=True)
    return MASK_RATE / jnp.sqrt(total / (tiles * tile_len * tile_len) + TINY_EPS)


def slope_of(params):
    lean = half_tanh(params)
    return 1.0 - lean * lean


def near_tiles(tile, tiles):
    prev, follow = jnp.maximum(tile - 1, 0), jnp.minimum(tile + 1, tiles - 1)
    return prev, follow, (tile > 0).astype(f32), (tile < tiles - 1).astype(f32)


def edge_params(tile, mate, cross):
    odd = lax.rem(tile, 2) > 0
    before = jnp.where(odd, mate[-MARGIN:, :], cross[...])
    after = jnp.where(odd, cross[...], mate[:MARGIN, :])
    return before, after


def mask_window(near, has_prev, has_next):
    rows = near.shape[0]
    return jnp.concatenate(
        [
            sigmoid(near[:MARGIN, :]) * has_prev,
            sigmoid(near[MARGIN : rows - MARGIN, :]),
            sigmoid(near[rows - MARGIN :, :]) * has_next,
        ],
        0,
    )


def start_all(pairs, sems):
    copies = [pltpu.make_async_copy(a, b, sems.at[i]) for i, (a, b) in enumerate(pairs)]
    for copy in copies:
        copy.start()
    return copies


def head_kernel(out):
    out[...] = jnp.zeros_like(out)


def pack_kernel(tile, place, head, weights, shifts, mask, packed, edge):
    at = pl.multiple_of(lax.rem(tile[0], 2) * (mask.shape[0] - MARGIN), MARGIN)
    edge[...] = mask[pl.ds(at, MARGIN), :]
    local = weights.shape[1]
    packed[...] = head[...]
    packed[0:1, :local] = weights[...]
    packed[1:3, :local] = shifts[...].astype(f32)
    packed[3:4, :local] = jnp.sqrt(weights[...])
    packed[...] = pltpu.roll(packed[...], place[0] * local, 1)


def target_terms(target, t):
    rows, cols = t["target_rows"], t["target_cols"]
    grid = rows.shape[0] // 2
    high, low = split(target)
    both = dot(rows[...], high)
    mid = both[:grid] + both[grid:] + dot(rows[:grid, :], low)
    high, low = split(mid)
    return halves(dot(high, cols[...])) + dot(low, cols[:, : 2 * grid])


def doses(info, scale):
    dose = jnp.sum(info[0:1, :], axis=1, keepdims=True)
    return 1.0 / dose, scale / dose


def ready_kernel(spots, tiles, tile, table, pupil, goal, own, mate, cross,
                 plain, crossed, target, turned_re, turned_im, slopes, near):
    t = {n: table.at[spot] for n, spot in spots.items()}
    here = tile[0]
    tile_len = own.shape[0]
    _, _, has_prev, has_next = near_tiles(here, tiles)
    before, after = edge_params(here, mate, cross)
    near[:MARGIN, :] = before
    near[MARGIN : MARGIN + tile_len, :] = own[...]
    near[MARGIN + tile_len :, :] = after
    turn_pupils(pupil, turned_re, turned_im)
    spec = window_spectrum(mask_window(near, has_prev, has_next), t)
    plain[...] = spec
    crossed[...] = swap(spec)
    target[...] = target_terms(goal[...], t)
    slopes[0] = slope_of(own[...])
    slopes[1] = slope_of(mate[...])


def first_kernel(spots, peers, scale, table, plain, crossed, target, turned_re, turned_im, *refs):
    parts = refs[:peers]
    t = {n: table.at[spot] for n, spot in spots.items()}
    back, pr, pi, info, whole = refs[peers : peers + 5]
    *work, s0, s1, s2, s3, shifts, roots, sems = refs[peers + 5 :]
    total = parts[0][...]
    for part in parts[1:]:
        total = total + part[...]
    info[...] = total
    whole[...] = total.astype(jnp.int32)
    for copy in start_all(((whole, shifts), (info, roots)), sems):
        copy.wait()
    pupils = placed_pupils(shifts, roots, turned_re, turned_im, pr, pi)
    work = [plain, crossed, *work]
    power = grid_fields(None, shifts, t, pupils, work)
    inv_dose, factor = doses(total, scale)
    misfit = grid_misfit(power, inv_dose, target[...], t)
    sums = (s0, s1, s2, s3)
    back[...] = gather_back(misfit, shifts, factor, t, pr, pi, work[2], work[3:], sums)


def next_kernel(spots, tiles, scale, tile, table, shifts, info, pr, pi, target, near, slopes, *refs):
    params, backs = refs[: tiles - 2], refs[tiles - 2 : 2 * tiles - 2]
    t = {n: table.at[spot] for n, spot in spots.items()}
    new, grads, rates, back, *work, s0, s1, s2, s3, wins = refs[2 * tiles - 2 :]
    here = tile[0]
    tile_len = wins.shape[2]
    fill_windows(backs, t, here, tiles, wins)
    square = jnp.zeros((8, tile_len), f32)
    for k in range(tiles):
        own = tile_of(k, here)
        for piece in pieces(tile_len):
            low, high = piece[:2]
            slope = slopes[k, low:high, :] if k < 2 else slope_of(params[k - 2][low:high, :])
            grad = piece_total(own, piece, wins) * slope
            grads[own, low:high, :] = grad
            square = square + squares_of(grad)
    rate = step_rate(square, tiles)
    rates[...] = jnp.broadcast_to(rate, rates.shape)
    prev, follow, has_prev, has_next = near_tiles(here, tiles)
    inner = slice(MARGIN, MARGIN + tile_len)
    new[:MARGIN, :] = near[:MARGIN, :] - grads[prev, tile_len - MARGIN :, :] * rate
    new[inner, :] = near[inner, :] - grads[here] * rate
    new[MARGIN + tile_len :, :] = near[MARGIN + tile_len :, :] - grads[follow, :MARGIN, :] * rate
    spec = window_spectrum(mask_window(new, has_prev, has_next), t)
    power = grid_fields(spec, shifts, t, lambda s: (pr[s], pi[s]), work)
    inv_dose, factor = doses(info[...], scale)
    misfit = grid_misfit(power, inv_dose, target[...], t)
    sums = (s0, s1, s2, s3)
    back[...] = gather_back(misfit, shifts, factor, t, pr, pi, work[2], work[3:], sums)


def slope_kernel(tiles, tile, grads, rates, *refs):
    params, slopes = refs[:tiles], refs[tiles]
    rate = rates[0:1, 0:1]
    for k in range(tiles):
        own = tile_of(k, tile[0])
        slopes[own] = slope_of(params[k][...] - grads[own] * rate)


def last_kernel(spots, tiles, tile, table, shifts, info, pr, pi, target, near, slopes, *refs):
    backs = refs[:tiles]
    t = {n: table.at[spot] for n, spot in spots.items()}
    final, row, *work, terms, wins, fresh, sems = refs[tiles:]
    fields = work[2]
    here = tile[0]
    tile_len = wins.shape[2]
    fill_windows(backs, t, here, tiles, wins)

    def grad_of(own, piece):
        return piece_total(own, piece, wins) * slopes[own, piece[0] : piece[1], :]

    square = jnp.zeros((8, tile_len), f32)
    for own in range(tiles):
        for piece in pieces(tile_len):
            square = square + squares_of(grad_of(own, piece))
    rate = step_rate(square, tiles)
    prev, follow, has_prev, has_next = near_tiles(here, tiles)
    first, *_, end = pieces(tile_len)
    fresh[:MARGIN, :] = near[:MARGIN, :] - grad_of(prev, end) * rate
    for piece in pieces(tile_len):
        at = slice(MARGIN + piece[0], MARGIN + piece[1])
        fresh[at, :] = near[at, :] - grad_of(here, piece) * rate
    fresh[MARGIN + tile_len :, :] = near[MARGIN + tile_len :, :] - grad_of(follow, first) * rate
    (leave,) = start_all(((fresh.at[pl.ds(MARGIN, tile_len), :], final),), sems)
    spec = window_spectrum(mask_window(fresh, has_prev, has_next), t)
    power = grid_fields(
        spec, shifts, t, lambda s: (pr[s], pi[s]), work, squares=True
    )
    inv_dose, _ = doses(info[...], 1.0)
    misfit = grid_misfit(power, inv_dose, target[...], t)

    def chunk(c, carry):
        rows = []
        for i in range(CHUNK):
            rows.append(jnp.sum(fields[c * CHUNK + i] * misfit, axis=0, keepdims=True))
        terms[pl.ds(pl.multiple_of(c * CHUNK, CHUNK), CHUNK), :] = jnp.concatenate(rows, 0)
        return carry

    count = fields.shape[0]
    lax.fori_loop(0, count // CHUNK, chunk, 0)
    high, low = split(terms[...])
    left = terms[...] - high.astype(f32) - low.astype(f32)
    ones = jnp.ones((8, terms.shape[1]), bf16)
    total = jnp.zeros((8, terms.shape[0]), f32)
    for part in (left.astype(bf16), low, high):
        total = total + lax.dot_general(
            ones, part, (((1,), (1,)), ((), ())), preferred_element_type=f32
        )
    row[...] = total
    leave.wait()


def weight_kernel(tiles, scale, tile, place, info, *refs):
    rows = refs[:tiles]
    out, stack = refs[tiles:]
    count = rows[0].shape[1]
    for k in range(tiles):
        stack[k] = rows[k][...]
    here = tile[0]
    total = stack[here]
    for k in range(1, tiles):
        total = total + stack[tile_of(k, here)]
    summed = total[0:1] * scale
    weight = info[0:1, :count]
    dose = jnp.sum(weight, axis=1, keepdims=True)
    mean = jnp.sum(summed, axis=1, keepdims=True) / dose
    grad = (summed / weight - mean) / dose
    spread = jnp.sqrt(jnp.sum(grad * grad, axis=1, keepdims=True) / count + TINY_EPS)
    new = weight * jnp.exp(-WEIGHT_RATE * grad / spread)
    size = out.shape[1]
    lanes = info.shape[1]
    if count < lanes:
        new = jnp.concatenate([new, jnp.zeros((1, lanes - count), f32)], 1)
    new = pltpu.roll(jnp.broadcast_to(new, (8, lanes)), lanes - place[0] * size, 1)
    out[...] = new[0:1, :size]


def crossed(value, axis, k):
    return lax.ppermute(value, axis, [(i, i ^ k) for i in range(lax.axis_size(axis))])


def all_of(value, axis):
    return [value] + [crossed(value, axis, k) for k in range(1, lax.axis_size(axis))]


def per_device(mask_param, target_image, source_weights, source_shifts, pupil_map):
    tile_len = mask_param.shape[1]
    box_len = pupil_map.shape[1]
    grid = box_len + 2 * MAX_SHIFT
    lanes = 2 * grid
    tiles = lax.axis_size("tile")
    peers = lax.axis_size("src")
    local = source_weights.shape[0]
    count = local * peers
    assert tiles & (tiles - 1) == 0 and peers & (peers - 1) == 0 and count <= 128 and count % CHUNK == 0
    tables = make_tables(tile_len, box_len, MAX_SHIFT)

    tile = lax.axis_index("tile").astype(jnp.int32).reshape(1)
    place = lax.axis_index("src").astype(jnp.int32).reshape(1)

    vmem = pl.BlockSpec(memory_space=pltpu.VMEM)
    smem = pl.BlockSpec(memory_space=pltpu.SMEM)
    left = pl.BlockSpec(memory_space=pltpu.HBM)
    params_of = pltpu.CompilerParams(vmem_limit_bytes=32 << 20)

    def struct(*shape, kind=f32):
        return jax.ShapeDtypeStruct(shape, kind)

    def cost(flops):
        return pl.CostEstimate(flops=flops, bytes_accessed=1 << 20, transcendentals=0)

    head = pl.pallas_call(
        head_kernel,
        out_shape=struct(8, 128),
        out_specs=vmem,
        compiler_params=params_of,
        cost_estimate=cost(1 << 34),
        name="head_step",
    )()
    packed, edge = pl.pallas_call(
        pack_kernel,
        out_shape=[struct(8, 128), struct(MARGIN, tile_len)],
        in_specs=[smem, smem] + [vmem] * 4,
        out_specs=[vmem] * 2,
        compiler_params=params_of,
        cost_estimate=cost(1 << 20),
        name="pack_sources",
    )(tile, place, head, source_weights[None], source_shifts.T, mask_param)
    packed = all_of(packed, "src")

    pairs = [(i, (i + 1) % tiles) for i in range(1, tiles, 2)]
    cross = lax.ppermute(edge, "tile", pairs + [(j, i) for i, j in pairs])
    mate = crossed(mask_param, "tile", 1)
    far = [crossed(mask_param, "tile", k) for k in range(2, tiles, 2)]

    whole, spots = pack_tables(tables)
    table = jnp.asarray(whole)
    work = [
        pltpu.VMEM((grid, lanes), f32),
        pltpu.VMEM((grid, lanes), f32),
        pltpu.VMEM((count, grid, lanes), f32),
        pltpu.VMEM((CHUNK * box_len, lanes), f32),
        pltpu.VMEM((CHUNK * box_len, lanes), f32),
    ]
    hold = [pltpu.VMEM((grid, lanes), f32)] * 4
    period = tile_len + 2 * MARGIN
    steps = [pltpu.VMEM((tiles + 2, period, tile_len), f32)]
    scale = 0.5 / (grid * grid * period * tile_len)
    source_len = struct(count, box_len, lanes)

    plain, crossed_spec, target, *turned, slopes, near = pl.pallas_call(
        functools.partial(ready_kernel, spots, tiles),
        out_shape=[struct(grid, lanes)] * 3
        + [struct(2 * MAX_SHIFT + 1, box_len, lanes)] * 2
        + [struct(2, tile_len, tile_len), struct(period, tile_len)],
        in_specs=[smem] + [vmem] * 6,
        out_specs=[vmem] * 7,
        compiler_params=params_of,
        cost_estimate=cost(1 << 30),
        name="ready_step",
    )(tile, table, pupil_map, target_image, mask_param, mate, cross)

    back, pr, pi, info, whole = pl.pallas_call(
        functools.partial(first_kernel, spots, peers, scale),
        out_shape=[struct(grid, lanes), source_len, source_len, struct(8, 128),
                   struct(8, 128, kind=jnp.int32)],
        in_specs=[vmem] * (6 + peers),
        out_specs=[vmem] * 5,
        scratch_shapes=work[2:] + hold + [
            pltpu.SMEM((8, 128), jnp.int32),
            pltpu.SMEM((8, 128), f32),
            pltpu.SemaphoreType.DMA((2,)),
        ],
        compiler_params=params_of,
        cost_estimate=cost(1 << 32),
        name="first_step",
    )(table, plain, crossed_spec, target, *turned, *packed)

    shared = (tile, table, whole, info, pr, pi, target)
    shared_specs = [smem, vmem, smem] + [vmem] * 4

    back, far = lax.optimization_barrier((back, far))
    backs = all_of(back, "tile")
    entries = [mask_param, mate]
    for one in far:
        entries += [one, crossed(one, "tile", 1)]
    near, grads, rates, back = pl.pallas_call(
        functools.partial(next_kernel, spots, tiles, scale),
        out_shape=[struct(period, tile_len), struct(tiles, tile_len, tile_len),
                   struct(8, 128), struct(grid, lanes)],
        in_specs=shared_specs + [vmem] * (2 * tiles),
        out_specs=[vmem] * 4,
        scratch_shapes=work + hold + steps,
        compiler_params=params_of,
        cost_estimate=cost(1 << 32),
        name="next_step",
    )(*shared, near, slopes, *entries[2:], *backs)

    backs = all_of(back, "tile")
    slopes = pl.pallas_call(
        functools.partial(slope_kernel, tiles),
        out_shape=struct(tiles, tile_len, tile_len),
        in_specs=[smem] + [vmem] * (2 + tiles),
        out_specs=vmem,
        compiler_params=params_of,
        cost_estimate=cost(1 << 28),
        name="slope_step",
    )(tile, grads, rates, *entries)
    final, row = pl.pallas_call(
        functools.partial(last_kernel, spots, tiles),
        out_shape=[struct(tile_len, tile_len), struct(8, count)],
        in_specs=shared_specs + [vmem] * (2 + tiles),
        out_specs=[left, vmem],
        scratch_shapes=work + [pltpu.VMEM((count, lanes), f32)] + steps + [
            pltpu.VMEM((period, tile_len), f32),
            pltpu.SemaphoreType.DMA((1,)),
        ],
        compiler_params=params_of,
        cost_estimate=cost(1 << 32),
        name="last_step",
    )(*shared, near, slopes, *backs)

    rows = all_of(row, "tile")
    out = pl.pallas_call(
        functools.partial(weight_kernel, tiles, 1.0 / (grid * grid)),
        out_shape=struct(1, local),
        in_specs=[smem] * 2 + [vmem] * (1 + tiles),
        out_specs=vmem,
        scratch_shapes=[pltpu.VMEM((tiles, 8, count), f32)],
        compiler_params=params_of,
        name="weight_step",
    )(tile, place, info, *rows)
    return final, out.reshape(local)


def solution(mesh):
    in_specs = (
        P(("group", "tile"), None),
        P(("group", "tile"), None),
        P(("group", "src")),
        P("src", None),
        P(),
    )
    out_specs = (P(("group", "tile"), None), P(("group", "src")))
    return jax.shard_map(
        per_device, mesh=mesh, in_specs=in_specs, out_specs=out_specs, check_vma=False
    )
```

```python
import functools
import math

import jax
import jax.numpy as jnp
import ml_dtypes
import numpy as np
from jax import lax
from jax.experimental import pallas as pl
from jax.experimental.pallas import tpu as pltpu
from jax.sharding import PartitionSpec as P


MARGIN = 64
MAX_SHIFT = 16
MASK_RATE = 0.5
WEIGHT_RATE = 0.3
TINY_EPS = 1e-06
CHUNK = 16
GROUP = 2


bf16 = jnp.bfloat16
f32 = jnp.float32


def np_split(table):
    table = np.asarray(table, np.float64)
    high = table.astype(np.float32).astype(ml_dtypes.bfloat16)
    low = (table - high.astype(np.float64)).astype(np.float32).astype(ml_dtypes.bfloat16)
    return high, low


def phases(freqs, pixels, period):
    return 2.0 * math.pi * np.mod(np.outer(freqs, pixels), period) / period


def make_tables(tile_len, box_len, max_shift):
    period = tile_len + 2 * MARGIN
    grid = box_len + 2 * max_shift
    wide = np.arange(grid) - grid // 2
    pix = np.arange(tile_len)
    full = np.arange(period)
    points = np.arange(grid)
    box = np.arange(box_len)
    out = {}
    ang = phases(wide, pix, period)
    high, low = np_split(np.concatenate([np.cos(ang), -np.sin(ang)], 0).T / (period * tile_len))
    out["spec_cols"] = np.concatenate([high, low], 1)
    ang_rows = phases(wide, full, period)
    high, low = np_split(np.concatenate([np.cos(ang_rows), np.sin(ang_rows)], 0))
    out["spec_rows"] = np.concatenate([high, low], 0)
    ang = phases(points, points, grid)
    cos, sin = np.cos(ang), np.sin(ang)
    for name, table in (
        ("lane_fwd", np.block([[cos, sin], [-sin, cos]])),
        ("lane_back", np.block([[cos, -sin], [sin, cos]])),
    ):
        high, low = np_split(table)
        out[name] = np.block([[high, low], [high, np.zeros_like(low)]])
    ang = phases(points, box, grid)
    high, low = np_split(np.concatenate([np.cos(ang), np.sin(ang)], 1))
    out["row_fwd"] = np.concatenate([high, high, low], 1)
    high, low = np_split(np.concatenate([np.cos(ang).T, np.sin(ang).T], 0))
    out["row_back"] = np.concatenate([high, high, low], 1)

    def dirichlet(offset):
        theta = 2.0 * math.pi * ((pix + offset)[None, :] / period - points[:, None] / grid)
        orders = np.arange(1, box_len)
        return 1.0 + 2.0 * np.cos(orders[:, None, None] * theta[None]).sum(0)

    rows, cols = dirichlet(MARGIN), dirichlet(0)
    high, low = np_split(rows @ rows.T / grid)
    out["mix_rows"] = np.concatenate([high, high, low], 1)
    mix = cols @ cols.T / grid
    high, low = np_split(np.block([[mix, mix], [mix, mix]]))
    out["mix_cols"] = np.block([[high, low], [high, np.zeros_like(low)]])
    high, low = np_split(rows)
    out["target_rows"] = np.concatenate([high, low], 0)
    high, low = np_split(np.concatenate([cols, cols], 0).T)
    out["target_cols"] = np.concatenate([high, low], 1)
    ang = phases(wide, pix, period)
    cos, sin = np.cos(ang), np.sin(ang)
    high, low = np_split(np.block([[cos, -sin], [-sin, -cos]]))
    out["grad_cols"] = np.concatenate([high, high, low], 0)
    ang = phases(full, np.arange(grid // 2), period)
    high, low = np_split(np.concatenate([np.cos(ang), np.sin(ang)], 1))
    out["grad_rows"] = np.concatenate([high, high, low], 1)
    return out


def pack_tables(tables):
    wide = [n for n in tables if tables[n].shape[1] > 256]
    narrow = sorted((n for n in tables if n not in wide), key=lambda n: -tables[n].shape[0])
    place, heights = {}, [0, 0]
    for n in wide:
        place[n] = (heights[0], 0)
        heights = [heights[0] + tables[n].shape[0]] * 2
    for n in narrow:
        side = int(heights[1] < heights[0])
        place[n] = (heights[side], 256 * side)
        heights[side] += tables[n].shape[0]
    whole = np.zeros((max(heights), 512), ml_dtypes.bfloat16)
    spots = {}
    for n, (row, col) in place.items():
        rows, cols = tables[n].shape
        whole[row : row + rows, col : col + cols] = tables[n]
        spots[n] = (slice(row, row + rows), slice(col, col + cols))
    return whole, spots


def split(value):
    high = value.astype(bf16)
    return high, (value - high.astype(f32)).astype(bf16)


def dot(left, right):
    return jnp.dot(left, right, preferred_element_type=f32)


def halves(value):
    width = value.shape[1] // 2
    return value[:, :width] + value[:, width:]


def lane_sign(rows, lanes, first):
    lane = lax.broadcasted_iota(jnp.int32, (rows, lanes), 1)
    return jnp.where(lane < lanes // 2, first, -first).astype(f32)


def swap(value):
    return pltpu.roll(value, value.shape[1] // 2, 1)


def half_tanh(value):
    return jnp.tanh(0.5 * value)


def sigmoid(value):
    return 0.5 * half_tanh(value) + 0.5


def window_spectrum(window, t):
    grid = t["spec_cols"].shape[1] // 4
    high, low = split(window)
    cols = t["spec_cols"]
    mid = halves(dot(high, cols[...])) + dot(low, cols[:, : 2 * grid])
    mid_high, mid_low = split(mid)
    rows = t["spec_rows"]
    both = halves(dot(rows[: 2 * grid, :], jnp.concatenate([mid_high, mid_low], 1)))
    both = both + dot(rows[2 * grid :, :], mid_high)
    return both[:grid] + lane_sign(grid, 2 * grid, 1.0) * swap(both[grid:])


def skewed(count, stages, first, second, carry):
    chunks = count // CHUNK
    first(0, stages[0])
    for c in range(1, chunks):
        first(c, stages[c % 2])
        carry = second(c - 1, stages[(c - 1) % 2], carry)
    return second(chunks - 1, stages[(chunks - 1) % 2], carry)


def turn_pupils(pupil, turned_re, turned_im):
    count, size, lanes = turned_re.shape
    grid = lanes // 2
    turned_re[0] = jnp.zeros((size, lanes), f32)
    turned_im[0] = jnp.zeros((size, lanes), f32)
    turned_re[0, :, :size] = pupil[0]
    turned_re[0, :, grid : grid + size] = pupil[0]
    turned_im[0, :, :size] = -pupil[1]
    turned_im[0, :, grid : grid + size] = pupil[1]
    real, imag = turned_re[0], turned_im[0]
    for by in range(1, count):
        turned_re[by] = pltpu.roll(real, by, 1)
        turned_im[by] = pltpu.roll(imag, by, 1)


def placed_pupils(shifts, roots, turned_re, turned_im, pr, pi):
    def make(s):
        by = shifts[2, s] + MAX_SHIFT
        real, imag = turned_re[by] * roots[3, s], turned_im[by] * roots[3, s]
        pr[s], pi[s] = real, imag
        return real, imag

    return make


def grid_fields(spec, shifts, t, pupils, work, squares=False):
    plain, crossed, fields, *stages = work
    count, grid, lanes = fields.shape
    box_len = t["row_fwd"].shape[1] // 6
    if spec is not None:
        plain[...] = spec
        crossed[...] = swap(spec)
    sign = lane_sign(box_len, lanes, -1.0)

    def first(c, stage):
        rows = []
        for i in range(CHUNK):
            s = c * CHUNK + i
            at = pl.ds(shifts[1, s] + MAX_SHIFT, box_len)
            real, imag = pupils(s)
            high, low = split(real * plain[at, :] + imag * crossed[at, :])
            rows.append(jnp.concatenate([high, low], 1))
        stage[...] = halves(dot(jnp.concatenate(rows, 0), t["lane_fwd"][...]))

    def second(c, stage, power):
        for base in range(0, CHUNK, GROUP):
            stacks = []
            for i in range(base, base + GROUP):
                part = stage[i * box_len : (i + 1) * box_len, :]
                high, low = split(jnp.concatenate([part, sign * swap(part)], 0))
                stacks.append(jnp.concatenate([high, low, high], 0))
            out = dot(t["row_fwd"][...], jnp.concatenate(stacks, 1))
            for i in range(GROUP):
                field = out[:, i * lanes : (i + 1) * lanes]
                square = field * field
                fields[c * CHUNK + base + i] = square if squares else field
                power = power + square
        return power

    return skewed(count, stages, first, second, jnp.zeros((grid, lanes), f32))


def grid_misfit(power, inv_dose, target, t):
    high, low = split(power)
    mid = halves(dot(jnp.concatenate([high, low], 1), t["mix_cols"][...]))
    high, low = split(mid)
    lit = dot(t["mix_rows"][...], jnp.concatenate([high, low, high], 0))
    return lit * inv_dose - target


def gather_back(misfit, shifts, scale, t, pr, pi, fields, stages, sums):
    count, box_len, lanes = pr.shape
    grid = lanes // 2
    for ref in sums:
        ref[...] = jnp.zeros_like(ref)
    sign = lane_sign(box_len, lanes, 1.0)

    def first(c, stage):
        for base in range(0, CHUNK, GROUP):
            stacks = []
            for i in range(base, base + GROUP):
                high, low = split(fields[c * CHUNK + i] * misfit)
                stacks.append(jnp.concatenate([high, low, high], 0))
            both = dot(t["row_back"][...], jnp.concatenate(stacks, 1))
            for i in range(GROUP):
                part = both[:, i * lanes : (i + 1) * lanes]
                at = (base + i) * box_len
                stage[at : at + box_len, :] = part[:box_len] + sign * swap(part[box_len:])

    def second(c, stage, carry):
        high, low = split(stage[...])
        hits = halves(dot(jnp.concatenate([high, low], 1), t["lane_back"][...]))
        for i in range(CHUNK):
            s = c * CHUNK + i
            rows = pl.ds(shifts[1, s] + MAX_SHIFT, box_len)
            hit = hits[i * box_len : (i + 1) * box_len]
            one, two = sums[2 * (i % 2)], sums[2 * (i % 2) + 1]
            one[rows, :] += pr[s] * hit
            two[rows, :] += pi[s] * hit
        return carry

    skewed(count, stages, first, second, 0)
    whole, turned = sums[0], sums[1]
    whole[...] = (whole[...] + sums[2][...] + swap(turned[...] + sums[3][...])) * scale
    middle = grid // 2
    turned[0:1, :] = jnp.zeros((1, lanes), f32)
    for a in range(1, middle):
        turned[a : a + 1, :] = whole[middle - a : middle - a + 1, :]
    ahead, behind = whole[middle:, :], turned[:middle, :]
    return jnp.concatenate([ahead + behind, ahead - behind], 0)


def tile_of(k, tile):
    return lax.bitwise_xor(tile, jnp.int32(k))


def fill_windows(backs, t, tile, tiles, wins):
    half = backs[0].shape[0] // 2
    tile_len = wins.shape[2]
    stacks = []
    for rows in (slice(0, half), slice(half, 2 * half)):
        parts = []
        for back in backs:
            high, low = split(back[rows, :])
            parts.append(jnp.concatenate([high, low, high], 1))
        stacks.append(jnp.concatenate(parts, 0))
    even = dot(stacks[0], t["grad_cols"][:, :tile_len])
    odd = dot(stacks[1], t["grad_cols"][:, tile_len:])
    wins[0, MARGIN + tile_len :, :] = jnp.zeros((MARGIN, tile_len), f32)
    wins[tiles + 1, :MARGIN, :] = jnp.zeros((MARGIN, tile_len), f32)
    for k in range(tiles):
        at = slice(k * half, (k + 1) * half)
        high, low = split(jnp.concatenate([even[at], odd[at]], 0))
        out = dot(t["grad_rows"][...], jnp.concatenate([high, low, high], 0))
        wins[tile_of(k, tile) + 1] = out


def pieces(tile_len):
    return (
        (0, MARGIN, 0, tile_len),
        (MARGIN, tile_len - MARGIN, 1, 0),
        (tile_len - MARGIN, tile_len, 2, -tile_len),
    )


def piece_total(own, piece, wins):
    low, high, near, shift = piece
    total = wins[own + 1, MARGIN + low : MARGIN + high, :]
    if near != 1:
        at = MARGIN + low + shift
        total = total + wins[own + near, at : at + MARGIN, :]
    return total


def squares_of(grad):
    return jnp.sum((grad * grad).reshape(-1, 8, grad.shape[1]), axis=0)


def step_rate(square, tiles):
    tile_len = square.shape[1]
    total = jnp.sum(jnp.sum(square, axis=0, keepdims=True), axis=1, keepdims=True)
    return MASK_RATE / jnp.sqrt(total / (tiles * tile_len * tile_len) + TINY_EPS)


def slope_of(params):
    lean = half_tanh(params)
    return 1.0 - lean * lean


def near_tiles(tile, tiles):
    prev, follow = jnp.maximum(tile - 1, 0), jnp.minimum(tile + 1, tiles - 1)
    return prev, follow, (tile > 0).astype(f32), (tile < tiles - 1).astype(f32)


def edge_params(tile, mate, cross):
    odd = lax.rem(tile, 2) > 0
    before = jnp.where(odd, mate[-MARGIN:, :], cross[...])
    after = jnp.where(odd, cross[...], mate[:MARGIN, :])
    return before, after


def mask_window(near, has_prev, has_next):
    rows = near.shape[0]
    return jnp.concatenate(
        [
            sigmoid(near[:MARGIN, :]) * has_prev,
            sigmoid(near[MARGIN : rows - MARGIN, :]),
            sigmoid(near[rows - MARGIN :, :]) * has_next,
        ],
        0,
    )


def start_all(pairs, sems):
    copies = [pltpu.make_async_copy(a, b, sems.at[i]) for i, (a, b) in enumerate(pairs)]
    for copy in copies:
        copy.start()
    return copies


def head_kernel(out):
    out[...] = jnp.zeros_like(out)


def pack_kernel(tile, place, head, weights, shifts, mask, packed, edge):
    at = pl.multiple_of(lax.rem(tile[0], 2) * (mask.shape[0] - MARGIN), MARGIN)
    edge[...] = mask[pl.ds(at, MARGIN), :]
    local = weights.shape[1]
    packed[...] = head[...]
    packed[0:1, :local] = weights[...]
    packed[1:3, :local] = shifts[...].astype(f32)
    packed[3:4, :local] = jnp.sqrt(weights[...])
    packed[...] = pltpu.roll(packed[...], place[0] * local, 1)


def target_terms(target, t):
    rows, cols = t["target_rows"], t["target_cols"]
    grid = rows.shape[0] // 2
    high, low = split(target)
    both = dot(rows[...], high)
    mid = both[:grid] + both[grid:] + dot(rows[:grid, :], low)
    high, low = split(mid)
    return halves(dot(high, cols[...])) + dot(low, cols[:, : 2 * grid])


def doses(info, scale):
    dose = jnp.sum(info[0:1, :], axis=1, keepdims=True)
    return 1.0 / dose, scale / dose


def ready_kernel(spots, tiles, tile, table, pupil, goal, own, mate, cross,
                 plain, crossed, target, turned_re, turned_im, slopes, near):
    t = {n: table.at[spot] for n, spot in spots.items()}
    here = tile[0]
    tile_len = own.shape[0]
    _, _, has_prev, has_next = near_tiles(here, tiles)
    before, after = edge_params(here, mate, cross)
    near[:MARGIN, :] = before
    near[MARGIN : MARGIN + tile_len, :] = own[...]
    near[MARGIN + tile_len :, :] = after
    turn_pupils(pupil, turned_re, turned_im)
    spec = window_spectrum(mask_window(near, has_prev, has_next), t)
    plain[...] = spec
    crossed[...] = swap(spec)
    target[...] = target_terms(goal[...], t)
    slopes[0] = slope_of(own[...])
    slopes[1] = slope_of(mate[...])


def first_kernel(spots, peers, scale, table, plain, crossed, target, turned_re, turned_im, *refs):
    parts = refs[:peers]
    t = {n: table.at[spot] for n, spot in spots.items()}
    back, pr, pi, info, whole = refs[peers : peers + 5]
    *work, s0, s1, s2, s3, shifts, roots, sems = refs[peers + 5 :]
    total = parts[0][...]
    for part in parts[1:]:
        total = total + part[...]
    info[...] = total
    whole[...] = total.astype(jnp.int32)
    for copy in start_all(((whole, shifts), (info, roots)), sems):
        copy.wait()
    pupils = placed_pupils(shifts, roots, turned_re, turned_im, pr, pi)
    work = [plain, crossed, *work]
    power = grid_fields(None, shifts, t, pupils, work)
    inv_dose, factor = doses(total, scale)
    misfit = grid_misfit(power, inv_dose, target[...], t)
    sums = (s0, s1, s2, s3)
    back[...] = gather_back(misfit, shifts, factor, t, pr, pi, work[2], work[3:], sums)


def next_kernel(spots, tiles, scale, tile, table, shifts, info, pr, pi, target, near, slopes, *refs):
    params, backs = refs[: tiles - 2], refs[tiles - 2 : 2 * tiles - 2]
    t = {n: table.at[spot] for n, spot in spots.items()}
    new, grads, rates, back, *work, s0, s1, s2, s3, wins = refs[2 * tiles - 2 :]
    here = tile[0]
    tile_len = wins.shape[2]
    fill_windows(backs, t, here, tiles, wins)
    square = jnp.zeros((8, tile_len), f32)
    for k in range(tiles):
        own = tile_of(k, here)
        for piece in pieces(tile_len):
            low, high = piece[:2]
            slope = slopes[k, low:high, :] if k < 2 else slope_of(params[k - 2][low:high, :])
            grad = piece_total(own, piece, wins) * slope
            grads[own, low:high, :] = grad
            square = square + squares_of(grad)
    rate = step_rate(square, tiles)
    rates[...] = jnp.broadcast_to(rate, rates.shape)
    prev, follow, has_prev, has_next = near_tiles(here, tiles)
    inner = slice(MARGIN, MARGIN + tile_len)
    new[:MARGIN, :] = near[:MARGIN, :] - grads[prev, tile_len - MARGIN :, :] * rate
    new[inner, :] = near[inner, :] - grads[here] * rate
    new[MARGIN + tile_len :, :] = near[MARGIN + tile_len :, :] - grads[follow, :MARGIN, :] * rate
    spec = window_spectrum(mask_window(new, has_prev, has_next), t)
    power = grid_fields(spec, shifts, t, lambda s: (pr[s], pi[s]), work)
    inv_dose, factor = doses(info[...], scale)
    misfit = grid_misfit(power, inv_dose, target[...], t)
    sums = (s0, s1, s2, s3)
    back[...] = gather_back(misfit, shifts, factor, t, pr, pi, work[2], work[3:], sums)


def slope_kernel(tiles, tile, grads, rates, *refs):
    params, slopes = refs[:tiles], refs[tiles]
    rate = rates[0:1, 0:1]
    for k in range(tiles):
        own = tile_of(k, tile[0])
        slopes[own] = slope_of(params[k][...] - grads[own] * rate)


def last_kernel(spots, tiles, tile, table, shifts, info, pr, pi, target, near, slopes, *refs):
    backs = refs[:tiles]
    t = {n: table.at[spot] for n, spot in spots.items()}
    final, row, *work, terms, wins, fresh, sems = refs[tiles:]
    fields = work[2]
    here = tile[0]
    tile_len = wins.shape[2]
    fill_windows(backs, t, here, tiles, wins)

    def grad_of(own, piece):
        return piece_total(own, piece, wins) * slopes[own, piece[0] : piece[1], :]

    square = jnp.zeros((8, tile_len), f32)
    for own in range(tiles):
        for piece in pieces(tile_len):
            square = square + squares_of(grad_of(own, piece))
    rate = step_rate(square, tiles)
    prev, follow, has_prev, has_next = near_tiles(here, tiles)
    first, *_, end = pieces(tile_len)
    fresh[:MARGIN, :] = near[:MARGIN, :] - grad_of(prev, end) * rate
    for piece in pieces(tile_len):
        at = slice(MARGIN + piece[0], MARGIN + piece[1])
        fresh[at, :] = near[at, :] - grad_of(here, piece) * rate
    fresh[MARGIN + tile_len :, :] = near[MARGIN + tile_len :, :] - grad_of(follow, first) * rate
    (leave,) = start_all(((fresh.at[pl.ds(MARGIN, tile_len), :], final),), sems)
    spec = window_spectrum(mask_window(fresh, has_prev, has_next), t)
    power = grid_fields(
        spec, shifts, t, lambda s: (pr[s], pi[s]), work, squares=True
    )
    inv_dose, _ = doses(info[...], 1.0)
    misfit = grid_misfit(power, inv_dose, target[...], t)

    def chunk(c, carry):
        rows = []
        for i in range(CHUNK):
            rows.append(jnp.sum(fields[c * CHUNK + i] * misfit, axis=0, keepdims=True))
        terms[pl.ds(pl.multiple_of(c * CHUNK, CHUNK), CHUNK), :] = jnp.concatenate(rows, 0)
        return carry

    count = fields.shape[0]
    lax.fori_loop(0, count // CHUNK, chunk, 0)
    high, low = split(terms[...])
    left = terms[...] - high.astype(f32) - low.astype(f32)
    ones = jnp.ones((8, terms.shape[1]), bf16)
    total = jnp.zeros((8, terms.shape[0]), f32)
    for part in (left.astype(bf16), low, high):
        total = total + lax.dot_general(
            ones, part, (((1,), (1,)), ((), ())), preferred_element_type=f32
        )
    row[...] = total
    leave.wait()


def weight_kernel(tiles, scale, tile, place, info, *refs):
    rows = refs[:tiles]
    out, stack = refs[tiles:]
    count = rows[0].shape[1]
    for k in range(tiles):
        stack[k] = rows[k][...]
    here = tile[0]
    total = stack[here]
    for k in range(1, tiles):
        total = total + stack[tile_of(k, here)]
    summed = total[0:1] * scale
    weight = info[0:1, :count]
    dose = jnp.sum(weight, axis=1, keepdims=True)
    mean = jnp.sum(summed, axis=1, keepdims=True) / dose
    grad = (summed / weight - mean) / dose
    spread = jnp.sqrt(jnp.sum(grad * grad, axis=1, keepdims=True) / count + TINY_EPS)
    new = weight * jnp.exp(-WEIGHT_RATE * grad / spread)
    size = out.shape[1]
    lanes = info.shape[1]
    if count < lanes:
        new = jnp.concatenate([new, jnp.zeros((1, lanes - count), f32)], 1)
    new = pltpu.roll(jnp.broadcast_to(new, (8, lanes)), lanes - place[0] * size, 1)
    out[...] = new[0:1, :size]


def crossed(value, axis, k):
    return lax.ppermute(value, axis, [(i, i ^ k) for i in range(lax.axis_size(axis))])


def all_of(value, axis):
    got = [value]
    for k in range(1, lax.axis_size(axis)):
        got.append(crossed(value, axis, k))
    return got


def per_device(mask_param, target_image, source_weights, source_shifts, pupil_map):
    tile_len = mask_param.shape[1]
    box_len = pupil_map.shape[1]
    grid = box_len + 2 * MAX_SHIFT
    lanes = 2 * grid
    tiles = lax.axis_size("tile")
    peers = lax.axis_size("src")
    local = source_weights.shape[0]
    count = local * peers
    assert tiles & (tiles - 1) == 0 and peers & (peers - 1) == 0 and count <= 128 and count % CHUNK == 0
    tables = make_tables(tile_len, box_len, MAX_SHIFT)

    tile = lax.axis_index("tile").astype(jnp.int32).reshape(1)
    place = lax.axis_index("src").astype(jnp.int32).reshape(1)

    vmem = pl.BlockSpec(memory_space=pltpu.VMEM)
    smem = pl.BlockSpec(memory_space=pltpu.SMEM)
    left = pl.BlockSpec(memory_space=pltpu.HBM)
    params_of = pltpu.CompilerParams(vmem_limit_bytes=32 << 20)

    def struct(*shape, kind=f32):
        return jax.ShapeDtypeStruct(shape, kind)

    def cost(flops):
        return pl.CostEstimate(flops=flops, bytes_accessed=1 << 20, transcendentals=0)

    head = pl.pallas_call(
        head_kernel,
        out_shape=struct(8, 128),
        out_specs=vmem,
        compiler_params=params_of,
        cost_estimate=cost(1 << 34),
        name="head_step",
    )()
    packed, edge = pl.pallas_call(
        pack_kernel,
        out_shape=[struct(8, 128), struct(MARGIN, tile_len)],
        in_specs=[smem, smem] + [vmem] * 4,
        out_specs=[vmem] * 2,
        compiler_params=params_of,
        cost_estimate=cost(1 << 20),
        name="pack_sources",
    )(tile, place, head, source_weights[None], source_shifts.T, mask_param)
    packed = all_of(packed, "src")

    pairs = [(i, (i + 1) % tiles) for i in range(1, tiles, 2)]
    cross = lax.ppermute(edge, "tile", pairs + [(j, i) for i, j in pairs])
    mate = crossed(mask_param, "tile", 1)
    far = [crossed(mask_param, "tile", k) for k in range(2, tiles, 2)]

    whole, spots = pack_tables(tables)
    table = jnp.asarray(whole)
    work = [
        pltpu.VMEM((grid, lanes), f32),
        pltpu.VMEM((grid, lanes), f32),
        pltpu.VMEM((count, grid, lanes), f32),
        pltpu.VMEM((CHUNK * box_len, lanes), f32),
        pltpu.VMEM((CHUNK * box_len, lanes), f32),
    ]
    hold = [pltpu.VMEM((grid, lanes), f32)] * 4
    period = tile_len + 2 * MARGIN
    steps = [pltpu.VMEM((tiles + 2, period, tile_len), f32)]
    scale = 0.5 / (grid * grid * period * tile_len)
    source_len = struct(count, box_len, lanes)

    plain, crossed_spec, target, *turned, slopes, near = pl.pallas_call(
        functools.partial(ready_kernel, spots, tiles),
        out_shape=[struct(grid, lanes)] * 3
        + [struct(2 * MAX_SHIFT + 1, box_len, lanes)] * 2
        + [struct(2, tile_len, tile_len), struct(period, tile_len)],
        in_specs=[smem] + [vmem] * 6,
        out_specs=[vmem] * 7,
        compiler_params=params_of,
        cost_estimate=cost(1 << 30),
        name="ready_step",
    )(tile, table, pupil_map, target_image, mask_param, mate, cross)

    back, pr, pi, info, whole = pl.pallas_call(
        functools.partial(first_kernel, spots, peers, scale),
        out_shape=[struct(grid, lanes), source_len, source_len, struct(8, 128),
                   struct(8, 128, kind=jnp.int32)],
        in_specs=[vmem] * (6 + peers),
        out_specs=[vmem] * 5,
        scratch_shapes=work[2:] + hold + [
            pltpu.SMEM((8, 128), jnp.int32),
            pltpu.SMEM((8, 128), f32),
            pltpu.SemaphoreType.DMA((2,)),
        ],
        compiler_params=params_of,
        cost_estimate=cost(1 << 32),
        name="first_step",
    )(table, plain, crossed_spec, target, *turned, *packed)

    shared = (tile, table, whole, info, pr, pi, target)
    shared_specs = [smem, vmem, smem] + [vmem] * 4

    back, far = lax.optimization_barrier((back, far))
    backs = all_of(back, "tile")
    entries = [mask_param, mate]
    for one in far:
        entries += [one, crossed(one, "tile", 1)]
    near, grads, rates, back = pl.pallas_call(
        functools.partial(next_kernel, spots, tiles, scale),
        out_shape=[struct(period, tile_len), struct(tiles, tile_len, tile_len),
                   struct(8, 128), struct(grid, lanes)],
        in_specs=shared_specs + [vmem] * (2 * tiles),
        out_specs=[vmem] * 4,
        scratch_shapes=work + hold + steps,
        compiler_params=params_of,
        cost_estimate=cost(1 << 32),
        name="next_step",
    )(*shared, near, slopes, *entries[2:], *backs)

    backs = all_of(back, "tile")
    slopes = pl.pallas_call(
        functools.partial(slope_kernel, tiles),
        out_shape=struct(tiles, tile_len, tile_len),
        in_specs=[smem] + [vmem] * (2 + tiles),
        out_specs=vmem,
        compiler_params=params_of,
        cost_estimate=cost(1 << 28),
        name="slope_step",
    )(tile, grads, rates, *entries)
    final, row = pl.pallas_call(
        functools.partial(last_kernel, spots, tiles),
        out_shape=[struct(tile_len, tile_len), struct(8, count)],
        in_specs=shared_specs + [vmem] * (2 + tiles),
        out_specs=[left, vmem],
        scratch_shapes=work + [pltpu.VMEM((count, lanes), f32)] + steps + [
            pltpu.VMEM((period, tile_len), f32),
            pltpu.SemaphoreType.DMA((1,)),
        ],
        compiler_params=params_of,
        cost_estimate=cost(1 << 32),
        name="last_step",
    )(*shared, near, slopes, *backs)

    rows = all_of(row, "tile")
    out = pl.pallas_call(
        functools.partial(weight_kernel, tiles, 1.0 / (grid * grid)),
        out_shape=struct(1, local),
        in_specs=[smem] * 2 + [vmem] * (1 + tiles),
        out_specs=vmem,
        scratch_shapes=[pltpu.VMEM((tiles, 8, count), f32)],
        compiler_params=params_of,
        name="weight_step",
    )(tile, place, info, *rows)
    return final, out.reshape(local)


def solution(mesh):
    in_specs = (
        P(("group", "tile"), None),
        P(("group", "tile"), None),
        P(("group", "src")),
        P("src", None),
        P(),
    )
    out_specs = (P(("group", "tile"), None), P(("group", "src")))
    return jax.shard_map(
        per_device, mesh=mesh, in_specs=in_specs, out_specs=out_specs, check_vma=False
    )
```

```python
import functools
import math

import jax
import jax.numpy as jnp
import ml_dtypes
import numpy as np
from jax import lax
from jax.experimental import pallas as pl
from jax.experimental.pallas import tpu as pltpu
from jax.sharding import PartitionSpec as P


MARGIN = 64
MAX_SHIFT = 16
MASK_RATE = 0.5
WEIGHT_RATE = 0.3
TINY_EPS = 1e-06
CHUNK = 16
GROUP = 2


bf16 = jnp.bfloat16
f32 = jnp.float32


def np_split(table):
    table = np.asarray(table, np.float64)
    high = table.astype(np.float32).astype(ml_dtypes.bfloat16)
    low = (table - high.astype(np.float64)).astype(np.float32).astype(ml_dtypes.bfloat16)
    return high, low


def phases(freqs, pixels, period):
    return 2.0 * math.pi * np.mod(np.outer(freqs, pixels), period) / period


def make_tables(tile_len, box_len, max_shift):
    period = tile_len + 2 * MARGIN
    grid = box_len + 2 * max_shift
    wide = np.arange(grid) - grid // 2
    pix = np.arange(tile_len)
    full = np.arange(period)
    points = np.arange(grid)
    box = np.arange(box_len)
    out = {}
    ang = phases(wide, pix, period)
    high, low = np_split(np.concatenate([np.cos(ang), -np.sin(ang)], 0).T / (period * tile_len))
    out["spec_cols"] = np.concatenate([high, low], 1)
    ang_rows = phases(wide, full, period)
    high, low = np_split(np.concatenate([np.cos(ang_rows), np.sin(ang_rows)], 0))
    out["spec_rows"] = np.concatenate([high, low], 0)
    ang = phases(points, points, grid)
    cos, sin = np.cos(ang), np.sin(ang)
    for name, table in (
        ("lane_fwd", np.block([[cos, sin], [-sin, cos]])),
        ("lane_back", np.block([[cos, -sin], [sin, cos]])),
    ):
        high, low = np_split(table)
        out[name] = np.block([[high, low], [high, np.zeros_like(low)]])
    ang = phases(points, box, grid)
    high, low = np_split(np.concatenate([np.cos(ang), np.sin(ang)], 1))
    out["row_fwd"] = np.concatenate([high, high, low], 1)
    high, low = np_split(np.concatenate([np.cos(ang).T, np.sin(ang).T], 0))
    out["row_back"] = np.concatenate([high, high, low], 1)

    def dirichlet(offset):
        theta = 2.0 * math.pi * ((pix + offset)[None, :] / period - points[:, None] / grid)
        orders = np.arange(1, box_len)
        return 1.0 + 2.0 * np.cos(orders[:, None, None] * theta[None]).sum(0)

    rows, cols = dirichlet(MARGIN), dirichlet(0)
    high, low = np_split(rows @ rows.T / grid)
    out["mix_rows"] = np.concatenate([high, high, low], 1)
    mix = cols @ cols.T / grid
    high, low = np_split(np.block([[mix, mix], [mix, mix]]))
    out["mix_cols"] = np.block([[high, low], [high, np.zeros_like(low)]])
    high, low = np_split(rows)
    out["target_rows"] = np.concatenate([high, low], 0)
    high, low = np_split(np.concatenate([cols, cols], 0).T)
    out["target_cols"] = np.concatenate([high, low], 1)
    ang = phases(wide, pix, period)
    cos, sin = np.cos(ang), np.sin(ang)
    high, low = np_split(np.block([[cos, -sin], [-sin, -cos]]))
    out["grad_cols"] = np.concatenate([high, high, low], 0)
    ang = phases(full, np.arange(grid // 2), period)
    high, low = np_split(np.concatenate([np.cos(ang), np.sin(ang)], 1))
    out["grad_rows"] = np.concatenate([high, high, low], 1)
    return out


def pack_tables(tables):
    wide = [n for n in tables if tables[n].shape[1] > 256]
    narrow = sorted((n for n in tables if n not in wide), key=lambda n: -tables[n].shape[0])
    place, heights = {}, [0, 0]
    for n in wide:
        place[n] = (heights[0], 0)
        heights = [heights[0] + tables[n].shape[0]] * 2
    for n in narrow:
        side = int(heights[1] < heights[0])
        place[n] = (heights[side], 256 * side)
        heights[side] += tables[n].shape[0]
    whole = np.zeros((max(heights), 512), ml_dtypes.bfloat16)
    spots = {}
    for n, (row, col) in place.items():
        rows, cols = tables[n].shape
        whole[row : row + rows, col : col + cols] = tables[n]
        spots[n] = (slice(row, row + rows), slice(col, col + cols))
    return whole, spots


def split(value):
    high = value.astype(bf16)
    return high, (value - high.astype(f32)).astype(bf16)


def dot(left, right):
    return jnp.dot(left, right, preferred_element_type=f32)


def halves(value):
    width = value.shape[1] // 2
    return value[:, :width] + value[:, width:]


def lane_sign(rows, lanes, first):
    lane = lax.broadcasted_iota(jnp.int32, (rows, lanes), 1)
    return jnp.where(lane < lanes // 2, first, -first).astype(f32)


def swap(value):
    return pltpu.roll(value, value.shape[1] // 2, 1)


def half_tanh(value):
    return jnp.tanh(0.5 * value)


def sigmoid(value):
    return 0.5 * half_tanh(value) + 0.5


def window_spectrum(window, t):
    grid = t["spec_cols"].shape[1] // 4
    high, low = split(window)
    cols = t["spec_cols"]
    mid = halves(dot(high, cols[...])) + dot(low, cols[:, : 2 * grid])
    mid_high, mid_low = split(mid)
    rows = t["spec_rows"]
    both = halves(dot(rows[: 2 * grid, :], jnp.concatenate([mid_high, mid_low], 1)))
    both = both + dot(rows[2 * grid :, :], mid_high)
    return both[:grid] + lane_sign(grid, 2 * grid, 1.0) * swap(both[grid:])


def skewed(count, stages, first, second, carry):
    chunks = count // CHUNK
    first(0, stages[0])
    for c in range(1, chunks):
        first(c, stages[c % 2])
        carry = second(c - 1, stages[(c - 1) % 2], carry)
    return second(chunks - 1, stages[(chunks - 1) % 2], carry)


def turn_pupils(pupil, turned_re, turned_im):
    count, size, lanes = turned_re.shape
    grid = lanes // 2
    turned_re[0] = jnp.zeros((size, lanes), f32)
    turned_im[0] = jnp.zeros((size, lanes), f32)
    turned_re[0, :, :size] = pupil[0]
    turned_re[0, :, grid : grid + size] = pupil[0]
    turned_im[0, :, :size] = -pupil[1]
    turned_im[0, :, grid : grid + size] = pupil[1]
    real, imag = turned_re[0], turned_im[0]
    for by in range(1, count):
        turned_re[by] = pltpu.roll(real, by, 1)
        turned_im[by] = pltpu.roll(imag, by, 1)


def placed_pupils(shifts, roots, turned_re, turned_im, pr, pi):
    def make(s):
        by = shifts[2, s] + MAX_SHIFT
        real, imag = turned_re[by] * roots[3, s], turned_im[by] * roots[3, s]
        pr[s], pi[s] = real, imag
        return real, imag

    return make


def grid_fields(spec, shifts, t, pupils, work, squares=False):
    plain, crossed, fields, *stages = work
    count, grid, lanes = fields.shape
    box_len = t["row_fwd"].shape[1] // 6
    if spec is not None:
        plain[...] = spec
        crossed[...] = swap(spec)
    sign = lane_sign(box_len, lanes, -1.0)

    def first(c, stage):
        rows = []
        for i in range(CHUNK):
            s = c * CHUNK + i
            at = pl.ds(shifts[1, s] + MAX_SHIFT, box_len)
            real, imag = pupils(s)
            high, low = split(real * plain[at, :] + imag * crossed[at, :])
            rows.append(jnp.concatenate([high, low], 1))
        stage[...] = halves(dot(jnp.concatenate(rows, 0), t["lane_fwd"][...]))

    def second(c, stage, power):
        for base in range(0, CHUNK, GROUP):
            stacks = []
            for i in range(base, base + GROUP):
                part = stage[i * box_len : (i + 1) * box_len, :]
                high, low = split(jnp.concatenate([part, sign * swap(part)], 0))
                stacks.append(jnp.concatenate([high, low, high], 0))
            out = dot(t["row_fwd"][...], jnp.concatenate(stacks, 1))
            for i in range(GROUP):
                field = out[:, i * lanes : (i + 1) * lanes]
                square = field * field
                fields[c * CHUNK + base + i] = square if squares else field
                power = power + square
        return power

    return skewed(count, stages, first, second, jnp.zeros((grid, lanes), f32))


def grid_misfit(power, inv_dose, target, t):
    high, low = split(power)
    mid = halves(dot(jnp.concatenate([high, low], 1), t["mix_cols"][...]))
    high, low = split(mid)
    lit = dot(t["mix_rows"][...], jnp.concatenate([high, low, high], 0))
    return lit * inv_dose - target


def gather_back(misfit, shifts, scale, t, pr, pi, fields, stages, sums):
    count, box_len, lanes = pr.shape
    grid = lanes // 2
    for ref in sums:
        ref[...] = jnp.zeros_like(ref)
    sign = lane_sign(box_len, lanes, 1.0)

    def first(c, stage):
        for base in range(0, CHUNK, GROUP):
            stacks = []
            for i in range(base, base + GROUP):
                high, low = split(fields[c * CHUNK + i] * misfit)
                stacks.append(jnp.concatenate([high, low, high], 0))
            both = dot(t["row_back"][...], jnp.concatenate(stacks, 1))
            for i in range(GROUP):
                part = both[:, i * lanes : (i + 1) * lanes]
                at = (base + i) * box_len
                stage[at : at + box_len, :] = part[:box_len] + sign * swap(part[box_len:])

    def second(c, stage, carry):
        high, low = split(stage[...])
        hits = halves(dot(jnp.concatenate([high, low], 1), t["lane_back"][...]))
        for i in range(CHUNK):
            s = c * CHUNK + i
            rows = pl.ds(shifts[1, s] + MAX_SHIFT, box_len)
            hit = hits[i * box_len : (i + 1) * box_len]
            one, two = sums[2 * (i % 2)], sums[2 * (i % 2) + 1]
            one[rows, :] += pr[s] * hit
            two[rows, :] += pi[s] * hit
        return carry

    skewed(count, stages, first, second, 0)
    whole, turned = sums[0], sums[1]
    whole[...] = (whole[...] + sums[2][...] + swap(turned[...] + sums[3][...])) * scale
    middle = grid // 2
    turned[0:1, :] = jnp.zeros((1, lanes), f32)
    for a in range(1, middle):
        turned[a : a + 1, :] = whole[middle - a : middle - a + 1, :]
    ahead, behind = whole[middle:, :], turned[:middle, :]
    return jnp.concatenate([ahead + behind, ahead - behind], 0)


def tile_of(k, tile):
    return lax.bitwise_xor(tile, jnp.int32(k))


def fill_windows(backs, t, tile, tiles, wins):
    half = backs[0].shape[0] // 2
    tile_len = wins.shape[2]
    stacks = []
    for rows in (slice(0, half), slice(half, 2 * half)):
        parts = []
        for back in backs:
            high, low = split(back[rows, :])
            parts.append(jnp.concatenate([high, low, high], 1))
        stacks.append(jnp.concatenate(parts, 0))
    even = dot(stacks[0], t["grad_cols"][:, :tile_len])
    odd = dot(stacks[1], t["grad_cols"][:, tile_len:])
    wins[0, MARGIN + tile_len :, :] = jnp.zeros((MARGIN, tile_len), f32)
    wins[tiles + 1, :MARGIN, :] = jnp.zeros((MARGIN, tile_len), f32)
    for k in range(tiles):
        at = slice(k * half, (k + 1) * half)
        high, low = split(jnp.concatenate([even[at], odd[at]], 0))
        out = dot(t["grad_rows"][...], jnp.concatenate([high, low, high], 0))
        wins[tile_of(k, tile) + 1] = out


def pieces(tile_len):
    return (
        (0, MARGIN, 0, tile_len),
        (MARGIN, tile_len - MARGIN, 1, 0),
        (tile_len - MARGIN, tile_len, 2, -tile_len),
    )


def piece_total(own, piece, wins):
    low, high, near, shift = piece
    total = wins[own + 1, MARGIN + low : MARGIN + high, :]
    if near != 1:
        at = MARGIN + low + shift
        total = total + wins[own + near, at : at + MARGIN, :]
    return total


def squares_of(grad):
    return jnp.sum((grad * grad).reshape(-1, 8, grad.shape[1]), axis=0)


def step_rate(square, tiles):
    tile_len = square.shape[1]
    total = jnp.sum(jnp.sum(square, axis=0, keepdims=True), axis=1, keepdims=True)
    return MASK_RATE / jnp.sqrt(total / (tiles * tile_len * tile_len) + TINY_EPS)


def slope_of(params):
    lean = half_tanh(params)
    return 1.0 - lean * lean


def near_tiles(tile, tiles):
    prev, follow = jnp.maximum(tile - 1, 0), jnp.minimum(tile + 1, tiles - 1)
    return prev, follow, (tile > 0).astype(f32), (tile < tiles - 1).astype(f32)


def edge_params(tile, mate, cross):
    odd = lax.rem(tile, 2) > 0
    before = jnp.where(odd, mate[-MARGIN:, :], cross[...])
    after = jnp.where(odd, cross[...], mate[:MARGIN, :])
    return before, after


def mask_window(near, has_prev, has_next):
    rows = near.shape[0]
    return jnp.concatenate(
        [
            sigmoid(near[:MARGIN, :]) * has_prev,
            sigmoid(near[MARGIN : rows - MARGIN, :]),
            sigmoid(near[rows - MARGIN :, :]) * has_next,
        ],
        0,
    )


def start_all(pairs, sems):
    copies = [pltpu.make_async_copy(a, b, sems.at[i]) for i, (a, b) in enumerate(pairs)]
    for copy in copies:
        copy.start()
    return copies


def head_kernel(out):
    out[...] = jnp.zeros_like(out)


def mark_kernel(value, out):
    out[...] = value[...]


def pack_kernel(tile, place, head, weights, shifts, mask, packed, edge):
    at = pl.multiple_of(lax.rem(tile[0], 2) * (mask.shape[0] - MARGIN), MARGIN)
    edge[...] = mask[pl.ds(at, MARGIN), :]
    local = weights.shape[1]
    packed[...] = head[...]
    packed[0:1, :local] = weights[...]
    packed[1:3, :local] = shifts[...].astype(f32)
    packed[3:4, :local] = jnp.sqrt(weights[...])
    packed[...] = pltpu.roll(packed[...], place[0] * local, 1)


def target_terms(target, t):
    rows, cols = t["target_rows"], t["target_cols"]
    grid = rows.shape[0] // 2
    high, low = split(target)
    both = dot(rows[...], high)
    mid = both[:grid] + both[grid:] + dot(rows[:grid, :], low)
    high, low = split(mid)
    return halves(dot(high, cols[...])) + dot(low, cols[:, : 2 * grid])


def doses(info, scale):
    dose = jnp.sum(info[0:1, :], axis=1, keepdims=True)
    return 1.0 / dose, scale / dose


def ready_kernel(spots, tiles, tile, table, pupil, goal, own, mate, cross,
                 plain, crossed, target, turned_re, turned_im, slopes, near):
    t = {n: table.at[spot] for n, spot in spots.items()}
    here = tile[0]
    tile_len = own.shape[0]
    _, _, has_prev, has_next = near_tiles(here, tiles)
    before, after = edge_params(here, mate, cross)
    near[:MARGIN, :] = before
    near[MARGIN : MARGIN + tile_len, :] = own[...]
    near[MARGIN + tile_len :, :] = after
    turn_pupils(pupil, turned_re, turned_im)
    spec = window_spectrum(mask_window(near, has_prev, has_next), t)
    plain[...] = spec
    crossed[...] = swap(spec)
    target[...] = target_terms(goal[...], t)
    slopes[0] = slope_of(own[...])
    slopes[1] = slope_of(mate[...])


def first_kernel(spots, peers, scale, table, plain, crossed, target, turned_re, turned_im, *refs):
    parts = refs[:peers]
    t = {n: table.at[spot] for n, spot in spots.items()}
    back, pr, pi, info, whole = refs[peers : peers + 5]
    *work, s0, s1, s2, s3, shifts, roots, sems = refs[peers + 5 :]
    total = parts[0][...]
    for part in parts[1:]:
        total = total + part[...]
    info[...] = total
    whole[...] = total.astype(jnp.int32)
    for copy in start_all(((whole, shifts), (info, roots)), sems):
        copy.wait()
    pupils = placed_pupils(shifts, roots, turned_re, turned_im, pr, pi)
    work = [plain, crossed, *work]
    power = grid_fields(None, shifts, t, pupils, work)
    inv_dose, factor = doses(total, scale)
    misfit = grid_misfit(power, inv_dose, target[...], t)
    sums = (s0, s1, s2, s3)
    back[...] = gather_back(misfit, shifts, factor, t, pr, pi, work[2], work[3:], sums)


def next_kernel(spots, tiles, scale, tile, table, shifts, info, pr, pi, target, near, slopes, *refs):
    params, backs = refs[: tiles - 2], refs[tiles - 2 : 2 * tiles - 2]
    t = {n: table.at[spot] for n, spot in spots.items()}
    new, grads, rates, back, *work, s0, s1, s2, s3, wins = refs[2 * tiles - 2 :]
    here = tile[0]
    tile_len = wins.shape[2]
    fill_windows(backs, t, here, tiles, wins)
    square = jnp.zeros((8, tile_len), f32)
    for k in range(tiles):
        own = tile_of(k, here)
        for piece in pieces(tile_len):
            low, high = piece[:2]
            slope = slopes[k, low:high, :] if k < 2 else slope_of(params[k - 2][low:high, :])
            grad = piece_total(own, piece, wins) * slope
            grads[own, low:high, :] = grad
            square = square + squares_of(grad)
    rate = step_rate(square, tiles)
    rates[...] = jnp.broadcast_to(rate, rates.shape)
    prev, follow, has_prev, has_next = near_tiles(here, tiles)
    inner = slice(MARGIN, MARGIN + tile_len)
    new[:MARGIN, :] = near[:MARGIN, :] - grads[prev, tile_len - MARGIN :, :] * rate
    new[inner, :] = near[inner, :] - grads[here] * rate
    new[MARGIN + tile_len :, :] = near[MARGIN + tile_len :, :] - grads[follow, :MARGIN, :] * rate
    spec = window_spectrum(mask_window(new, has_prev, has_next), t)
    power = grid_fields(spec, shifts, t, lambda s: (pr[s], pi[s]), work)
    inv_dose, factor = doses(info[...], scale)
    misfit = grid_misfit(power, inv_dose, target[...], t)
    sums = (s0, s1, s2, s3)
    back[...] = gather_back(misfit, shifts, factor, t, pr, pi, work[2], work[3:], sums)


def slope_kernel(tiles, tile, grads, rates, *refs):
    params, slopes = refs[:tiles], refs[tiles]
    rate = rates[0:1, 0:1]
    for k in range(tiles):
        own = tile_of(k, tile[0])
        slopes[own] = slope_of(params[k][...] - grads[own] * rate)


def last_kernel(spots, tiles, tile, table, shifts, info, pr, pi, target, near, slopes, *refs):
    backs = refs[:tiles]
    t = {n: table.at[spot] for n, spot in spots.items()}
    final, row, *work, terms, wins, fresh, sems = refs[tiles:]
    fields = work[2]
    here = tile[0]
    tile_len = wins.shape[2]
    fill_windows(backs, t, here, tiles, wins)

    def grad_of(own, piece):
        return piece_total(own, piece, wins) * slopes[own, piece[0] : piece[1], :]

    square = jnp.zeros((8, tile_len), f32)
    for own in range(tiles):
        for piece in pieces(tile_len):
            square = square + squares_of(grad_of(own, piece))
    rate = step_rate(square, tiles)
    prev, follow, has_prev, has_next = near_tiles(here, tiles)
    first, *_, end = pieces(tile_len)
    fresh[:MARGIN, :] = near[:MARGIN, :] - grad_of(prev, end) * rate
    for piece in pieces(tile_len):
        at = slice(MARGIN + piece[0], MARGIN + piece[1])
        fresh[at, :] = near[at, :] - grad_of(here, piece) * rate
    fresh[MARGIN + tile_len :, :] = near[MARGIN + tile_len :, :] - grad_of(follow, first) * rate
    (leave,) = start_all(((fresh.at[pl.ds(MARGIN, tile_len), :], final),), sems)
    spec = window_spectrum(mask_window(fresh, has_prev, has_next), t)
    power = grid_fields(
        spec, shifts, t, lambda s: (pr[s], pi[s]), work, squares=True
    )
    inv_dose, _ = doses(info[...], 1.0)
    misfit = grid_misfit(power, inv_dose, target[...], t)

    def chunk(c, carry):
        rows = []
        for i in range(CHUNK):
            rows.append(jnp.sum(fields[c * CHUNK + i] * misfit, axis=0, keepdims=True))
        terms[pl.ds(pl.multiple_of(c * CHUNK, CHUNK), CHUNK), :] = jnp.concatenate(rows, 0)
        return carry

    count = fields.shape[0]
    lax.fori_loop(0, count // CHUNK, chunk, 0)
    high, low = split(terms[...])
    left = terms[...] - high.astype(f32) - low.astype(f32)
    ones = jnp.ones((8, terms.shape[1]), bf16)
    total = jnp.zeros((8, terms.shape[0]), f32)
    for part in (left.astype(bf16), low, high):
        total = total + lax.dot_general(
            ones, part, (((1,), (1,)), ((), ())), preferred_element_type=f32
        )
    row[...] = total
    leave.wait()


def weight_kernel(tiles, scale, tile, place, info, *refs):
    rows = refs[:tiles]
    out, stack = refs[tiles:]
    count = rows[0].shape[1]
    for k in range(tiles):
        stack[k] = rows[k][...]
    here = tile[0]
    total = stack[here]
    for k in range(1, tiles):
        total = total + stack[tile_of(k, here)]
    summed = total[0:1] * scale
    weight = info[0:1, :count]
    dose = jnp.sum(weight, axis=1, keepdims=True)
    mean = jnp.sum(summed, axis=1, keepdims=True) / dose
    grad = (summed / weight - mean) / dose
    spread = jnp.sqrt(jnp.sum(grad * grad, axis=1, keepdims=True) / count + TINY_EPS)
    new = weight * jnp.exp(-WEIGHT_RATE * grad / spread)
    size = out.shape[1]
    lanes = info.shape[1]
    if count < lanes:
        new = jnp.concatenate([new, jnp.zeros((1, lanes - count), f32)], 1)
    new = pltpu.roll(jnp.broadcast_to(new, (8, lanes)), lanes - place[0] * size, 1)
    out[...] = new[0:1, :size]


def crossed(value, axis, k):
    return lax.ppermute(value, axis, [(i, i ^ k) for i in range(lax.axis_size(axis))])


def all_of(value, axis):
    got = [value]
    for k in range(1, lax.axis_size(axis)):
        got.append(crossed(value, axis, k))
    return got


def per_device(mask_param, target_image, source_weights, source_shifts, pupil_map):
    tile_len = mask_param.shape[1]
    box_len = pupil_map.shape[1]
    grid = box_len + 2 * MAX_SHIFT
    lanes = 2 * grid
    tiles = lax.axis_size("tile")
    peers = lax.axis_size("src")
    local = source_weights.shape[0]
    count = local * peers
    assert tiles & (tiles - 1) == 0 and peers & (peers - 1) == 0 and count <= 128 and count % CHUNK == 0
    tables = make_tables(tile_len, box_len, MAX_SHIFT)

    tile = lax.axis_index("tile").astype(jnp.int32).reshape(1)
    place = lax.axis_index("src").astype(jnp.int32).reshape(1)

    vmem = pl.BlockSpec(memory_space=pltpu.VMEM)
    smem = pl.BlockSpec(memory_space=pltpu.SMEM)
    left = pl.BlockSpec(memory_space=pltpu.HBM)
    params_of = pltpu.CompilerParams(vmem_limit_bytes=32 << 20)

    def struct(*shape, kind=f32):
        return jax.ShapeDtypeStruct(shape, kind)

    def cost(flops):
        return pl.CostEstimate(flops=flops, bytes_accessed=1 << 20, transcendentals=0)

    head = pl.pallas_call(
        head_kernel,
        out_shape=struct(8, 128),
        out_specs=vmem,
        compiler_params=params_of,
        cost_estimate=cost(1 << 34),
        name="head_step",
    )()
    packed, edge = pl.pallas_call(
        pack_kernel,
        out_shape=[struct(8, 128), struct(MARGIN, tile_len)],
        in_specs=[smem, smem] + [vmem] * 4,
        out_specs=[vmem] * 2,
        compiler_params=params_of,
        cost_estimate=cost(1 << 20),
        name="pack_sources",
    )(tile, place, head, source_weights[None], source_shifts.T, mask_param)
    packed = all_of(packed, "src")

    pairs = [(i, (i + 1) % tiles) for i in range(1, tiles, 2)]
    cross = lax.ppermute(edge, "tile", pairs + [(j, i) for i, j in pairs])
    mate = crossed(mask_param, "tile", 1)
    far = [crossed(mask_param, "tile", k) for k in range(2, tiles, 2)]

    whole, spots = pack_tables(tables)
    table = jnp.asarray(whole)
    work = [
        pltpu.VMEM((grid, lanes), f32),
        pltpu.VMEM((grid, lanes), f32),
        pltpu.VMEM((count, grid, lanes), f32),
        pltpu.VMEM((CHUNK * box_len, lanes), f32),
        pltpu.VMEM((CHUNK * box_len, lanes), f32),
    ]
    hold = [pltpu.VMEM((grid, lanes), f32)] * 4
    period = tile_len + 2 * MARGIN
    steps = [pltpu.VMEM((tiles + 2, period, tile_len), f32)]
    scale = 0.5 / (grid * grid * period * tile_len)
    source_len = struct(count, box_len, lanes)

    plain, crossed_spec, target, *turned, slopes, near = pl.pallas_call(
        functools.partial(ready_kernel, spots, tiles),
        out_shape=[struct(grid, lanes)] * 3
        + [struct(2 * MAX_SHIFT + 1, box_len, lanes)] * 2
        + [struct(2, tile_len, tile_len), struct(period, tile_len)],
        in_specs=[smem] + [vmem] * 6,
        out_specs=[vmem] * 7,
        compiler_params=params_of,
        cost_estimate=cost(1 << 30),
        name="ready_step",
    )(tile, table, pupil_map, target_image, mask_param, mate, cross)

    back, pr, pi, info, whole = pl.pallas_call(
        functools.partial(first_kernel, spots, peers, scale),
        out_shape=[struct(grid, lanes), source_len, source_len, struct(8, 128),
                   struct(8, 128, kind=jnp.int32)],
        in_specs=[vmem] * (6 + peers),
        out_specs=[vmem] * 5,
        scratch_shapes=work[2:] + hold + [
            pltpu.SMEM((8, 128), jnp.int32),
            pltpu.SMEM((8, 128), f32),
            pltpu.SemaphoreType.DMA((2,)),
        ],
        compiler_params=params_of,
        cost_estimate=cost(1 << 32),
        name="first_step",
    )(table, plain, crossed_spec, target, *turned, *packed)

    shared = (tile, table, whole, info, pr, pi, target)
    shared_specs = [smem, vmem, smem] + [vmem] * 4

    backs = all_of(back, "tile")
    backs[0] = pl.pallas_call(
        mark_kernel,
        out_shape=struct(grid, lanes),
        in_specs=[vmem],
        out_specs=vmem,
        compiler_params=params_of,
        cost_estimate=cost(1 << 20),
        name="mark_step",
    )(back)
    far, backs[0] = lax.optimization_barrier((far, backs[0]))
    entries = [mask_param, mate]
    for one in far:
        entries += [one, crossed(one, "tile", 1)]
    near, grads, rates, back = pl.pallas_call(
        functools.partial(next_kernel, spots, tiles, scale),
        out_shape=[struct(period, tile_len), struct(tiles, tile_len, tile_len),
                   struct(8, 128), struct(grid, lanes)],
        in_specs=shared_specs + [vmem] * (2 * tiles),
        out_specs=[vmem] * 4,
        scratch_shapes=work + hold + steps,
        compiler_params=params_of,
        cost_estimate=cost(1 << 32),
        name="next_step",
    )(*shared, near, slopes, *entries[2:], *backs)

    backs = all_of(back, "tile")
    slopes = pl.pallas_call(
        functools.partial(slope_kernel, tiles),
        out_shape=struct(tiles, tile_len, tile_len),
        in_specs=[smem] + [vmem] * (2 + tiles),
        out_specs=vmem,
        compiler_params=params_of,
        cost_estimate=cost(1 << 28),
        name="slope_step",
    )(tile, grads, rates, *entries)
    final, row = pl.pallas_call(
        functools.partial(last_kernel, spots, tiles),
        out_shape=[struct(tile_len, tile_len), struct(8, count)],
        in_specs=shared_specs + [vmem] * (2 + tiles),
        out_specs=[left, vmem],
        scratch_shapes=work + [pltpu.VMEM((count, lanes), f32)] + steps + [
            pltpu.VMEM((period, tile_len), f32),
            pltpu.SemaphoreType.DMA((1,)),
        ],
        compiler_params=params_of,
        cost_estimate=cost(1 << 32),
        name="last_step",
    )(*shared, near, slopes, *backs)

    rows = all_of(row, "tile")
    out = pl.pallas_call(
        functools.partial(weight_kernel, tiles, 1.0 / (grid * grid)),
        out_shape=struct(1, local),
        in_specs=[smem] * 2 + [vmem] * (1 + tiles),
        out_specs=vmem,
        scratch_shapes=[pltpu.VMEM((tiles, 8, count), f32)],
        compiler_params=params_of,
        name="weight_step",
    )(tile, place, info, *rows)
    return final, out.reshape(local)


def solution(mesh):
    in_specs = (
        P(("group", "tile"), None),
        P(("group", "tile"), None),
        P(("group", "src")),
        P("src", None),
        P(),
    )
    out_specs = (P(("group", "tile"), None), P(("group", "src")))
    return jax.shard_map(
        per_device, mesh=mesh, in_specs=in_specs, out_specs=out_specs, check_vma=False
    )
```

```python
import functools
import math

import jax
import jax.numpy as jnp
import ml_dtypes
import numpy as np
from jax import lax
from jax.experimental import pallas as pl
from jax.experimental.pallas import tpu as pltpu
from jax.sharding import PartitionSpec as P


MARGIN = 64
MAX_SHIFT = 16
MASK_RATE = 0.5
WEIGHT_RATE = 0.3
TINY_EPS = 1e-06
CHUNK = 16
GROUP = 2


bf16 = jnp.bfloat16
f32 = jnp.float32


def np_split(table):
    table = np.asarray(table, np.float64)
    high = table.astype(np.float32).astype(ml_dtypes.bfloat16)
    low = (table - high.astype(np.float64)).astype(np.float32).astype(ml_dtypes.bfloat16)
    return high, low


def phases(freqs, pixels, period):
    return 2.0 * math.pi * np.mod(np.outer(freqs, pixels), period) / period


def make_tables(tile_len, box_len, max_shift):
    period = tile_len + 2 * MARGIN
    grid = box_len + 2 * max_shift
    wide = np.arange(grid) - grid // 2
    pix = np.arange(tile_len)
    full = np.arange(period)
    points = np.arange(grid)
    box = np.arange(box_len)
    out = {}
    ang = phases(wide, pix, period)
    high, low = np_split(np.concatenate([np.cos(ang), -np.sin(ang)], 0).T / (period * tile_len))
    out["spec_cols"] = np.concatenate([high, low], 1)
    ang_rows = phases(wide, full, period)
    high, low = np_split(np.concatenate([np.cos(ang_rows), np.sin(ang_rows)], 0))
    out["spec_rows"] = np.concatenate([high, low], 0)
    ang = phases(points, points, grid)
    cos, sin = np.cos(ang), np.sin(ang)
    for name, table in (
        ("lane_fwd", np.block([[cos, sin], [-sin, cos]])),
        ("lane_back", np.block([[cos, -sin], [sin, cos]])),
    ):
        high, low = np_split(table)
        out[name] = np.block([[high, low], [high, np.zeros_like(low)]])
    ang = phases(points, box, grid)
    high, low = np_split(np.concatenate([np.cos(ang), np.sin(ang)], 1))
    out["row_fwd"] = np.concatenate([high, high, low], 1)
    high, low = np_split(np.concatenate([np.cos(ang).T, np.sin(ang).T], 0))
    out["row_back"] = np.concatenate([high, high, low], 1)

    def dirichlet(offset):
        theta = 2.0 * math.pi * ((pix + offset)[None, :] / period - points[:, None] / grid)
        orders = np.arange(1, box_len)
        return 1.0 + 2.0 * np.cos(orders[:, None, None] * theta[None]).sum(0)

    rows, cols = dirichlet(MARGIN), dirichlet(0)
    high, low = np_split(rows @ rows.T / grid)
    out["mix_rows"] = np.concatenate([high, high, low], 1)
    mix = cols @ cols.T / grid
    high, low = np_split(np.block([[mix, mix], [mix, mix]]))
    out["mix_cols"] = np.block([[high, low], [high, np.zeros_like(low)]])
    high, low = np_split(rows)
    out["target_rows"] = np.concatenate([high, low], 0)
    high, low = np_split(np.concatenate([cols, cols], 0).T)
    out["target_cols"] = np.concatenate([high, low], 1)
    ang = phases(wide, pix, period)
    cos, sin = np.cos(ang), np.sin(ang)
    high, low = np_split(np.block([[cos, -sin], [-sin, -cos]]))
    out["grad_cols"] = np.concatenate([high, high, low], 0)
    ang = phases(full, np.arange(grid // 2), period)
    high, low = np_split(np.concatenate([np.cos(ang), np.sin(ang)], 1))
    out["grad_rows"] = np.concatenate([high, high, low], 1)
    return out


def pack_tables(tables):
    wide = [n for n in tables if tables[n].shape[1] > 256]
    narrow = sorted((n for n in tables if n not in wide), key=lambda n: -tables[n].shape[0])
    place, heights = {}, [0, 0]
    for n in wide:
        place[n] = (heights[0], 0)
        heights = [heights[0] + tables[n].shape[0]] * 2
    for n in narrow:
        side = int(heights[1] < heights[0])
        place[n] = (heights[side], 256 * side)
        heights[side] += tables[n].shape[0]
    whole = np.zeros((max(heights), 512), ml_dtypes.bfloat16)
    spots = {}
    for n, (row, col) in place.items():
        rows, cols = tables[n].shape
        whole[row : row + rows, col : col + cols] = tables[n]
        spots[n] = (slice(row, row + rows), slice(col, col + cols))
    return whole, spots


def split(value):
    high = value.astype(bf16)
    return high, (value - high.astype(f32)).astype(bf16)


def dot(left, right):
    return jnp.dot(left, right, preferred_element_type=f32)


def halves(value):
    width = value.shape[1] // 2
    return value[:, :width] + value[:, width:]


def lane_sign(rows, lanes, first):
    lane = lax.broadcasted_iota(jnp.int32, (rows, lanes), 1)
    return jnp.where(lane < lanes // 2, first, -first).astype(f32)


def swap(value):
    return pltpu.roll(value, value.shape[1] // 2, 1)


def half_tanh(value):
    return jnp.tanh(0.5 * value)


def sigmoid(value):
    return 0.5 * half_tanh(value) + 0.5


def window_spectrum(window, t):
    grid = t["spec_cols"].shape[1] // 4
    high, low = split(window)
    cols = t["spec_cols"]
    mid = halves(dot(high, cols[...])) + dot(low, cols[:, : 2 * grid])
    mid_high, mid_low = split(mid)
    rows = t["spec_rows"]
    both = halves(dot(rows[: 2 * grid, :], jnp.concatenate([mid_high, mid_low], 1)))
    both = both + dot(rows[2 * grid :, :], mid_high)
    return both[:grid] + lane_sign(grid, 2 * grid, 1.0) * swap(both[grid:])


def skewed(count, stages, first, second, carry):
    chunks = count // CHUNK
    first(0, stages[0])
    for c in range(1, chunks):
        first(c, stages[c % 2])
        carry = second(c - 1, stages[(c - 1) % 2], carry)
    return second(chunks - 1, stages[(chunks - 1) % 2], carry)


def turn_pupils(pupil, turned_re, turned_im):
    count, size, lanes = turned_re.shape
    grid = lanes // 2
    turned_re[0] = jnp.zeros((size, lanes), f32)
    turned_im[0] = jnp.zeros((size, lanes), f32)
    turned_re[0, :, :size] = pupil[0]
    turned_re[0, :, grid : grid + size] = pupil[0]
    turned_im[0, :, :size] = -pupil[1]
    turned_im[0, :, grid : grid + size] = pupil[1]
    real, imag = turned_re[0], turned_im[0]
    for by in range(1, count):
        turned_re[by] = pltpu.roll(real, by, 1)
        turned_im[by] = pltpu.roll(imag, by, 1)


def placed_pupils(shifts, roots, turned_re, turned_im, pr, pi):
    def make(s):
        by = shifts[2, s] + MAX_SHIFT
        real, imag = turned_re[by] * roots[3, s], turned_im[by] * roots[3, s]
        pr[s], pi[s] = real, imag
        return real, imag

    return make


def grid_fields(spec, shifts, t, pupils, work, squares=False):
    plain, crossed, fields, *stages = work
    count, grid, lanes = fields.shape
    box_len = t["row_fwd"].shape[1] // 6
    if spec is not None:
        plain[...] = spec
        crossed[...] = swap(spec)
    sign = lane_sign(box_len, lanes, -1.0)

    def first(c, stage):
        rows = []
        for i in range(CHUNK):
            s = c * CHUNK + i
            at = pl.ds(shifts[1, s] + MAX_SHIFT, box_len)
            real, imag = pupils(s)
            high, low = split(real * plain[at, :] + imag * crossed[at, :])
            rows.append(jnp.concatenate([high, low], 1))
        stage[...] = halves(dot(jnp.concatenate(rows, 0), t["lane_fwd"][...]))

    def second(c, stage, power):
        for base in range(0, CHUNK, GROUP):
            stacks = []
            for i in range(base, base + GROUP):
                part = stage[i * box_len : (i + 1) * box_len, :]
                high, low = split(jnp.concatenate([part, sign * swap(part)], 0))
                stacks.append(jnp.concatenate([high, low, high], 0))
            out = dot(t["row_fwd"][...], jnp.concatenate(stacks, 1))
            for i in range(GROUP):
                field = out[:, i * lanes : (i + 1) * lanes]
                square = field * field
                fields[c * CHUNK + base + i] = square if squares else field
                power = power + square
        return power

    return skewed(count, stages, first, second, jnp.zeros((grid, lanes), f32))


def grid_misfit(power, inv_dose, target, t):
    high, low = split(power)
    mid = halves(dot(jnp.concatenate([high, low], 1), t["mix_cols"][...]))
    high, low = split(mid)
    lit = dot(t["mix_rows"][...], jnp.concatenate([high, low, high], 0))
    return lit * inv_dose - target


def gather_back(misfit, shifts, scale, t, pr, pi, fields, stages, sums):
    count, box_len, lanes = pr.shape
    grid = lanes // 2
    for ref in sums:
        ref[...] = jnp.zeros_like(ref)
    sign = lane_sign(box_len, lanes, 1.0)

    def first(c, stage):
        for base in range(0, CHUNK, GROUP):
            stacks = []
            for i in range(base, base + GROUP):
                high, low = split(fields[c * CHUNK + i] * misfit)
                stacks.append(jnp.concatenate([high, low, high], 0))
            both = dot(t["row_back"][...], jnp.concatenate(stacks, 1))
            for i in range(GROUP):
                part = both[:, i * lanes : (i + 1) * lanes]
                at = (base + i) * box_len
                stage[at : at + box_len, :] = part[:box_len] + sign * swap(part[box_len:])

    def second(c, stage, carry):
        high, low = split(stage[...])
        hits = halves(dot(jnp.concatenate([high, low], 1), t["lane_back"][...]))
        for i in range(CHUNK):
            s = c * CHUNK + i
            rows = pl.ds(shifts[1, s] + MAX_SHIFT, box_len)
            hit = hits[i * box_len : (i + 1) * box_len]
            one, two = sums[2 * (i % 2)], sums[2 * (i % 2) + 1]
            one[rows, :] += pr[s] * hit
            two[rows, :] += pi[s] * hit
        return carry

    skewed(count, stages, first, second, 0)
    whole, turned = sums[0], sums[1]
    whole[...] = (whole[...] + sums[2][...] + swap(turned[...] + sums[3][...])) * scale
    middle = grid // 2
    turned[0:1, :] = jnp.zeros((1, lanes), f32)
    for a in range(1, middle):
        turned[a : a + 1, :] = whole[middle - a : middle - a + 1, :]
    ahead, behind = whole[middle:, :], turned[:middle, :]
    return jnp.concatenate([ahead + behind, ahead - behind], 0)


def tile_of(k, tile):
    return lax.bitwise_xor(tile, jnp.int32(k))


def fill_windows(backs, t, tile, tiles, wins):
    half = backs[0].shape[0] // 2
    tile_len = wins.shape[2]
    stacks = []
    for rows in (slice(0, half), slice(half, 2 * half)):
        parts = []
        for back in backs:
            high, low = split(back[rows, :])
            parts.append(jnp.concatenate([high, low, high], 1))
        stacks.append(jnp.concatenate(parts, 0))
    even = dot(stacks[0], t["grad_cols"][:, :tile_len])
    odd = dot(stacks[1], t["grad_cols"][:, tile_len:])
    wins[0, MARGIN + tile_len :, :] = jnp.zeros((MARGIN, tile_len), f32)
    wins[tiles + 1, :MARGIN, :] = jnp.zeros((MARGIN, tile_len), f32)
    for k in range(tiles):
        at = slice(k * half, (k + 1) * half)
        high, low = split(jnp.concatenate([even[at], odd[at]], 0))
        out = dot(t["grad_rows"][...], jnp.concatenate([high, low, high], 0))
        wins[tile_of(k, tile) + 1] = out


def pieces(tile_len):
    return (
        (0, MARGIN, 0, tile_len),
        (MARGIN, tile_len - MARGIN, 1, 0),
        (tile_len - MARGIN, tile_len, 2, -tile_len),
    )


def piece_total(own, piece, wins):
    low, high, near, shift = piece
    total = wins[own + 1, MARGIN + low : MARGIN + high, :]
    if near != 1:
        at = MARGIN + low + shift
        total = total + wins[own + near, at : at + MARGIN, :]
    return total


def squares_of(grad):
    return jnp.sum((grad * grad).reshape(-1, 8, grad.shape[1]), axis=0)


def step_rate(square, tiles):
    tile_len = square.shape[1]
    total = jnp.sum(jnp.sum(square, axis=0, keepdims=True), axis=1, keepdims=True)
    return MASK_RATE / jnp.sqrt(total / (tiles * tile_len * tile_len) + TINY_EPS)


def slope_of(params):
    lean = half_tanh(params)
    return 1.0 - lean * lean


def near_tiles(tile, tiles):
    prev, follow = jnp.maximum(tile - 1, 0), jnp.minimum(tile + 1, tiles - 1)
    return prev, follow, (tile > 0).astype(f32), (tile < tiles - 1).astype(f32)


def edge_params(tile, mate, cross):
    odd = lax.rem(tile, 2) > 0
    before = jnp.where(odd, mate[-MARGIN:, :], cross[...])
    after = jnp.where(odd, cross[...], mate[:MARGIN, :])
    return before, after


def mask_window(near, has_prev, has_next):
    rows = near.shape[0]
    return jnp.concatenate(
        [
            sigmoid(near[:MARGIN, :]) * has_prev,
            sigmoid(near[MARGIN : rows - MARGIN, :]),
            sigmoid(near[rows - MARGIN :, :]) * has_next,
        ],
        0,
    )


def start_all(pairs, sems):
    copies = [pltpu.make_async_copy(a, b, sems.at[i]) for i, (a, b) in enumerate(pairs)]
    for copy in copies:
        copy.start()
    return copies


def head_kernel(out):
    out[...] = jnp.zeros_like(out)


def mark_kernel(value, out):
    out[...] = value[...]


def pack_kernel(place, head, weights, shifts, packed):
    local = weights.shape[1]
    packed[...] = head[...]
    packed[0:1, :local] = weights[...]
    packed[1:3, :local] = shifts[...].astype(f32)
    packed[3:4, :local] = jnp.sqrt(weights[...])
    packed[...] = pltpu.roll(packed[...], place[0] * local, 1)


def edge_kernel(tile, mask, edge):
    at = pl.multiple_of(lax.rem(tile[0], 2) * (mask.shape[0] - MARGIN), MARGIN)
    edge[...] = mask[pl.ds(at, MARGIN), :]


def target_terms(target, t):
    rows, cols = t["target_rows"], t["target_cols"]
    grid = rows.shape[0] // 2
    high, low = split(target)
    both = dot(rows[...], high)
    mid = both[:grid] + both[grid:] + dot(rows[:grid, :], low)
    high, low = split(mid)
    return halves(dot(high, cols[...])) + dot(low, cols[:, : 2 * grid])


def doses(info, scale):
    dose = jnp.sum(info[0:1, :], axis=1, keepdims=True)
    return 1.0 / dose, scale / dose


def ready_kernel(spots, tiles, tile, table, pupil, goal, own, mate, cross,
                 plain, crossed, target, turned_re, turned_im, slopes, near):
    t = {n: table.at[spot] for n, spot in spots.items()}
    here = tile[0]
    tile_len = own.shape[0]
    _, _, has_prev, has_next = near_tiles(here, tiles)
    before, after = edge_params(here, mate, cross)
    near[:MARGIN, :] = before
    near[MARGIN : MARGIN + tile_len, :] = own[...]
    near[MARGIN + tile_len :, :] = after
    turn_pupils(pupil, turned_re, turned_im)
    spec = window_spectrum(mask_window(near, has_prev, has_next), t)
    plain[...] = spec
    crossed[...] = swap(spec)
    target[...] = target_terms(goal[...], t)
    slopes[0] = slope_of(own[...])
    slopes[1] = slope_of(mate[...])


def first_kernel(spots, peers, scale, table, plain, crossed, target, turned_re, turned_im, *refs):
    parts = refs[:peers]
    t = {n: table.at[spot] for n, spot in spots.items()}
    back, pr, pi, info, whole = refs[peers : peers + 5]
    *work, s0, s1, s2, s3, shifts, roots, sems = refs[peers + 5 :]
    total = parts[0][...]
    for part in parts[1:]:
        total = total + part[...]
    info[...] = total
    whole[...] = total.astype(jnp.int32)
    for copy in start_all(((whole, shifts), (info, roots)), sems):
        copy.wait()
    pupils = placed_pupils(shifts, roots, turned_re, turned_im, pr, pi)
    work = [plain, crossed, *work]
    power = grid_fields(None, shifts, t, pupils, work)
    inv_dose, factor = doses(total, scale)
    misfit = grid_misfit(power, inv_dose, target[...], t)
    sums = (s0, s1, s2, s3)
    back[...] = gather_back(misfit, shifts, factor, t, pr, pi, work[2], work[3:], sums)


def next_kernel(spots, tiles, scale, tile, table, shifts, info, pr, pi, target, near, slopes, *refs):
    params, backs = refs[: tiles - 2], refs[tiles - 2 : 2 * tiles - 2]
    t = {n: table.at[spot] for n, spot in spots.items()}
    new, grads, rates, back, *work, s0, s1, s2, s3, wins = refs[2 * tiles - 2 :]
    here = tile[0]
    tile_len = wins.shape[2]
    fill_windows(backs, t, here, tiles, wins)
    square = jnp.zeros((8, tile_len), f32)
    for k in range(tiles):
        own = tile_of(k, here)
        for piece in pieces(tile_len):
            low, high = piece[:2]
            slope = slopes[k, low:high, :] if k < 2 else slope_of(params[k - 2][low:high, :])
            grad = piece_total(own, piece, wins) * slope
            grads[own, low:high, :] = grad
            square = square + squares_of(grad)
    rate = step_rate(square, tiles)
    rates[...] = jnp.broadcast_to(rate, rates.shape)
    prev, follow, has_prev, has_next = near_tiles(here, tiles)
    inner = slice(MARGIN, MARGIN + tile_len)
    new[:MARGIN, :] = near[:MARGIN, :] - grads[prev, tile_len - MARGIN :, :] * rate
    new[inner, :] = near[inner, :] - grads[here] * rate
    new[MARGIN + tile_len :, :] = near[MARGIN + tile_len :, :] - grads[follow, :MARGIN, :] * rate
    spec = window_spectrum(mask_window(new, has_prev, has_next), t)
    power = grid_fields(spec, shifts, t, lambda s: (pr[s], pi[s]), work)
    inv_dose, factor = doses(info[...], scale)
    misfit = grid_misfit(power, inv_dose, target[...], t)
    sums = (s0, s1, s2, s3)
    back[...] = gather_back(misfit, shifts, factor, t, pr, pi, work[2], work[3:], sums)


def slope_kernel(tiles, tile, grads, rates, *refs):
    params, slopes = refs[:tiles], refs[tiles]
    rate = rates[0:1, 0:1]
    for k in range(tiles):
        own = tile_of(k, tile[0])
        slopes[own] = slope_of(params[k][...] - grads[own] * rate)


def last_kernel(spots, tiles, tile, table, shifts, info, pr, pi, target, near, slopes, *refs):
    backs = refs[:tiles]
    t = {n: table.at[spot] for n, spot in spots.items()}
    final, row, *work, terms, wins, fresh, sems = refs[tiles:]
    fields = work[2]
    here = tile[0]
    tile_len = wins.shape[2]
    fill_windows(backs, t, here, tiles, wins)

    def grad_of(own, piece):
        return piece_total(own, piece, wins) * slopes[own, piece[0] : piece[1], :]

    square = jnp.zeros((8, tile_len), f32)
    for own in range(tiles):
        for piece in pieces(tile_len):
            square = square + squares_of(grad_of(own, piece))
    rate = step_rate(square, tiles)
    prev, follow, has_prev, has_next = near_tiles(here, tiles)
    first, *_, end = pieces(tile_len)
    fresh[:MARGIN, :] = near[:MARGIN, :] - grad_of(prev, end) * rate
    for piece in pieces(tile_len):
        at = slice(MARGIN + piece[0], MARGIN + piece[1])
        fresh[at, :] = near[at, :] - grad_of(here, piece) * rate
    fresh[MARGIN + tile_len :, :] = near[MARGIN + tile_len :, :] - grad_of(follow, first) * rate
    (leave,) = start_all(((fresh.at[pl.ds(MARGIN, tile_len), :], final),), sems)
    spec = window_spectrum(mask_window(fresh, has_prev, has_next), t)
    power = grid_fields(
        spec, shifts, t, lambda s: (pr[s], pi[s]), work, squares=True
    )
    inv_dose, _ = doses(info[...], 1.0)
    misfit = grid_misfit(power, inv_dose, target[...], t)

    def chunk(c, carry):
        rows = []
        for i in range(CHUNK):
            rows.append(jnp.sum(fields[c * CHUNK + i] * misfit, axis=0, keepdims=True))
        terms[pl.ds(pl.multiple_of(c * CHUNK, CHUNK), CHUNK), :] = jnp.concatenate(rows, 0)
        return carry

    count = fields.shape[0]
    lax.fori_loop(0, count // CHUNK, chunk, 0)
    high, low = split(terms[...])
    left = terms[...] - high.astype(f32) - low.astype(f32)
    ones = jnp.ones((8, terms.shape[1]), bf16)
    total = jnp.zeros((8, terms.shape[0]), f32)
    for part in (left.astype(bf16), low, high):
        total = total + lax.dot_general(
            ones, part, (((1,), (1,)), ((), ())), preferred_element_type=f32
        )
    row[...] = total
    leave.wait()


def weight_kernel(tiles, scale, tile, place, info, *refs):
    rows = refs[:tiles]
    out, stack = refs[tiles:]
    count = rows[0].shape[1]
    for k in range(tiles):
        stack[k] = rows[k][...]
    here = tile[0]
    total = stack[here]
    for k in range(1, tiles):
        total = total + stack[tile_of(k, here)]
    summed = total[0:1] * scale
    weight = info[0:1, :count]
    dose = jnp.sum(weight, axis=1, keepdims=True)
    mean = jnp.sum(summed, axis=1, keepdims=True) / dose
    grad = (summed / weight - mean) / dose
    spread = jnp.sqrt(jnp.sum(grad * grad, axis=1, keepdims=True) / count + TINY_EPS)
    new = weight * jnp.exp(-WEIGHT_RATE * grad / spread)
    size = out.shape[1]
    lanes = info.shape[1]
    if count < lanes:
        new = jnp.concatenate([new, jnp.zeros((1, lanes - count), f32)], 1)
    new = pltpu.roll(jnp.broadcast_to(new, (8, lanes)), lanes - place[0] * size, 1)
    out[...] = new[0:1, :size]


def crossed(value, axis, k):
    return lax.ppermute(value, axis, [(i, i ^ k) for i in range(lax.axis_size(axis))])


def all_of(value, axis):
    got = [value]
    for k in range(1, lax.axis_size(axis)):
        got.append(crossed(value, axis, k))
    return got


def per_device(mask_param, target_image, source_weights, source_shifts, pupil_map):
    tile_len = mask_param.shape[1]
    box_len = pupil_map.shape[1]
    grid = box_len + 2 * MAX_SHIFT
    lanes = 2 * grid
    tiles = lax.axis_size("tile")
    peers = lax.axis_size("src")
    local = source_weights.shape[0]
    count = local * peers
    assert tiles & (tiles - 1) == 0 and peers & (peers - 1) == 0 and count <= 128 and count % CHUNK == 0
    tables = make_tables(tile_len, box_len, MAX_SHIFT)

    tile = lax.axis_index("tile").astype(jnp.int32).reshape(1)
    place = lax.axis_index("src").astype(jnp.int32).reshape(1)

    vmem = pl.BlockSpec(memory_space=pltpu.VMEM)
    smem = pl.BlockSpec(memory_space=pltpu.SMEM)
    left = pl.BlockSpec(memory_space=pltpu.HBM)
    params_of = pltpu.CompilerParams(vmem_limit_bytes=32 << 20)

    def struct(*shape, kind=f32):
        return jax.ShapeDtypeStruct(shape, kind)

    def cost(flops):
        return pl.CostEstimate(flops=flops, bytes_accessed=1 << 20, transcendentals=0)

    head = pl.pallas_call(
        head_kernel,
        out_shape=struct(8, 128),
        out_specs=vmem,
        compiler_params=params_of,
        cost_estimate=cost(1 << 34),
        name="head_step",
    )()
    packed = pl.pallas_call(
        pack_kernel,
        out_shape=struct(8, 128),
        in_specs=[smem] + [vmem] * 3,
        out_specs=vmem,
        compiler_params=params_of,
        cost_estimate=cost(1 << 20),
        name="pack_sources",
    )(place, head, source_weights[None], source_shifts.T)
    _, mask_now = lax.optimization_barrier((packed, mask_param))
    edge = pl.pallas_call(
        edge_kernel,
        out_shape=struct(MARGIN, tile_len),
        in_specs=[smem, vmem],
        out_specs=vmem,
        compiler_params=params_of,
        cost_estimate=cost(1 << 20),
        name="edge_rows",
    )(tile, mask_now)
    packed = all_of(packed, "src")

    pairs = [(i, (i + 1) % tiles) for i in range(1, tiles, 2)]
    cross = lax.ppermute(edge, "tile", pairs + [(j, i) for i, j in pairs])
    mate = crossed(mask_param, "tile", 1)
    far = [crossed(mask_param, "tile", k) for k in range(2, tiles, 2)]

    whole, spots = pack_tables(tables)
    table = jnp.asarray(whole)
    work = [
        pltpu.VMEM((grid, lanes), f32),
        pltpu.VMEM((grid, lanes), f32),
        pltpu.VMEM((count, grid, lanes), f32),
        pltpu.VMEM((CHUNK * box_len, lanes), f32),
        pltpu.VMEM((CHUNK * box_len, lanes), f32),
    ]
    hold = [pltpu.VMEM((grid, lanes), f32)] * 4
    period = tile_len + 2 * MARGIN
    steps = [pltpu.VMEM((tiles + 2, period, tile_len), f32)]
    scale = 0.5 / (grid * grid * period * tile_len)
    source_len = struct(count, box_len, lanes)

    plain, crossed_spec, target, *turned, slopes, near = pl.pallas_call(
        functools.partial(ready_kernel, spots, tiles),
        out_shape=[struct(grid, lanes)] * 3
        + [struct(2 * MAX_SHIFT + 1, box_len, lanes)] * 2
        + [struct(2, tile_len, tile_len), struct(period, tile_len)],
        in_specs=[smem] + [vmem] * 6,
        out_specs=[vmem] * 7,
        compiler_params=params_of,
        cost_estimate=cost(1 << 30),
        name="ready_step",
    )(tile, table, pupil_map, target_image, mask_param, mate, cross)

    back, pr, pi, info, whole = pl.pallas_call(
        functools.partial(first_kernel, spots, peers, scale),
        out_shape=[struct(grid, lanes), source_len, source_len, struct(8, 128),
                   struct(8, 128, kind=jnp.int32)],
        in_specs=[vmem] * (6 + peers),
        out_specs=[vmem] * 5,
        scratch_shapes=work[2:] + hold + [
            pltpu.SMEM((8, 128), jnp.int32),
            pltpu.SMEM((8, 128), f32),
            pltpu.SemaphoreType.DMA((2,)),
        ],
        compiler_params=params_of,
        cost_estimate=cost(1 << 32),
        name="first_step",
    )(table, plain, crossed_spec, target, *turned, *packed)

    shared = (tile, table, whole, info, pr, pi, target)
    shared_specs = [smem, vmem, smem] + [vmem] * 4

    backs = all_of(back, "tile")
    backs[0] = pl.pallas_call(
        mark_kernel,
        out_shape=struct(grid, lanes),
        in_specs=[vmem],
        out_specs=vmem,
        compiler_params=params_of,
        cost_estimate=cost(1 << 20),
        name="mark_step",
    )(back)
    far, backs[0] = lax.optimization_barrier((far, backs[0]))
    entries = [mask_param, mate]
    for one in far:
        entries += [one, crossed(one, "tile", 1)]
    near, grads, rates, back = pl.pallas_call(
        functools.partial(next_kernel, spots, tiles, scale),
        out_shape=[struct(period, tile_len), struct(tiles, tile_len, tile_len),
                   struct(8, 128), struct(grid, lanes)],
        in_specs=shared_specs + [vmem] * (2 * tiles),
        out_specs=[vmem] * 4,
        scratch_shapes=work + hold + steps,
        compiler_params=params_of,
        cost_estimate=cost(1 << 32),
        name="next_step",
    )(*shared, near, slopes, *entries[2:], *backs)

    backs = all_of(back, "tile")
    slopes = pl.pallas_call(
        functools.partial(slope_kernel, tiles),
        out_shape=struct(tiles, tile_len, tile_len),
        in_specs=[smem] + [vmem] * (2 + tiles),
        out_specs=vmem,
        compiler_params=params_of,
        cost_estimate=cost(1 << 28),
        name="slope_step",
    )(tile, grads, rates, *entries)
    final, row = pl.pallas_call(
        functools.partial(last_kernel, spots, tiles),
        out_shape=[struct(tile_len, tile_len), struct(8, count)],
        in_specs=shared_specs + [vmem] * (2 + tiles),
        out_specs=[left, vmem],
        scratch_shapes=work + [pltpu.VMEM((count, lanes), f32)] + steps + [
            pltpu.VMEM((period, tile_len), f32),
            pltpu.SemaphoreType.DMA((1,)),
        ],
        compiler_params=params_of,
        cost_estimate=cost(1 << 32),
        name="last_step",
    )(*shared, near, slopes, *backs)

    rows = all_of(row, "tile")
    out = pl.pallas_call(
        functools.partial(weight_kernel, tiles, 1.0 / (grid * grid)),
        out_shape=struct(1, local),
        in_specs=[smem] * 2 + [vmem] * (1 + tiles),
        out_specs=vmem,
        scratch_shapes=[pltpu.VMEM((tiles, 8, count), f32)],
        compiler_params=params_of,
        name="weight_step",
    )(tile, place, info, *rows)
    return final, out.reshape(local)


def solution(mesh):
    in_specs = (
        P(("group", "tile"), None),
        P(("group", "tile"), None),
        P(("group", "src")),
        P("src", None),
        P(),
    )
    out_specs = (P(("group", "tile"), None), P(("group", "src")))
    return jax.shard_map(
        per_device, mesh=mesh, in_specs=in_specs, out_specs=out_specs, check_vma=False
    )
```

```python
import functools
import math

import jax
import jax.numpy as jnp
import ml_dtypes
import numpy as np
from jax import lax
from jax.experimental import pallas as pl
from jax.experimental.pallas import tpu as pltpu
from jax.sharding import PartitionSpec as P


MARGIN = 64
MAX_SHIFT = 16
MASK_RATE = 0.5
WEIGHT_RATE = 0.3
TINY_EPS = 1e-06
CHUNK = 32
GROUP = 2


bf16 = jnp.bfloat16
f32 = jnp.float32


def np_split(table):
    table = np.asarray(table, np.float64)
    high = table.astype(np.float32).astype(ml_dtypes.bfloat16)
    low = (table - high.astype(np.float64)).astype(np.float32).astype(ml_dtypes.bfloat16)
    return high, low


def phases(freqs, pixels, period):
    return 2.0 * math.pi * np.mod(np.outer(freqs, pixels), period) / period


def make_tables(tile_len, box_len, max_shift):
    period = tile_len + 2 * MARGIN
    grid = box_len + 2 * max_shift
    wide = np.arange(grid) - grid // 2
    pix = np.arange(tile_len)
    full = np.arange(period)
    points = np.arange(grid)
    box = np.arange(box_len)
    out = {}
    ang = phases(wide, pix, period)
    high, low = np_split(np.concatenate([np.cos(ang), -np.sin(ang)], 0).T / (period * tile_len))
    out["spec_cols"] = np.concatenate([high, low], 1)
    ang_rows = phases(wide, full, period)
    high, low = np_split(np.concatenate([np.cos(ang_rows), np.sin(ang_rows)], 0))
    out["spec_rows"] = np.concatenate([high, low], 0)
    ang = phases(points, points, grid)
    cos, sin = np.cos(ang), np.sin(ang)
    for name, table in (
        ("lane_fwd", np.block([[cos, sin], [-sin, cos]])),
        ("lane_back", np.block([[cos, -sin], [sin, cos]])),
    ):
        high, low = np_split(table)
        out[name] = np.block([[high, low], [high, np.zeros_like(low)]])
    ang = phases(points, box, grid)
    high, low = np_split(np.concatenate([np.cos(ang), np.sin(ang)], 1))
    out["row_fwd"] = np.concatenate([high, high, low], 1)
    high, low = np_split(np.concatenate([np.cos(ang).T, np.sin(ang).T], 0))
    out["row_back"] = np.concatenate([high, high, low], 1)

    def dirichlet(offset):
        theta = 2.0 * math.pi * ((pix + offset)[None, :] / period - points[:, None] / grid)
        orders = np.arange(1, box_len)
        return 1.0 + 2.0 * np.cos(orders[:, None, None] * theta[None]).sum(0)

    rows, cols = dirichlet(MARGIN), dirichlet(0)
    high, low = np_split(rows @ rows.T / grid)
    out["mix_rows"] = np.concatenate([high, high, low], 1)
    mix = cols @ cols.T / grid
    high, low = np_split(np.block([[mix, mix], [mix, mix]]))
    out["mix_cols"] = np.block([[high, low], [high, np.zeros_like(low)]])
    high, low = np_split(rows)
    out["target_rows"] = np.concatenate([high, low], 0)
    high, low = np_split(np.concatenate([cols, cols], 0).T)
    out["target_cols"] = np.concatenate([high, low], 1)
    ang = phases(wide, pix, period)
    cos, sin = np.cos(ang), np.sin(ang)
    high, low = np_split(np.block([[cos, -sin], [-sin, -cos]]))
    out["grad_cols"] = np.concatenate([high, high, low], 0)
    ang = phases(full, np.arange(grid // 2), period)
    high, low = np_split(np.concatenate([np.cos(ang), np.sin(ang)], 1))
    out["grad_rows"] = np.concatenate([high, high, low], 1)
    return out


def pack_tables(tables):
    wide = [n for n in tables if tables[n].shape[1] > 256]
    narrow = sorted((n for n in tables if n not in wide), key=lambda n: -tables[n].shape[0])
    place, heights = {}, [0, 0]
    for n in wide:
        place[n] = (heights[0], 0)
        heights = [heights[0] + tables[n].shape[0]] * 2
    for n in narrow:
        side = int(heights[1] < heights[0])
        place[n] = (heights[side], 256 * side)
        heights[side] += tables[n].shape[0]
    whole = np.zeros((max(heights), 512), ml_dtypes.bfloat16)
    spots = {}
    for n, (row, col) in place.items():
        rows, cols = tables[n].shape
        whole[row : row + rows, col : col + cols] = tables[n]
        spots[n] = (slice(row, row + rows), slice(col, col + cols))
    return whole, spots


def split(value):
    high = value.astype(bf16)
    return high, (value - high.astype(f32)).astype(bf16)


def dot(left, right):
    return jnp.dot(left, right, preferred_element_type=f32)


def halves(value):
    width = value.shape[1] // 2
    return value[:, :width] + value[:, width:]


def lane_sign(rows, lanes, first):
    lane = lax.broadcasted_iota(jnp.int32, (rows, lanes), 1)
    return jnp.where(lane < lanes // 2, first, -first).astype(f32)


def swap(value):
    return pltpu.roll(value, value.shape[1] // 2, 1)


def half_tanh(value):
    return jnp.tanh(0.5 * value)


def sigmoid(value):
    return 0.5 * half_tanh(value) + 0.5


def window_spectrum(window, t):
    grid = t["spec_cols"].shape[1] // 4
    high, low = split(window)
    cols = t["spec_cols"]
    mid = halves(dot(high, cols[...])) + dot(low, cols[:, : 2 * grid])
    mid_high, mid_low = split(mid)
    rows = t["spec_rows"]
    both = halves(dot(rows[: 2 * grid, :], jnp.concatenate([mid_high, mid_low], 1)))
    both = both + dot(rows[2 * grid :, :], mid_high)
    return both[:grid] + lane_sign(grid, 2 * grid, 1.0) * swap(both[grid:])


def skewed(count, stages, first, second, carry):
    chunks = count // CHUNK
    first(0, stages[0])
    for c in range(1, chunks):
        first(c, stages[c % 2])
        carry = second(c - 1, stages[(c - 1) % 2], carry)
    return second(chunks - 1, stages[(chunks - 1) % 2], carry)


def turn_pupils(pupil, turned_re, turned_im):
    count, size, lanes = turned_re.shape
    grid = lanes // 2
    turned_re[0] = jnp.zeros((size, lanes), f32)
    turned_im[0] = jnp.zeros((size, lanes), f32)
    turned_re[0, :, :size] = pupil[0]
    turned_re[0, :, grid : grid + size] = pupil[0]
    turned_im[0, :, :size] = -pupil[1]
    turned_im[0, :, grid : grid + size] = pupil[1]
    real, imag = turned_re[0], turned_im[0]
    for by in range(1, count):
        turned_re[by] = pltpu.roll(real, by, 1)
        turned_im[by] = pltpu.roll(imag, by, 1)


def placed_pupils(shifts, roots, turned_re, turned_im, pr, pi):
    def make(s):
        by = shifts[2, s] + MAX_SHIFT
        real, imag = turned_re[by] * roots[3, s], turned_im[by] * roots[3, s]
        pr[s], pi[s] = real, imag
        return real, imag

    return make


def grid_fields(spec, shifts, t, pupils, work, squares=False):
    plain, crossed, fields, *stages = work
    count, grid, lanes = fields.shape
    box_len = t["row_fwd"].shape[1] // 6
    plain[...] = spec
    crossed[...] = swap(spec)
    sign = lane_sign(box_len, lanes, -1.0)

    def first(c, stage):
        rows = []
        for i in range(CHUNK):
            s = c * CHUNK + i
            at = pl.ds(shifts[1, s] + MAX_SHIFT, box_len)
            real, imag = pupils(s)
            high, low = split(real * plain[at, :] + imag * crossed[at, :])
            rows.append(jnp.concatenate([high, low], 1))
        stage[...] = halves(dot(jnp.concatenate(rows, 0), t["lane_fwd"][...]))

    def second(c, stage, power):
        for base in range(0, CHUNK, GROUP):
            stacks = []
            for i in range(base, base + GROUP):
                part = stage[i * box_len : (i + 1) * box_len, :]
                high, low = split(jnp.concatenate([part, sign * swap(part)], 0))
                stacks.append(jnp.concatenate([high, low, high], 0))
            out = dot(t["row_fwd"][...], jnp.concatenate(stacks, 1))
            for i in range(GROUP):
                field = out[:, i * lanes : (i + 1) * lanes]
                square = field * field
                fields[c * CHUNK + base + i] = square if squares else field
                power = power + square
        return power

    return skewed(count, stages, first, second, jnp.zeros((grid, lanes), f32))


def grid_misfit(power, inv_dose, target, t):
    high, low = split(power)
    mid = halves(dot(jnp.concatenate([high, low], 1), t["mix_cols"][...]))
    high, low = split(mid)
    lit = dot(t["mix_rows"][...], jnp.concatenate([high, low, high], 0))
    return lit * inv_dose - target


def gather_back(misfit, shifts, scale, t, pr, pi, fields, stages, sums):
    count, box_len, lanes = pr.shape
    grid = lanes // 2
    for ref in sums:
        ref[...] = jnp.zeros_like(ref)
    sign = lane_sign(box_len, lanes, 1.0)

    def first(c, stage):
        for base in range(0, CHUNK, GROUP):
            stacks = []
            for i in range(base, base + GROUP):
                high, low = split(fields[c * CHUNK + i] * misfit)
                stacks.append(jnp.concatenate([high, low, high], 0))
            both = dot(t["row_back"][...], jnp.concatenate(stacks, 1))
            for i in range(GROUP):
                part = both[:, i * lanes : (i + 1) * lanes]
                at = (base + i) * box_len
                stage[at : at + box_len, :] = part[:box_len] + sign * swap(part[box_len:])

    def second(c, stage, carry):
        high, low = split(stage[...])
        hits = halves(dot(jnp.concatenate([high, low], 1), t["lane_back"][...]))
        for i in range(CHUNK):
            s = c * CHUNK + i
            rows = pl.ds(shifts[1, s] + MAX_SHIFT, box_len)
            hit = hits[i * box_len : (i + 1) * box_len]
            one, two = sums[2 * (i % 2)], sums[2 * (i % 2) + 1]
            one[rows, :] += pr[s] * hit
            two[rows, :] += pi[s] * hit
        return carry

    skewed(count, stages, first, second, 0)
    whole, turned = sums[0], sums[1]
    whole[...] = (whole[...] + sums[2][...] + swap(turned[...] + sums[3][...])) * scale
    middle = grid // 2
    turned[0:1, :] = jnp.zeros((1, lanes), f32)
    for a in range(1, middle):
        turned[a : a + 1, :] = whole[middle - a : middle - a + 1, :]
    ahead, behind = whole[middle:, :], turned[:middle, :]
    return jnp.concatenate([ahead + behind, ahead - behind], 0)


def tile_of(k, tile):
    return lax.bitwise_xor(tile, jnp.int32(k))


def fill_windows(backs, t, tile, tiles, wins):
    half = backs[0].shape[0] // 2
    tile_len = wins.shape[2]
    stacks = []
    for rows in (slice(0, half), slice(half, 2 * half)):
        parts = []
        for back in backs:
            high, low = split(back[rows, :])
            parts.append(jnp.concatenate([high, low, high], 1))
        stacks.append(jnp.concatenate(parts, 0))
    even = dot(stacks[0], t["grad_cols"][:, :tile_len])
    odd = dot(stacks[1], t["grad_cols"][:, tile_len:])
    wins[0, MARGIN + tile_len :, :] = jnp.zeros((MARGIN, tile_len), f32)
    wins[tiles + 1, :MARGIN, :] = jnp.zeros((MARGIN, tile_len), f32)
    for k in range(tiles):
        at = slice(k * half, (k + 1) * half)
        high, low = split(jnp.concatenate([even[at], odd[at]], 0))
        out = dot(t["grad_rows"][...], jnp.concatenate([high, low, high], 0))
        wins[tile_of(k, tile) + 1] = out


def pieces(tile_len):
    return (
        (0, MARGIN, 0, tile_len),
        (MARGIN, tile_len - MARGIN, 1, 0),
        (tile_len - MARGIN, tile_len, 2, -tile_len),
    )


def piece_total(own, piece, wins):
    low, high, near, shift = piece
    total = wins[own + 1, MARGIN + low : MARGIN + high, :]
    if near != 1:
        at = MARGIN + low + shift
        total = total + wins[own + near, at : at + MARGIN, :]
    return total


def squares_of(grad):
    return jnp.sum((grad * grad).reshape(-1, 8, grad.shape[1]), axis=0)


def step_rate(square, tiles):
    tile_len = square.shape[1]
    total = jnp.sum(jnp.sum(square, axis=0, keepdims=True), axis=1, keepdims=True)
    return MASK_RATE / jnp.sqrt(total / (tiles * tile_len * tile_len) + TINY_EPS)


def slope_of(params):
    lean = half_tanh(params)
    return 1.0 - lean * lean


def near_tiles(tile, tiles):
    prev, follow = jnp.maximum(tile - 1, 0), jnp.minimum(tile + 1, tiles - 1)
    return prev, follow, (tile > 0).astype(f32), (tile < tiles - 1).astype(f32)


def edge_params(tile, mate, cross):
    odd = lax.rem(tile, 2) > 0
    before = jnp.where(odd, mate[-MARGIN:, :], cross[...])
    after = jnp.where(odd, cross[...], mate[:MARGIN, :])
    return before, after


def mask_window(near, has_prev, has_next):
    rows = near.shape[0]
    return jnp.concatenate(
        [
            sigmoid(near[:MARGIN, :]) * has_prev,
            sigmoid(near[MARGIN : rows - MARGIN, :]),
            sigmoid(near[rows - MARGIN :, :]) * has_next,
        ],
        0,
    )


def start_all(pairs, sems):
    copies = [pltpu.make_async_copy(a, b, sems.at[i]) for i, (a, b) in enumerate(pairs)]
    for copy in copies:
        copy.start()
    return copies


def head_kernel(out):
    out[...] = jnp.zeros_like(out)


def mark_kernel(value, out):
    out[...] = value[...]


def pack_kernel(place, head, weights, shifts, packed):
    local = weights.shape[1]
    packed[...] = head[...]
    packed[0:1, :local] = weights[...]
    packed[1:3, :local] = shifts[...].astype(f32)
    packed[3:4, :local] = jnp.sqrt(weights[...])
    packed[...] = pltpu.roll(packed[...], place[0] * local, 1)


def edge_kernel(tile, mask, edge):
    at = pl.multiple_of(lax.rem(tile[0], 2) * (mask.shape[0] - MARGIN), MARGIN)
    edge[...] = mask[pl.ds(at, MARGIN), :]


def target_terms(target, t):
    rows, cols = t["target_rows"], t["target_cols"]
    grid = rows.shape[0] // 2
    high, low = split(target)
    both = dot(rows[...], high)
    mid = both[:grid] + both[grid:] + dot(rows[:grid, :], low)
    high, low = split(mid)
    return halves(dot(high, cols[...])) + dot(low, cols[:, : 2 * grid])


def doses(info, scale):
    dose = jnp.sum(info[0:1, :], axis=1, keepdims=True)
    return 1.0 / dose, scale / dose


def early_kernel(spots, table, pupil, goal, own, mate, target, turned_re, turned_im, slopes):
    t = {n: table.at[spot] for n, spot in spots.items()}
    turn_pupils(pupil, turned_re, turned_im)
    target[...] = target_terms(goal[...], t)
    slopes[0] = slope_of(own[...])
    slopes[1] = slope_of(mate[...])


def first_kernel(spots, peers, tiles, scale, tile, table, own, mate, cross,
                 target, turned_re, turned_im, *refs):
    parts = refs[:peers]
    t = {n: table.at[spot] for n, spot in spots.items()}
    back, pr, pi, info, whole, near = refs[peers : peers + 6]
    *work, s0, s1, s2, s3, shifts, roots, sems = refs[peers + 6 :]
    total = parts[0][...]
    for part in parts[1:]:
        total = total + part[...]
    info[...] = total
    whole[...] = total.astype(jnp.int32)
    copies = start_all(((whole, shifts), (info, roots)), sems)
    here = tile[0]
    tile_len = own.shape[0]
    _, _, has_prev, has_next = near_tiles(here, tiles)
    before, after = edge_params(here, mate, cross)
    near[:MARGIN, :] = before
    near[MARGIN : MARGIN + tile_len, :] = own[...]
    near[MARGIN + tile_len :, :] = after
    spec = window_spectrum(mask_window(near, has_prev, has_next), t)
    for copy in copies:
        copy.wait()
    pupils = placed_pupils(shifts, roots, turned_re, turned_im, pr, pi)
    power = grid_fields(spec, shifts, t, pupils, work)
    inv_dose, factor = doses(total, scale)
    misfit = grid_misfit(power, inv_dose, target[...], t)
    sums = (s0, s1, s2, s3)
    back[...] = gather_back(misfit, shifts, factor, t, pr, pi, work[2], work[3:], sums)


def next_kernel(spots, tiles, scale, tile, table, shifts, info, pr, pi, target, near, slopes, *refs):
    params, backs = refs[: tiles - 2], refs[tiles - 2 : 2 * tiles - 2]
    t = {n: table.at[spot] for n, spot in spots.items()}
    new, grads, rates, back, *work, s0, s1, s2, s3, wins = refs[2 * tiles - 2 :]
    here = tile[0]
    tile_len = wins.shape[2]
    fill_windows(backs, t, here, tiles, wins)
    square = jnp.zeros((8, tile_len), f32)
    for k in range(tiles):
        own = tile_of(k, here)
        for piece in pieces(tile_len):
            low, high = piece[:2]
            slope = slopes[k, low:high, :] if k < 2 else slope_of(params[k - 2][low:high, :])
            grad = piece_total(own, piece, wins) * slope
            grads[own, low:high, :] = grad
            square = square + squares_of(grad)
    rate = step_rate(square, tiles)
    rates[...] = jnp.broadcast_to(rate, rates.shape)
    prev, follow, has_prev, has_next = near_tiles(here, tiles)
    inner = slice(MARGIN, MARGIN + tile_len)
    new[:MARGIN, :] = near[:MARGIN, :] - grads[prev, tile_len - MARGIN :, :] * rate
    new[inner, :] = near[inner, :] - grads[here] * rate
    new[MARGIN + tile_len :, :] = near[MARGIN + tile_len :, :] - grads[follow, :MARGIN, :] * rate
    spec = window_spectrum(mask_window(new, has_prev, has_next), t)
    power = grid_fields(spec, shifts, t, lambda s: (pr[s], pi[s]), work)
    inv_dose, factor = doses(info[...], scale)
    misfit = grid_misfit(power, inv_dose, target[...], t)
    sums = (s0, s1, s2, s3)
    back[...] = gather_back(misfit, shifts, factor, t, pr, pi, work[2], work[3:], sums)


def slope_kernel(tiles, tile, grads, rates, *refs):
    params, slopes = refs[:tiles], refs[tiles]
    rate = rates[0:1, 0:1]
    for k in range(tiles):
        own = tile_of(k, tile[0])
        slopes[own] = slope_of(params[k][...] - grads[own] * rate)


def last_kernel(spots, tiles, tile, table, shifts, info, pr, pi, target, near, slopes, *refs):
    backs = refs[:tiles]
    t = {n: table.at[spot] for n, spot in spots.items()}
    final, row, *work, terms, wins, fresh, sems = refs[tiles:]
    fields = work[2]
    here = tile[0]
    tile_len = wins.shape[2]
    fill_windows(backs, t, here, tiles, wins)

    def grad_of(own, piece):
        return piece_total(own, piece, wins) * slopes[own, piece[0] : piece[1], :]

    square = jnp.zeros((8, tile_len), f32)
    for own in range(tiles):
        for piece in pieces(tile_len):
            square = square + squares_of(grad_of(own, piece))
    rate = step_rate(square, tiles)
    prev, follow, has_prev, has_next = near_tiles(here, tiles)
    first, *_, end = pieces(tile_len)
    fresh[:MARGIN, :] = near[:MARGIN, :] - grad_of(prev, end) * rate
    for piece in pieces(tile_len):
        at = slice(MARGIN + piece[0], MARGIN + piece[1])
        fresh[at, :] = near[at, :] - grad_of(here, piece) * rate
    fresh[MARGIN + tile_len :, :] = near[MARGIN + tile_len :, :] - grad_of(follow, first) * rate
    (leave,) = start_all(((fresh.at[pl.ds(MARGIN, tile_len), :], final),), sems)
    spec = window_spectrum(mask_window(fresh, has_prev, has_next), t)
    power = grid_fields(
        spec, shifts, t, lambda s: (pr[s], pi[s]), work, squares=True
    )
    inv_dose, _ = doses(info[...], 1.0)
    misfit = grid_misfit(power, inv_dose, target[...], t)

    def chunk(c, carry):
        rows = []
        for i in range(CHUNK):
            rows.append(jnp.sum(fields[c * CHUNK + i] * misfit, axis=0, keepdims=True))
        terms[pl.ds(pl.multiple_of(c * CHUNK, CHUNK), CHUNK), :] = jnp.concatenate(rows, 0)
        return carry

    count = fields.shape[0]
    lax.fori_loop(0, count // CHUNK, chunk, 0)
    high, low = split(terms[...])
    left = terms[...] - high.astype(f32) - low.astype(f32)
    ones = jnp.ones((8, terms.shape[1]), bf16)
    total = jnp.zeros((8, terms.shape[0]), f32)
    for part in (left.astype(bf16), low, high):
        total = total + lax.dot_general(
            ones, part, (((1,), (1,)), ((), ())), preferred_element_type=f32
        )
    row[...] = total
    leave.wait()


def weight_kernel(tiles, scale, tile, place, info, *refs):
    rows = refs[:tiles]
    out, stack = refs[tiles:]
    count = rows[0].shape[1]
    for k in range(tiles):
        stack[k] = rows[k][...]
    here = tile[0]
    total = stack[here]
    for k in range(1, tiles):
        total = total + stack[tile_of(k, here)]
    summed = total[0:1] * scale
    weight = info[0:1, :count]
    dose = jnp.sum(weight, axis=1, keepdims=True)
    mean = jnp.sum(summed, axis=1, keepdims=True) / dose
    grad = (summed / weight - mean) / dose
    spread = jnp.sqrt(jnp.sum(grad * grad, axis=1, keepdims=True) / count + TINY_EPS)
    new = weight * jnp.exp(-WEIGHT_RATE * grad / spread)
    size = out.shape[1]
    lanes = info.shape[1]
    if count < lanes:
        new = jnp.concatenate([new, jnp.zeros((1, lanes - count), f32)], 1)
    new = pltpu.roll(jnp.broadcast_to(new, (8, lanes)), lanes - place[0] * size, 1)
    out[...] = new[0:1, :size]


def crossed(value, axis, k):
    return lax.ppermute(value, axis, [(i, i ^ k) for i in range(lax.axis_size(axis))])


def all_of(value, axis):
    got = [value]
    for k in range(1, lax.axis_size(axis)):
        got.append(crossed(value, axis, k))
    return got


def per_device(mask_param, target_image, source_weights, source_shifts, pupil_map):
    tile_len = mask_param.shape[1]
    box_len = pupil_map.shape[1]
    grid = box_len + 2 * MAX_SHIFT
    lanes = 2 * grid
    tiles = lax.axis_size("tile")
    peers = lax.axis_size("src")
    local = source_weights.shape[0]
    count = local * peers
    assert tiles & (tiles - 1) == 0 and peers & (peers - 1) == 0 and count <= 128 and count % CHUNK == 0
    tables = make_tables(tile_len, box_len, MAX_SHIFT)

    tile = lax.axis_index("tile").astype(jnp.int32).reshape(1)
    place = lax.axis_index("src").astype(jnp.int32).reshape(1)

    vmem = pl.BlockSpec(memory_space=pltpu.VMEM)
    smem = pl.BlockSpec(memory_space=pltpu.SMEM)
    left = pl.BlockSpec(memory_space=pltpu.HBM)
    params_of = pltpu.CompilerParams(vmem_limit_bytes=32 << 20)

    def struct(*shape, kind=f32):
        return jax.ShapeDtypeStruct(shape, kind)

    def cost(flops):
        return pl.CostEstimate(flops=flops, bytes_accessed=1 << 20, transcendentals=0)

    head = pl.pallas_call(
        head_kernel,
        out_shape=struct(8, 128),
        out_specs=vmem,
        compiler_params=params_of,
        cost_estimate=cost(1 << 34),
        name="head_step",
    )()
    packed = pl.pallas_call(
        pack_kernel,
        out_shape=struct(8, 128),
        in_specs=[smem] + [vmem] * 3,
        out_specs=vmem,
        compiler_params=params_of,
        cost_estimate=cost(1 << 20),
        name="pack_sources",
    )(place, head, source_weights[None], source_shifts.T)
    _, mask_now = lax.optimization_barrier((packed, mask_param))
    edge = pl.pallas_call(
        edge_kernel,
        out_shape=struct(MARGIN, tile_len),
        in_specs=[smem, vmem],
        out_specs=vmem,
        compiler_params=params_of,
        cost_estimate=cost(1 << 20),
        name="edge_rows",
    )(tile, mask_now)
    packed = all_of(packed, "src")

    pairs = [(i, (i + 1) % tiles) for i in range(1, tiles, 2)]
    cross = lax.ppermute(edge, "tile", pairs + [(j, i) for i, j in pairs])
    mate = crossed(mask_param, "tile", 1)
    far = [crossed(mask_param, "tile", k) for k in range(2, tiles, 2)]

    whole, spots = pack_tables(tables)
    table = jnp.asarray(whole)
    work = [
        pltpu.VMEM((grid, lanes), f32),
        pltpu.VMEM((grid, lanes), f32),
        pltpu.VMEM((count, grid, lanes), f32),
        pltpu.VMEM((CHUNK * box_len, lanes), f32),
        pltpu.VMEM((CHUNK * box_len, lanes), f32),
    ]
    hold = [pltpu.VMEM((grid, lanes), f32)] * 4
    period = tile_len + 2 * MARGIN
    steps = [pltpu.VMEM((tiles + 2, period, tile_len), f32)]
    scale = 0.5 / (grid * grid * period * tile_len)
    source_len = struct(count, box_len, lanes)

    target, *turned, slopes = pl.pallas_call(
        functools.partial(early_kernel, spots),
        out_shape=[struct(grid, lanes)]
        + [struct(2 * MAX_SHIFT + 1, box_len, lanes)] * 2
        + [struct(2, tile_len, tile_len)],
        in_specs=[vmem] * 5,
        out_specs=[vmem] * 4,
        compiler_params=params_of,
        cost_estimate=cost(1 << 30),
        name="early_step",
    )(table, pupil_map, target_image, mask_param, mate)

    back, pr, pi, info, whole, near = pl.pallas_call(
        functools.partial(first_kernel, spots, peers, tiles, scale),
        out_shape=[struct(grid, lanes), source_len, source_len, struct(8, 128),
                   struct(8, 128, kind=jnp.int32), struct(period, tile_len)],
        in_specs=[smem] + [vmem] * (7 + peers),
        out_specs=[vmem] * 6,
        scratch_shapes=work + hold + [
            pltpu.SMEM((8, 128), jnp.int32),
            pltpu.SMEM((8, 128), f32),
            pltpu.SemaphoreType.DMA((2,)),
        ],
        compiler_params=params_of,
        cost_estimate=cost(1 << 32),
        name="first_step",
    )(tile, table, mask_param, mate, cross, target, *turned, *packed)

    shared = (tile, table, whole, info, pr, pi, target)
    shared_specs = [smem, vmem, smem] + [vmem] * 4

    backs = all_of(back, "tile")
    backs[0] = pl.pallas_call(
        mark_kernel,
        out_shape=struct(grid, lanes),
        in_specs=[vmem],
        out_specs=vmem,
        compiler_params=params_of,
        cost_estimate=cost(1 << 20),
        name="mark_step",
    )(back)
    far, backs[0] = lax.optimization_barrier((far, backs[0]))
    entries = [mask_param, mate]
    for one in far:
        entries += [one, crossed(one, "tile", 1)]
    near, grads, rates, back = pl.pallas_call(
        functools.partial(next_kernel, spots, tiles, scale),
        out_shape=[struct(period, tile_len), struct(tiles, tile_len, tile_len),
                   struct(8, 128), struct(grid, lanes)],
        in_specs=shared_specs + [vmem] * (2 * tiles),
        out_specs=[vmem] * 4,
        scratch_shapes=work + hold + steps,
        compiler_params=params_of,
        cost_estimate=cost(1 << 32),
        name="next_step",
    )(*shared, near, slopes, *entries[2:], *backs)

    backs = all_of(back, "tile")
    slopes = pl.pallas_call(
        functools.partial(slope_kernel, tiles),
        out_shape=struct(tiles, tile_len, tile_len),
        in_specs=[smem] + [vmem] * (2 + tiles),
        out_specs=vmem,
        compiler_params=params_of,
        cost_estimate=cost(1 << 28),
        name="slope_step",
    )(tile, grads, rates, *entries)
    final, row = pl.pallas_call(
        functools.partial(last_kernel, spots, tiles),
        out_shape=[struct(tile_len, tile_len), struct(8, count)],
        in_specs=shared_specs + [vmem] * (2 + tiles),
        out_specs=[left, vmem],
        scratch_shapes=work + [pltpu.VMEM((count, lanes), f32)] + steps + [
            pltpu.VMEM((period, tile_len), f32),
            pltpu.SemaphoreType.DMA((1,)),
        ],
        compiler_params=params_of,
        cost_estimate=cost(1 << 32),
        name="last_step",
    )(*shared, near, slopes, *backs)

    rows = all_of(row, "tile")
    out = pl.pallas_call(
        functools.partial(weight_kernel, tiles, 1.0 / (grid * grid)),
        out_shape=struct(1, local),
        in_specs=[smem] * 2 + [vmem] * (1 + tiles),
        out_specs=vmem,
        scratch_shapes=[pltpu.VMEM((tiles, 8, count), f32)],
        compiler_params=params_of,
        name="weight_step",
    )(tile, place, info, *rows)
    return final, out.reshape(local)


def solution(mesh):
    in_specs = (
        P(("group", "tile"), None),
        P(("group", "tile"), None),
        P(("group", "src")),
        P("src", None),
        P(),
    )
    out_specs = (P(("group", "tile"), None), P(("group", "src")))
    return jax.shard_map(
        per_device, mesh=mesh, in_specs=in_specs, out_specs=out_specs, check_vma=False
    )
```

```python
import functools
import math

import jax
import jax.numpy as jnp
import ml_dtypes
import numpy as np
from jax import lax
from jax.experimental import pallas as pl
from jax.experimental.pallas import tpu as pltpu
from jax.sharding import PartitionSpec as P


MARGIN = 64
MAX_SHIFT = 16
MASK_RATE = 0.5
WEIGHT_RATE = 0.3
TINY_EPS = 1e-06
CHUNK = 32
FIRST_CHUNK = 16
GROUP = 2


bf16 = jnp.bfloat16
f32 = jnp.float32


def np_split(table):
    table = np.asarray(table, np.float64)
    high = table.astype(np.float32).astype(ml_dtypes.bfloat16)
    low = (table - high.astype(np.float64)).astype(np.float32).astype(ml_dtypes.bfloat16)
    return high, low


def phases(freqs, pixels, period):
    return 2.0 * math.pi * np.mod(np.outer(freqs, pixels), period) / period


def make_tables(tile_len, box_len, max_shift):
    period = tile_len + 2 * MARGIN
    grid = box_len + 2 * max_shift
    wide = np.arange(grid) - grid // 2
    pix = np.arange(tile_len)
    full = np.arange(period)
    points = np.arange(grid)
    box = np.arange(box_len)
    out = {}
    ang = phases(wide, pix, period)
    high, low = np_split(np.concatenate([np.cos(ang), -np.sin(ang)], 0).T / (period * tile_len))
    out["spec_cols"] = np.concatenate([high, low], 1)
    ang_rows = phases(wide, full, period)
    high, low = np_split(np.concatenate([np.cos(ang_rows), np.sin(ang_rows)], 0))
    out["spec_rows"] = np.concatenate([high, low], 0)
    ang = phases(points, points, grid)
    cos, sin = np.cos(ang), np.sin(ang)
    for name, table in (
        ("lane_fwd", np.block([[cos, sin], [-sin, cos]])),
        ("lane_back", np.block([[cos, -sin], [sin, cos]])),
    ):
        high, low = np_split(table)
        out[name] = np.block([[high, low], [high, np.zeros_like(low)]])
    ang = phases(points, box, grid)
    high, low = np_split(np.concatenate([np.cos(ang), np.sin(ang)], 1))
    out["row_fwd"] = np.concatenate([high, high, low], 1)
    high, low = np_split(np.concatenate([np.cos(ang).T, np.sin(ang).T], 0))
    out["row_back"] = np.concatenate([high, high, low], 1)

    def dirichlet(offset):
        theta = 2.0 * math.pi * ((pix + offset)[None, :] / period - points[:, None] / grid)
        orders = np.arange(1, box_len)
        return 1.0 + 2.0 * np.cos(orders[:, None, None] * theta[None]).sum(0)

    rows, cols = dirichlet(MARGIN), dirichlet(0)
    high, low = np_split(rows @ rows.T / grid)
    out["mix_rows"] = np.concatenate([high, high, low], 1)
    mix = cols @ cols.T / grid
    high, low = np_split(np.block([[mix, mix], [mix, mix]]))
    out["mix_cols"] = np.block([[high, low], [high, np.zeros_like(low)]])
    high, low = np_split(rows)
    out["target_rows"] = np.concatenate([high, low], 0)
    high, low = np_split(np.concatenate([cols, cols], 0).T)
    out["target_cols"] = np.concatenate([high, low], 1)
    ang = phases(wide, pix, period)
    cos, sin = np.cos(ang), np.sin(ang)
    high, low = np_split(np.block([[cos, -sin], [-sin, -cos]]))
    out["grad_cols"] = np.concatenate([high, high, low], 0)
    ang = phases(full, np.arange(grid // 2), period)
    high, low = np_split(np.concatenate([np.cos(ang), np.sin(ang)], 1))
    out["grad_rows"] = np.concatenate([high, high, low], 1)
    return out


def pack_tables(tables):
    wide = [n for n in tables if tables[n].shape[1] > 256]
    narrow = sorted((n for n in tables if n not in wide), key=lambda n: -tables[n].shape[0])
    place, heights = {}, [0, 0]
    for n in wide:
        place[n] = (heights[0], 0)
        heights = [heights[0] + tables[n].shape[0]] * 2
    for n in narrow:
        side = int(heights[1] < heights[0])
        place[n] = (heights[side], 256 * side)
        heights[side] += tables[n].shape[0]
    whole = np.zeros((max(heights), 512), ml_dtypes.bfloat16)
    spots = {}
    for n, (row, col) in place.items():
        rows, cols = tables[n].shape
        whole[row : row + rows, col : col + cols] = tables[n]
        spots[n] = (slice(row, row + rows), slice(col, col + cols))
    return whole, spots


def split(value):
    high = value.astype(bf16)
    return high, (value - high.astype(f32)).astype(bf16)


def dot(left, right):
    return jnp.dot(left, right, preferred_element_type=f32)


def halves(value):
    width = value.shape[1] // 2
    return value[:, :width] + value[:, width:]


def lane_sign(rows, lanes, first):
    lane = lax.broadcasted_iota(jnp.int32, (rows, lanes), 1)
    return jnp.where(lane < lanes // 2, first, -first).astype(f32)


def swap(value):
    return pltpu.roll(value, value.shape[1] // 2, 1)


def half_tanh(value):
    return jnp.tanh(0.5 * value)


def sigmoid(value):
    return 0.5 * half_tanh(value) + 0.5


def window_spectrum(window, t):
    grid = t["spec_cols"].shape[1] // 4
    high, low = split(window)
    cols = t["spec_cols"]
    mid = halves(dot(high, cols[...])) + dot(low, cols[:, : 2 * grid])
    mid_high, mid_low = split(mid)
    rows = t["spec_rows"]
    both = halves(dot(rows[: 2 * grid, :], jnp.concatenate([mid_high, mid_low], 1)))
    both = both + dot(rows[2 * grid :, :], mid_high)
    return both[:grid] + lane_sign(grid, 2 * grid, 1.0) * swap(both[grid:])


def skewed(chunks, stages, first, second, carry):
    first(0, stages[0])
    for c in range(1, chunks):
        first(c, stages[c % 2])
        carry = second(c - 1, stages[(c - 1) % 2], carry)
    return second(chunks - 1, stages[(chunks - 1) % 2], carry)


def turn_pupils(pupil, turned_re, turned_im):
    count, size, lanes = turned_re.shape
    grid = lanes // 2
    turned_re[0] = jnp.zeros((size, lanes), f32)
    turned_im[0] = jnp.zeros((size, lanes), f32)
    turned_re[0, :, :size] = pupil[0]
    turned_re[0, :, grid : grid + size] = pupil[0]
    turned_im[0, :, :size] = -pupil[1]
    turned_im[0, :, grid : grid + size] = pupil[1]
    real, imag = turned_re[0], turned_im[0]
    for by in range(1, count):
        turned_re[by] = pltpu.roll(real, by, 1)
        turned_im[by] = pltpu.roll(imag, by, 1)


def placed_pupils(shifts, roots, turned_re, turned_im, pr, pi):
    def make(s):
        by = shifts[2, s] + MAX_SHIFT
        real, imag = turned_re[by] * roots[3, s], turned_im[by] * roots[3, s]
        pr[s], pi[s] = real, imag
        return real, imag

    return make


def grid_fields(spec, shifts, t, pupils, work, squares=False):
    plain, crossed, fields, *stages = work
    count, grid, lanes = fields.shape
    box_len = t["row_fwd"].shape[1] // 6
    size = stages[0].shape[0] // box_len
    plain[...] = spec
    crossed[...] = swap(spec)
    sign = lane_sign(box_len, lanes, -1.0)

    def first(c, stage):
        rows = []
        for i in range(size):
            s = c * size + i
            at = pl.ds(shifts[1, s] + MAX_SHIFT, box_len)
            real, imag = pupils(s)
            high, low = split(real * plain[at, :] + imag * crossed[at, :])
            rows.append(jnp.concatenate([high, low], 1))
        stage[...] = halves(dot(jnp.concatenate(rows, 0), t["lane_fwd"][...]))

    def second(c, stage, power):
        for base in range(0, size, GROUP):
            stacks = []
            for i in range(base, base + GROUP):
                part = stage[i * box_len : (i + 1) * box_len, :]
                high, low = split(jnp.concatenate([part, sign * swap(part)], 0))
                stacks.append(jnp.concatenate([high, low, high], 0))
            out = dot(t["row_fwd"][...], jnp.concatenate(stacks, 1))
            for i in range(GROUP):
                field = out[:, i * lanes : (i + 1) * lanes]
                square = field * field
                fields[c * size + base + i] = square if squares else field
                power = power + square
        return power

    return skewed(count // size, stages, first, second, jnp.zeros((grid, lanes), f32))


def grid_misfit(power, inv_dose, target, t):
    high, low = split(power)
    mid = halves(dot(jnp.concatenate([high, low], 1), t["mix_cols"][...]))
    high, low = split(mid)
    lit = dot(t["mix_rows"][...], jnp.concatenate([high, low, high], 0))
    return lit * inv_dose - target


def gather_back(misfit, shifts, scale, t, pr, pi, fields, stages, sums):
    count, box_len, lanes = pr.shape
    grid = lanes // 2
    size = stages[0].shape[0] // box_len
    for ref in sums:
        ref[...] = jnp.zeros_like(ref)
    sign = lane_sign(box_len, lanes, 1.0)

    def first(c, stage):
        for base in range(0, size, GROUP):
            stacks = []
            for i in range(base, base + GROUP):
                high, low = split(fields[c * size + i] * misfit)
                stacks.append(jnp.concatenate([high, low, high], 0))
            both = dot(t["row_back"][...], jnp.concatenate(stacks, 1))
            for i in range(GROUP):
                part = both[:, i * lanes : (i + 1) * lanes]
                at = (base + i) * box_len
                stage[at : at + box_len, :] = part[:box_len] + sign * swap(part[box_len:])

    def second(c, stage, carry):
        high, low = split(stage[...])
        hits = halves(dot(jnp.concatenate([high, low], 1), t["lane_back"][...]))
        for i in range(size):
            s = c * size + i
            rows = pl.ds(shifts[1, s] + MAX_SHIFT, box_len)
            hit = hits[i * box_len : (i + 1) * box_len]
            one, two = sums[2 * (i % 2)], sums[2 * (i % 2) + 1]
            one[rows, :] += pr[s] * hit
            two[rows, :] += pi[s] * hit
        return carry

    skewed(count // size, stages, first, second, 0)
    whole, turned = sums[0], sums[1]
    whole[...] = (whole[...] + sums[2][...] + swap(turned[...] + sums[3][...])) * scale
    middle = grid // 2
    turned[0:1, :] = jnp.zeros((1, lanes), f32)
    for a in range(1, middle):
        turned[a : a + 1, :] = whole[middle - a : middle - a + 1, :]
    ahead, behind = whole[middle:, :], turned[:middle, :]
    return jnp.concatenate([ahead + behind, ahead - behind], 0)


def tile_of(k, tile):
    return lax.bitwise_xor(tile, jnp.int32(k))


def fill_windows(backs, t, tile, tiles, wins):
    half = backs[0].shape[0] // 2
    tile_len = wins.shape[2]
    stacks = []
    for rows in (slice(0, half), slice(half, 2 * half)):
        parts = []
        for back in backs:
            high, low = split(back[rows, :])
            parts.append(jnp.concatenate([high, low, high], 1))
        stacks.append(jnp.concatenate(parts, 0))
    even = dot(stacks[0], t["grad_cols"][:, :tile_len])
    odd = dot(stacks[1], t["grad_cols"][:, tile_len:])
    wins[0, MARGIN + tile_len :, :] = jnp.zeros((MARGIN, tile_len), f32)
    wins[tiles + 1, :MARGIN, :] = jnp.zeros((MARGIN, tile_len), f32)
    for k in range(tiles):
        at = slice(k * half, (k + 1) * half)
        high, low = split(jnp.concatenate([even[at], odd[at]], 0))
        out = dot(t["grad_rows"][...], jnp.concatenate([high, low, high], 0))
        wins[tile_of(k, tile) + 1] = out


def pieces(tile_len):
    return (
        (0, MARGIN, 0, tile_len),
        (MARGIN, tile_len - MARGIN, 1, 0),
        (tile_len - MARGIN, tile_len, 2, -tile_len),
    )


def piece_total(own, piece, wins):
    low, high, near, shift = piece
    total = wins[own + 1, MARGIN + low : MARGIN + high, :]
    if near != 1:
        at = MARGIN + low + shift
        total = total + wins[own + near, at : at + MARGIN, :]
    return total


def squares_of(grad):
    return jnp.sum((grad * grad).reshape(-1, 8, grad.shape[1]), axis=0)


def step_rate(square, tiles):
    tile_len = square.shape[1]
    total = jnp.sum(jnp.sum(square, axis=0, keepdims=True), axis=1, keepdims=True)
    return MASK_RATE / jnp.sqrt(total / (tiles * tile_len * tile_len) + TINY_EPS)


def slope_of(params):
    lean = half_tanh(params)
    return 1.0 - lean * lean


def near_tiles(tile, tiles):
    prev, follow = jnp.maximum(tile - 1, 0), jnp.minimum(tile + 1, tiles - 1)
    return prev, follow, (tile > 0).astype(f32), (tile < tiles - 1).astype(f32)


def edge_params(tile, mate, cross):
    odd = lax.rem(tile, 2) > 0
    before = jnp.where(odd, mate[-MARGIN:, :], cross[...])
    after = jnp.where(odd, cross[...], mate[:MARGIN, :])
    return before, after


def mask_window(near, has_prev, has_next):
    rows = near.shape[0]
    return jnp.concatenate(
        [
            sigmoid(near[:MARGIN, :]) * has_prev,
            sigmoid(near[MARGIN : rows - MARGIN, :]),
            sigmoid(near[rows - MARGIN :, :]) * has_next,
        ],
        0,
    )


def start_all(pairs, sems):
    copies = [pltpu.make_async_copy(a, b, sems.at[i]) for i, (a, b) in enumerate(pairs)]
    for copy in copies:
        copy.start()
    return copies


def head_kernel(out):
    out[...] = jnp.zeros_like(out)


def mark_kernel(value, out):
    out[...] = value[...]


def pack_kernel(place, head, weights, shifts, packed):
    local = weights.shape[1]
    packed[...] = head[...]
    packed[0:1, :local] = weights[...]
    packed[1:3, :local] = shifts[...].astype(f32)
    packed[3:4, :local] = jnp.sqrt(weights[...])
    packed[...] = pltpu.roll(packed[...], place[0] * local, 1)


def edge_kernel(tile, mask, edge):
    at = pl.multiple_of(lax.rem(tile[0], 2) * (mask.shape[0] - MARGIN), MARGIN)
    edge[...] = mask[pl.ds(at, MARGIN), :]


def target_terms(target, t):
    rows, cols = t["target_rows"], t["target_cols"]
    grid = rows.shape[0] // 2
    high, low = split(target)
    both = dot(rows[...], high)
    mid = both[:grid] + both[grid:] + dot(rows[:grid, :], low)
    high, low = split(mid)
    return halves(dot(high, cols[...])) + dot(low, cols[:, : 2 * grid])


def doses(info, scale):
    dose = jnp.sum(info[0:1, :], axis=1, keepdims=True)
    return 1.0 / dose, scale / dose


def early_kernel(spots, table, pupil, goal, own, mate, target, turned_re, turned_im, slopes):
    t = {n: table.at[spot] for n, spot in spots.items()}
    turn_pupils(pupil, turned_re, turned_im)
    target[...] = target_terms(goal[...], t)
    slopes[0] = slope_of(own[...])
    slopes[1] = slope_of(mate[...])


def first_kernel(spots, peers, tiles, scale, tile, table, own, mate, cross,
                 target, turned_re, turned_im, *refs):
    parts = refs[:peers]
    t = {n: table.at[spot] for n, spot in spots.items()}
    back, pr, pi, info, whole, near = refs[peers : peers + 6]
    *work, s0, s1, s2, s3, shifts, roots, sems = refs[peers + 6 :]
    total = parts[0][...]
    for part in parts[1:]:
        total = total + part[...]
    info[...] = total
    whole[...] = total.astype(jnp.int32)
    copies = start_all(((whole, shifts), (info, roots)), sems)
    here = tile[0]
    tile_len = own.shape[0]
    _, _, has_prev, has_next = near_tiles(here, tiles)
    before, after = edge_params(here, mate, cross)
    near[:MARGIN, :] = before
    near[MARGIN : MARGIN + tile_len, :] = own[...]
    near[MARGIN + tile_len :, :] = after
    spec = window_spectrum(mask_window(near, has_prev, has_next), t)
    for copy in copies:
        copy.wait()
    pupils = placed_pupils(shifts, roots, turned_re, turned_im, pr, pi)
    power = grid_fields(spec, shifts, t, pupils, work)
    inv_dose, factor = doses(total, scale)
    misfit = grid_misfit(power, inv_dose, target[...], t)
    sums = (s0, s1, s2, s3)
    back[...] = gather_back(misfit, shifts, factor, t, pr, pi, work[2], work[3:], sums)


def next_kernel(spots, tiles, scale, tile, table, shifts, info, pr, pi, target, near, slopes, *refs):
    params, backs = refs[: tiles - 2], refs[tiles - 2 : 2 * tiles - 2]
    t = {n: table.at[spot] for n, spot in spots.items()}
    new, grads, rates, back, *work, s0, s1, s2, s3, wins = refs[2 * tiles - 2 :]
    here = tile[0]
    tile_len = wins.shape[2]
    fill_windows(backs, t, here, tiles, wins)
    square = jnp.zeros((8, tile_len), f32)
    for k in range(tiles):
        own = tile_of(k, here)
        for piece in pieces(tile_len):
            low, high = piece[:2]
            slope = slopes[k, low:high, :] if k < 2 else slope_of(params[k - 2][low:high, :])
            grad = piece_total(own, piece, wins) * slope
            grads[own, low:high, :] = grad
            square = square + squares_of(grad)
    rate = step_rate(square, tiles)
    rates[...] = jnp.broadcast_to(rate, rates.shape)
    prev, follow, has_prev, has_next = near_tiles(here, tiles)
    inner = slice(MARGIN, MARGIN + tile_len)
    new[:MARGIN, :] = near[:MARGIN, :] - grads[prev, tile_len - MARGIN :, :] * rate
    new[inner, :] = near[inner, :] - grads[here] * rate
    new[MARGIN + tile_len :, :] = near[MARGIN + tile_len :, :] - grads[follow, :MARGIN, :] * rate
    spec = window_spectrum(mask_window(new, has_prev, has_next), t)
    power = grid_fields(spec, shifts, t, lambda s: (pr[s], pi[s]), work)
    inv_dose, factor = doses(info[...], scale)
    misfit = grid_misfit(power, inv_dose, target[...], t)
    sums = (s0, s1, s2, s3)
    back[...] = gather_back(misfit, shifts, factor, t, pr, pi, work[2], work[3:], sums)


def slope_kernel(tiles, tile, grads, rates, *refs):
    params, slopes = refs[:tiles], refs[tiles]
    rate = rates[0:1, 0:1]
    for k in range(tiles):
        own = tile_of(k, tile[0])
        slopes[own] = slope_of(params[k][...] - grads[own] * rate)


def last_kernel(spots, tiles, tile, table, shifts, info, pr, pi, target, near, slopes, *refs):
    backs = refs[:tiles]
    t = {n: table.at[spot] for n, spot in spots.items()}
    final, row, *work, terms, wins, fresh, sems = refs[tiles:]
    fields = work[2]
    here = tile[0]
    tile_len = wins.shape[2]
    fill_windows(backs, t, here, tiles, wins)

    def grad_of(own, piece):
        return piece_total(own, piece, wins) * slopes[own, piece[0] : piece[1], :]

    square = jnp.zeros((8, tile_len), f32)
    for own in range(tiles):
        for piece in pieces(tile_len):
            square = square + squares_of(grad_of(own, piece))
    rate = step_rate(square, tiles)
    prev, follow, has_prev, has_next = near_tiles(here, tiles)
    first, *_, end = pieces(tile_len)
    fresh[:MARGIN, :] = near[:MARGIN, :] - grad_of(prev, end) * rate
    for piece in pieces(tile_len):
        at = slice(MARGIN + piece[0], MARGIN + piece[1])
        fresh[at, :] = near[at, :] - grad_of(here, piece) * rate
    fresh[MARGIN + tile_len :, :] = near[MARGIN + tile_len :, :] - grad_of(follow, first) * rate
    (leave,) = start_all(((fresh.at[pl.ds(MARGIN, tile_len), :], final),), sems)
    spec = window_spectrum(mask_window(fresh, has_prev, has_next), t)
    power = grid_fields(
        spec, shifts, t, lambda s: (pr[s], pi[s]), work, squares=True
    )
    inv_dose, _ = doses(info[...], 1.0)
    misfit = grid_misfit(power, inv_dose, target[...], t)

    def chunk(c, carry):
        rows = []
        for i in range(CHUNK):
            rows.append(jnp.sum(fields[c * CHUNK + i] * misfit, axis=0, keepdims=True))
        terms[pl.ds(pl.multiple_of(c * CHUNK, CHUNK), CHUNK), :] = jnp.concatenate(rows, 0)
        return carry

    count = fields.shape[0]
    lax.fori_loop(0, count // CHUNK, chunk, 0)
    high, low = split(terms[...])
    left = terms[...] - high.astype(f32) - low.astype(f32)
    ones = jnp.ones((8, terms.shape[1]), bf16)
    total = jnp.zeros((8, terms.shape[0]), f32)
    for part in (left.astype(bf16), low, high):
        total = total + lax.dot_general(
            ones, part, (((1,), (1,)), ((), ())), preferred_element_type=f32
        )
    row[...] = total
    leave.wait()


def weight_kernel(tiles, scale, tile, place, info, *refs):
    rows = refs[:tiles]
    out, stack = refs[tiles:]
    count = rows[0].shape[1]
    for k in range(tiles):
        stack[k] = rows[k][...]
    here = tile[0]
    total = stack[here]
    for k in range(1, tiles):
        total = total + stack[tile_of(k, here)]
    summed = total[0:1] * scale
    weight = info[0:1, :count]
    dose = jnp.sum(weight, axis=1, keepdims=True)
    mean = jnp.sum(summed, axis=1, keepdims=True) / dose
    grad = (summed / weight - mean) / dose
    spread = jnp.sqrt(jnp.sum(grad * grad, axis=1, keepdims=True) / count + TINY_EPS)
    new = weight * jnp.exp(-WEIGHT_RATE * grad / spread)
    size = out.shape[1]
    lanes = info.shape[1]
    if count < lanes:
        new = jnp.concatenate([new, jnp.zeros((1, lanes - count), f32)], 1)
    new = pltpu.roll(jnp.broadcast_to(new, (8, lanes)), lanes - place[0] * size, 1)
    out[...] = new[0:1, :size]


def crossed(value, axis, k):
    return lax.ppermute(value, axis, [(i, i ^ k) for i in range(lax.axis_size(axis))])


def all_of(value, axis):
    got = [value]
    for k in range(1, lax.axis_size(axis)):
        got.append(crossed(value, axis, k))
    return got


def per_device(mask_param, target_image, source_weights, source_shifts, pupil_map):
    tile_len = mask_param.shape[1]
    box_len = pupil_map.shape[1]
    grid = box_len + 2 * MAX_SHIFT
    lanes = 2 * grid
    tiles = lax.axis_size("tile")
    peers = lax.axis_size("src")
    local = source_weights.shape[0]
    count = local * peers
    assert tiles & (tiles - 1) == 0 and peers & (peers - 1) == 0 and count <= 128 and count % CHUNK == 0
    tables = make_tables(tile_len, box_len, MAX_SHIFT)

    tile = lax.axis_index("tile").astype(jnp.int32).reshape(1)
    place = lax.axis_index("src").astype(jnp.int32).reshape(1)

    vmem = pl.BlockSpec(memory_space=pltpu.VMEM)
    smem = pl.BlockSpec(memory_space=pltpu.SMEM)
    left = pl.BlockSpec(memory_space=pltpu.HBM)
    params_of = pltpu.CompilerParams(vmem_limit_bytes=32 << 20)

    def struct(*shape, kind=f32):
        return jax.ShapeDtypeStruct(shape, kind)

    def cost(flops):
        return pl.CostEstimate(flops=flops, bytes_accessed=1 << 20, transcendentals=0)

    head = pl.pallas_call(
        head_kernel,
        out_shape=struct(8, 128),
        out_specs=vmem,
        compiler_params=params_of,
        cost_estimate=cost(1 << 34),
        name="head_step",
    )()
    packed = pl.pallas_call(
        pack_kernel,
        out_shape=struct(8, 128),
        in_specs=[smem] + [vmem] * 3,
        out_specs=vmem,
        compiler_params=params_of,
        cost_estimate=cost(1 << 20),
        name="pack_sources",
    )(place, head, source_weights[None], source_shifts.T)
    _, mask_now = lax.optimization_barrier((packed, mask_param))
    edge = pl.pallas_call(
        edge_kernel,
        out_shape=struct(MARGIN, tile_len),
        in_specs=[smem, vmem],
        out_specs=vmem,
        compiler_params=params_of,
        cost_estimate=cost(1 << 20),
        name="edge_rows",
    )(tile, mask_now)
    packed = all_of(packed, "src")

    pairs = [(i, (i + 1) % tiles) for i in range(1, tiles, 2)]
    cross = lax.ppermute(edge, "tile", pairs + [(j, i) for i, j in pairs])
    mate = crossed(mask_param, "tile", 1)
    far = [crossed(mask_param, "tile", k) for k in range(2, tiles, 2)]

    whole, spots = pack_tables(tables)
    table = jnp.asarray(whole)

    def work_of(chunk):
        return [
            pltpu.VMEM((grid, lanes), f32),
            pltpu.VMEM((grid, lanes), f32),
            pltpu.VMEM((count, grid, lanes), f32),
            pltpu.VMEM((chunk * box_len, lanes), f32),
            pltpu.VMEM((chunk * box_len, lanes), f32),
        ]

    work = work_of(CHUNK)
    hold = [pltpu.VMEM((grid, lanes), f32)] * 4
    period = tile_len + 2 * MARGIN
    steps = [pltpu.VMEM((tiles + 2, period, tile_len), f32)]
    scale = 0.5 / (grid * grid * period * tile_len)
    source_len = struct(count, box_len, lanes)

    target, *turned, slopes = pl.pallas_call(
        functools.partial(early_kernel, spots),
        out_shape=[struct(grid, lanes)]
        + [struct(2 * MAX_SHIFT + 1, box_len, lanes)] * 2
        + [struct(2, tile_len, tile_len)],
        in_specs=[vmem] * 5,
        out_specs=[vmem] * 4,
        compiler_params=params_of,
        cost_estimate=cost(1 << 30),
        name="early_step",
    )(table, pupil_map, target_image, mask_param, mate)

    back, pr, pi, info, whole, near = pl.pallas_call(
        functools.partial(first_kernel, spots, peers, tiles, scale),
        out_shape=[struct(grid, lanes), source_len, source_len, struct(8, 128),
                   struct(8, 128, kind=jnp.int32), struct(period, tile_len)],
        in_specs=[smem] + [vmem] * (7 + peers),
        out_specs=[vmem] * 6,
        scratch_shapes=work_of(FIRST_CHUNK) + hold + [
            pltpu.SMEM((8, 128), jnp.int32),
            pltpu.SMEM((8, 128), f32),
            pltpu.SemaphoreType.DMA((2,)),
        ],
        compiler_params=params_of,
        cost_estimate=cost(1 << 32),
        name="first_step",
    )(tile, table, mask_param, mate, cross, target, *turned, *packed)

    shared = (tile, table, whole, info, pr, pi, target)
    shared_specs = [smem, vmem, smem] + [vmem] * 4

    backs = all_of(back, "tile")
    backs[0] = pl.pallas_call(
        mark_kernel,
        out_shape=struct(grid, lanes),
        in_specs=[vmem],
        out_specs=vmem,
        compiler_params=params_of,
        cost_estimate=cost(1 << 20),
        name="mark_step",
    )(back)
    far, backs[0] = lax.optimization_barrier((far, backs[0]))
    entries = [mask_param, mate]
    for one in far:
        entries += [one, crossed(one, "tile", 1)]
    near, grads, rates, back = pl.pallas_call(
        functools.partial(next_kernel, spots, tiles, scale),
        out_shape=[struct(period, tile_len), struct(tiles, tile_len, tile_len),
                   struct(8, 128), struct(grid, lanes)],
        in_specs=shared_specs + [vmem] * (2 * tiles),
        out_specs=[vmem] * 4,
        scratch_shapes=work + hold + steps,
        compiler_params=params_of,
        cost_estimate=cost(1 << 32),
        name="next_step",
    )(*shared, near, slopes, *entries[2:], *backs)

    backs = all_of(back, "tile")
    slopes = pl.pallas_call(
        functools.partial(slope_kernel, tiles),
        out_shape=struct(tiles, tile_len, tile_len),
        in_specs=[smem] + [vmem] * (2 + tiles),
        out_specs=vmem,
        compiler_params=params_of,
        cost_estimate=cost(1 << 28),
        name="slope_step",
    )(tile, grads, rates, *entries)
    final, row = pl.pallas_call(
        functools.partial(last_kernel, spots, tiles),
        out_shape=[struct(tile_len, tile_len), struct(8, count)],
        in_specs=shared_specs + [vmem] * (2 + tiles),
        out_specs=[left, vmem],
        scratch_shapes=work + [pltpu.VMEM((count, lanes), f32)] + steps + [
            pltpu.VMEM((period, tile_len), f32),
            pltpu.SemaphoreType.DMA((1,)),
        ],
        compiler_params=params_of,
        cost_estimate=cost(1 << 32),
        name="last_step",
    )(*shared, near, slopes, *backs)

    rows = all_of(row, "tile")
    out = pl.pallas_call(
        functools.partial(weight_kernel, tiles, 1.0 / (grid * grid)),
        out_shape=struct(1, local),
        in_specs=[smem] * 2 + [vmem] * (1 + tiles),
        out_specs=vmem,
        scratch_shapes=[pltpu.VMEM((tiles, 8, count), f32)],
        compiler_params=params_of,
        name="weight_step",
    )(tile, place, info, *rows)
    return final, out.reshape(local)


def solution(mesh):
    in_specs = (
        P(("group", "tile"), None),
        P(("group", "tile"), None),
        P(("group", "src")),
        P("src", None),
        P(),
    )
    out_specs = (P(("group", "tile"), None), P(("group", "src")))
    return jax.shard_map(
        per_device, mesh=mesh, in_specs=in_specs, out_specs=out_specs, check_vma=False
    )
```
